32 devices in a mesh: shard: 8 (over z, core), rep: 4 (over y, x).
Axes of the slice: x: 2, y: 2, z: 4, core: 2. Of those that a mesh axis runs over, the one named last changes fastest.
Arguments:
- tokens: bfloat16 [49152, 640], P(('shard', 'rep')), may hold values from -6 to 6
- seq_lengths: int32 [64], replicated, may hold values from 256 to 1024, as said below
- seq_device: int32 [64], replicated, may hold values from 0 to 31, as said below
- w_query: bfloat16 [640, 1024], P('shard'), may hold values from -0.25 to 0.25
- w_keyval: bfloat16 [640, 512], P('shard'), may hold values from -0.25 to 0.25
- w_project: bfloat16 [1024, 640], P('shard'), may hold values from -0.1875 to 0.1875
- w_gate: bfloat16 [640, 2048], P('shard'), may hold values from -0.25 to 0.25
- w_upward: bfloat16 [640, 2048], P('shard'), may hold values from -0.25 to 0.25
- w_down: bfloat16 [2048, 640], P('shard'), may hold values from -0.125 to 0.125
- gain_input: bfloat16 [640], P('shard'), may hold values from 0.5 to 2
- gain_query: bfloat16 [256], P('shard'), may hold values from 0.5 to 2
- gain_key: bfloat16 [256], P('shard'), may hold values from 0.5 to 2
- gain_attend: bfloat16 [640], P('shard'), may hold values from 0.5 to 2
- gain_before: bfloat16 [640], P('shard'), may hold values from 0.5 to 2
- gain_after: bfloat16 [640], P('shard'), may hold values from 0.5 to 2
- cotangent: bfloat16 [49152, 640], P(('shard', 'rep')), may hold values from -6 to 6
Outputs:
- activations: bfloat16 [49152, 640], P(('shard', 'rep'))
- input_grad: float32 [49152, 640], P(('shard', 'rep'))
- query_grad: float32 [640, 1024], P('shard')
- keyval_grad: float32 [640, 512], P('shard')
- project_grad: float32 [1024, 640], P('shard')
- gate_grad: float32 [640, 2048], P('shard')
- upward_grad: float32 [640, 2048], P('shard')
- down_grad: float32 [2048, 640], P('shard')
- inputgain_grad: float32 [640], P('shard')
- querygain_grad: float32 [256], P('shard')
- keygain_grad: float32 [256], P('shard')
- attendgain_grad: float32 [640], P('shard')
- beforegain_grad: float32 [640], P('shard')
- aftergain_grad: float32 [640], P('shard')
The draws below stay inside these ranges and needn't reach their ends.
Inputs may be any that keep to these rules, and one draw needn't show every extreme that they name: `seq_lengths`: some sequence has exactly 1024 tokens. `seq_device`: every device index holds exactly two sequences, whose lengths sum to at most 1536; on some device they sum to exactly 1536.
All inputs are finite; a program needn't handle non-finite values.
Results may differ from the reference program's by a relative error of at most 0.017.
Values may be sent and summed in bfloat16 or wider, within the bound.
A program may use at most 256 MiB of HBM per device.

```python
import math
import jax
import jax.numpy as jnp
from jax import lax

D = 640
QH = 4
HD = 256
FF = 2048
MAXLEN = 1024
CAP = 1536
TOKENS = 49152
N_SHARD = 8
N_REP = 4


def seq_layout(key):
    devices = N_REP * N_SHARD
    base = jax.random.fold_in(key, 11)
    k_first, k_second, k_full, k_order = jax.random.split(base, 4)
    first = jax.random.randint(k_first, (devices,), MAXLEN // 4, MAXLEN + 1, dtype=jnp.int32)
    upper = jnp.minimum(MAXLEN, CAP - first) + 1
    second = jax.random.randint(k_second, (devices,), MAXLEN // 4, upper, dtype=jnp.int32)
    full = jax.random.randint(k_full, (), 0, devices, dtype=jnp.int32)
    owner = jnp.arange(devices, dtype=jnp.int32)
    first = jnp.where(owner == full, MAXLEN, first).astype(jnp.int32)
    second = jnp.where(owner == full, CAP - MAXLEN, second).astype(jnp.int32)
    lengths = jnp.concatenate([first, second])
    owners = jnp.concatenate([owner, owner])
    order = jax.random.permutation(k_order, 2 * devices)
    return (lengths[order], owners[order])


def draw_seq_lengths(key, part):
    return seq_layout(key)[0]


def draw_seq_device(key, part):
    return seq_layout(key)[1]


def block_levels(stream_key, extent, cuts, low, high):
    level, own = 1.0, jax.random.fold_in(stream_key, 6)
    for dim, blocks in cuts:
        steps = jnp.exp(jax.random.uniform(jax.random.fold_in(own, dim), (blocks,), jnp.float32, low / len(cuts), high / len(cuts)))
        level = level * jnp.repeat(steps, extent[dim] // blocks).reshape([-1 if axis == dim else 1 for axis in range(len(extent))])
    return level


def normal_values(rng, extent, scale, limit, cuts=(), held_as=jnp.bfloat16):
    drawn = scale * jax.random.normal(rng, extent, jnp.float32)
    if cuts:
        drawn = drawn * block_levels(rng, extent, cuts, -0.22, 0.18)
    return jnp.clip(drawn, -limit, limit).astype(held_as)


def setup_inputs(seed: int = 0) -> dict:
    key_list = jax.random.split(jax.random.key(seed), 17)
    tokens = normal_values(key_list[0], (TOKENS, D), 1.0, 6.0, ((0, 32),))
    seq_lengths = draw_seq_lengths(jax.random.fold_in(key_list[16], 71), 0)
    seq_device = draw_seq_device(jax.random.fold_in(key_list[16], 71), 0)
    w_query = normal_values(key_list[3], (D, QH * HD), D ** -0.5, 0.25, ((0, 8),))
    w_keyval = normal_values(key_list[4], (D, 2 * HD), D ** -0.5, 0.25, ((0, 8),))
    w_project = normal_values(key_list[5], (QH * HD, D), (QH * HD) ** -0.5, 0.1875, ((0, 8),))
    w_gate = normal_values(key_list[6], (D, FF), D ** -0.5, 0.25, ((0, 8),))
    w_upward = normal_values(key_list[7], (D, FF), D ** -0.5, 0.25, ((0, 8),))
    w_down = normal_values(key_list[8], (FF, D), FF ** -0.5, 0.125, ((0, 8),))
    gain_input = jnp.clip(jnp.exp(math.log(2.0) - 1.3862944 * jax.random.uniform(key_list[9], (D,), jnp.float32) ** block_levels(key_list[9], (D,), ((0, 8),), -0.2, 0.2)), 0.5, 2.0).astype(jnp.bfloat16)
    gain_query = jnp.clip(jnp.exp(math.log(2.0) - 1.3862944 * jax.random.uniform(key_list[10], (HD,), jnp.float32) ** block_levels(key_list[10], (HD,), ((0, 8),), -0.2, 0.2)), 0.5, 2.0).astype(jnp.bfloat16)
    gain_key = jnp.clip(jnp.exp(math.log(2.0) - 1.3862944 * jax.random.uniform(key_list[11], (HD,), jnp.float32) ** block_levels(key_list[11], (HD,), ((0, 8),), -0.2, 0.2)), 0.5, 2.0).astype(jnp.bfloat16)
    gain_attend = jnp.clip(jnp.exp(math.log(2.0) - 1.3862944 * jax.random.uniform(key_list[12], (D,), jnp.float32) ** block_levels(key_list[12], (D,), ((0, 8),), -0.2, 0.2)), 0.5, 2.0).astype(jnp.bfloat16)
    gain_before = jnp.clip(jnp.exp(math.log(2.0) - 1.3862944 * jax.random.uniform(key_list[13], (D,), jnp.float32) ** block_levels(key_list[13], (D,), ((0, 8),), -0.2, 0.2)), 0.5, 2.0).astype(jnp.bfloat16)
    gain_after = jnp.clip(jnp.exp(math.log(2.0) - 1.3862944 * jax.random.uniform(key_list[14], (D,), jnp.float32) ** block_levels(key_list[14], (D,), ((0, 8),), -0.2, 0.2)), 0.5, 2.0).astype(jnp.bfloat16)
    cotangent = normal_values(key_list[15], (TOKENS, D), 1.0, 6.0, ((0, 32),))
    return dict(tokens=tokens, seq_lengths=seq_lengths, seq_device=seq_device, w_query=w_query, w_keyval=w_keyval, w_project=w_project, w_gate=w_gate, w_upward=w_upward, w_down=w_down, gain_input=gain_input, gain_query=gain_query, gain_key=gain_key, gain_attend=gain_attend, gain_before=gain_before, gain_after=gain_after, cotangent=cotangent)


EPS = 1e-06
THETA = 1000000.0
NEG = -1e+30

@jax.custom_vjp
def low(v):
    return lax.optimization_barrier(v.astype(jnp.bfloat16)).astype(jnp.float32)

@jax.custom_vjp
def low_back(v):
    return v

def low_keep(v):
    return (low(v), None)

def low_pass(kept, grad):
    return (grad,)

def back_keep(v):
    return (v, None)

def back_low(kept, grad):
    return (low(grad),)
low.defvjp(low_keep, low_pass)
low_back.defvjp(back_keep, back_low)

def matmul(left, right):
    return jnp.dot(left, right, precision=lax.Precision.HIGHEST, preferred_element_type=jnp.float32)

def normed(value, gain):
    return value * lax.rsqrt(lax.optimization_barrier(jnp.mean(value * value, axis=-1, keepdims=True)) + EPS) * gain

def rotary(position, width):
    freqs = THETA ** (-(jnp.arange(width // 2, dtype=jnp.float32) * 2.0 / width))
    angles = position.astype(jnp.float32)[:, None] * freqs[None, :]
    return (jnp.cos(angles), jnp.sin(angles))

def rotate(value, cosine, sine):
    half = value.shape[-1] // 2
    first = value[..., :half]
    second = value[..., half:]
    return jnp.concatenate([first * cosine - second * sine, second * cosine + first * sine], axis=-1)

def layout(seq_lengths, seq_device, device, rows):
    mine = seq_device == device
    lens = jnp.where(mine, seq_lengths, 0).astype(jnp.int32)
    ends = jnp.cumsum(lens, dtype=jnp.int32)
    starts = (ends - lens).astype(jnp.int32)
    row_ids = jnp.arange(rows, dtype=jnp.int32)
    begun = mine[None, :] & (starts[None, :] <= row_ids[:, None])
    segment = lax.optimization_barrier(jnp.sum(begun.astype(jnp.int32), axis=1, dtype=jnp.int32))
    own_start = lax.optimization_barrier(jnp.max(jnp.where(begun, starts[None, :], 0), axis=1)).astype(jnp.int32)
    position = (row_ids - own_start).astype(jnp.int32)
    live = row_ids < jnp.sum(lens, dtype=jnp.int32)
    return (segment, position, live)

def attend_block(query, seg_query, row_query, keys, values, seg_keys, row_keys):
    scale = HD ** (-0.5)
    scores = jnp.einsum('qhd,kd->hqk', query, keys, precision=lax.Precision.HIGHEST) * scale
    allowed = (seg_query[:, None] == seg_keys[None, :]) & (row_keys[None, :] <= row_query[:, None])
    scores = low_back(jnp.where(allowed[None], scores, NEG))
    peak = lax.optimization_barrier(jnp.max(scores, axis=-1, keepdims=True))
    expo = jnp.exp(scores - peak)
    probs = expo / lax.optimization_barrier(jnp.sum(expo, axis=-1, keepdims=True))
    return jnp.einsum('hqk,kd->qhd', low(probs), values, precision=lax.Precision.HIGHEST)

def forward(params, x, segment, position):
    w_query, w_keyval, w_project, w_gate, w_upward, w_down, gain_input, gain_query, gain_key, gain_attend, gain_before, gain_after = params
    rows = x.shape[0]
    cosine, sine = rotary(position, HD)
    h_low = low(normed(x, gain_input))
    q_raw = low_back(matmul(h_low, w_query)).reshape(rows, QH, HD)
    kv_raw = low_back(matmul(h_low, w_keyval))
    queries = low(rotate(normed(q_raw, gain_query), cosine[:, None, :], sine[:, None, :]))
    keys = low(rotate(normed(kv_raw[:, :HD], gain_key), cosine, sine))
    values = low(kv_raw[:, HD:])
    block = rows // 3
    row_ids = jnp.arange(rows, dtype=jnp.int32)
    attend = jax.checkpoint(attend_block)
    pieces = lax.map(lambda item: attend(item[0], item[1], item[2], keys, values, segment, row_ids), (queries.reshape(3, block, QH, HD), segment.reshape(3, block), row_ids.reshape(3, block)))
    attended = low(low_back(pieces.reshape(rows, QH * HD)))
    branch = low_back(matmul(attended, w_project))
    x_mid = x + normed(branch, gain_attend)
    h_two = low(normed(x_mid, gain_before))
    gate = low_back(matmul(h_two, w_gate))
    upper = low_back(matmul(h_two, w_upward))
    hidden = low(jax.nn.gelu(gate, approximate=True) * upper)
    ffn = low_back(matmul(hidden, w_down))
    return x_mid + normed(ffn, gain_after)

def reference(tokens, seq_lengths, seq_device, w_query, w_keyval, w_project, w_gate, w_upward, w_down, gain_input, gain_query, gain_key, gain_attend, gain_before, gain_after, cotangent):
    devices = N_REP * N_SHARD
    params = tuple((w.astype(jnp.float32) for w in (w_query, w_keyval, w_project, w_gate, w_upward, w_down, gain_input, gain_query, gain_key, gain_attend, gain_before, gain_after)))
    x_all = tokens.astype(jnp.float32).reshape(devices, CAP, D)
    cot_all = cotangent.astype(jnp.float32).reshape(devices, CAP, D)

    def one_device(totals, item):
        x_rows, cot_rows, device = item
        segment, position, live = layout(seq_lengths, seq_device, device, CAP)
        result, backward = jax.vjp(lambda p, xx: forward(p, xx, segment, position), params, x_rows)
        grads, d_input = backward(jnp.where(live[:, None], cot_rows, jnp.float32(0.0)))
        totals = tuple((a + b for a, b in zip(totals, grads)))
        return (totals, (result.astype(jnp.bfloat16), d_input))
    zeros = tuple((jnp.zeros_like(p) for p in params))
    totals, (results, d_inputs) = lax.scan(one_device, zeros, (x_all, cot_all, jnp.arange(devices, dtype=jnp.int32)))
    return (results.reshape(TOKENS, D), d_inputs.reshape(TOKENS, D), totals[0], totals[1], totals[2], totals[3], totals[4], totals[5], totals[6], totals[7], totals[8], totals[9], totals[10], totals[11])
```

```python
import functools
import math

import jax
import jax.numpy as jnp
import numpy as np
from jax import lax
from jax.experimental import pallas as pl
from jax.experimental.pallas import tpu as pltpu
from jax.sharding import PartitionSpec as P

QH = 4
HD = 256
EPS = 1e-06
THETA = 1000000.0
RB = 256
COLUMN_STEPS = 8
F32 = jnp.float32
BF = jnp.bfloat16
EXP_SCALE = HD ** (-0.5) * math.log2(math.e)
GELU_C = math.sqrt(2.0 / math.pi)


def dot(left, right):
    return lax.dot_general(left, right, (((1,), (0,)), ((), ())), preferred_element_type=F32)


def dot_nt(left, right):
    return lax.dot_general(left, right, (((1,), (1,)), ((), ())), preferred_element_type=F32)


def inv_rms(value):
    return lax.rsqrt(jnp.mean(value * value, axis=-1, keepdims=True) + EPS)


def rotate(value, cosine, sine):
    first, second = value[:, : HD // 2], value[:, HD // 2 :]
    return jnp.concatenate(
        [first * cosine - second * sine, second * cosine + first * sine], axis=-1
    )


def seen_mask(bound, query_block, key_block, rb):
    keys = key_block * rb + lax.broadcasted_iota(jnp.int32, (rb, rb), 0)
    rows = query_block * rb + lax.broadcasted_iota(jnp.int32, (rb, rb), 1)
    return (keys <= rows) & (keys >= jnp.where(rows >= bound, bound, 0))


def first_block(bound, block, rb):
    return jnp.where(block * rb >= bound, bound // rb, 0)


def attend_kernel(
    info, x_ref, w_ref, wp_ref, g_ref, cos_ref, sin_ref,
    q_out, k_out, v_out, raw_out, att_out, lse_out, branch_out, mid_out,
    k_all, vt_all, acc, den,
):
    i = pl.program_id(0)
    bound = info[0]
    rb = x_ref.shape[0]
    d = x_ref.shape[1]
    x = x_ref[...].astype(F32)
    h = (x * inv_rms(x) * g_ref[0:1, :]).astype(BF)
    cosine, sine = cos_ref[...], sin_ref[...]
    qgain, kgain = g_ref[4:5, :HD], g_ref[5:6, :HD]
    for head in range(QH):
        raw = dot(h, w_ref[:, head * HD : (head + 1) * HD])
        raw_out[:, head * HD : (head + 1) * HD] = raw.astype(BF)
        q_out[head] = rotate(raw * inv_rms(raw) * qgain, cosine, sine).astype(BF)
    raw = dot(h, w_ref[:, QH * HD : (QH + 1) * HD])
    raw_out[:, QH * HD :] = raw.astype(BF)
    keys = rotate(raw * inv_rms(raw) * kgain, cosine, sine).astype(BF)
    values = dot(h, w_ref[:, (QH + 1) * HD :]).astype(BF)
    k_out[...] = keys
    v_out[...] = values
    k_all[i] = keys
    vt_all[i] = values.T
    acc[...] = jnp.zeros_like(acc)
    den[...] = jnp.zeros_like(den)

    def step(j, carry):
        mask = seen_mask(bound, i, j, rb)
        for head in range(QH):
            cols = slice(head * rb, (head + 1) * rb)
            scores = dot_nt(k_all[j], q_out[head])
            probs = jnp.where(mask, jnp.exp2(scores * EXP_SCALE), 0.0)
            den[:, cols] += jnp.sum(probs.reshape(rb // 8, 8, rb), axis=0)
            acc[:, cols] += dot(vt_all[j], probs.astype(BF))
        return carry

    lax.fori_loop(first_block(bound, i, rb), i + 1, step, 0)
    lse = []
    for head in range(QH):
        cols = slice(head * rb, (head + 1) * rb)
        total = jnp.sum(den[:, cols], axis=0, keepdims=True)
        lse.append(jnp.log2(total))
        att_out[:, head * HD : (head + 1) * HD] = (acc[:, cols] * (1.0 / total)).T.astype(BF)
    lse_out[...] = jnp.concatenate(lse + lse, axis=0)
    branch = dot(att_out[...], wp_ref[...])
    branch_out[...] = branch
    mid_out[...] = x + branch * inv_rms(branch) * g_ref[1:2, :]


def attend(info, x, w_qkv, w_project, gains, cosine, sine):
    rows, d = x.shape
    rb = RB
    nb = rows // rb
    whole = lambda a: pl.BlockSpec(a.shape, lambda i, *_: (0,) * a.ndim, pipeline_mode=pl.Buffered(1))
    row = lambda width: pl.BlockSpec((rb, width), lambda i, *_: (i, 0))
    qw = QH * HD
    return pl.pallas_call(
        attend_kernel,
        grid_spec=pltpu.PrefetchScalarGridSpec(
            num_scalar_prefetch=1,
            grid=(nb,),
            in_specs=[row(d), whole(w_qkv), whole(w_project), whole(gains), row(HD // 2), row(HD // 2)],
            out_specs=[
                pl.BlockSpec((QH, rb, HD), lambda i, *_: (0, i, 0)),
                row(HD), row(HD), row(qw + HD), row(qw),
                pl.BlockSpec((8, rb), lambda i, *_: (0, i)),
                row(d), row(d),
            ],
            scratch_shapes=[
                pltpu.VMEM((nb, rb, HD), BF),
                pltpu.VMEM((nb, HD, rb), BF),
                pltpu.VMEM((HD, QH * rb), F32),
                pltpu.VMEM((8, QH * rb), F32),
            ],
        ),
        out_shape=[
            jax.ShapeDtypeStruct((QH, rows, HD), BF),
            jax.ShapeDtypeStruct((rows, HD), BF),
            jax.ShapeDtypeStruct((rows, HD), BF),
            jax.ShapeDtypeStruct((rows, qw + HD), BF),
            jax.ShapeDtypeStruct((rows, qw), BF),
            jax.ShapeDtypeStruct((8, rows), F32),
            jax.ShapeDtypeStruct((rows, d), F32),
            jax.ShapeDtypeStruct((rows, d), F32),
        ],
        compiler_params=pltpu.CompilerParams(vmem_limit_bytes=56 * 2**20),
        cost_estimate=pl.CostEstimate(flops=14 * 10**9, bytes_accessed=30 * 10**6, transcendentals=4 * 10**6),
        name="attend",
    )(info, x, w_qkv, w_project, gains, cosine, sine)


def norm_back(grad, unit, r, gain):
    scaled = grad * gain
    return r * (scaled - unit * jnp.mean(scaled * unit, axis=-1, keepdims=True))


def column_sum(value):
    return jnp.sum(value, axis=0, keepdims=True)


def feed_kernel(
    nb, n_cols, info, mid_ref, branch_ref, att_ref, cot_ref, attc_ref, gu_ref, wd_ref, wp_ref, g_ref,
    act_out, dmid_out, datt_out, spread_out, gg_out, gu_grad, down_grad, project_grad,
    hid, dgu, h2t, dft, dbt, act_s, mul_s,
):
    i = pl.program_id(0)
    rb, d = mid_ref.shape
    ff = wd_ref.shape[0]
    fc = ff // 4

    @pl.when(i < nb)
    def _():
        start = pl.multiple_of(i * rb, rb)
        rows = pl.ds(start, rb)
        mid = mid_ref[...]
        r_mid = inv_rms(mid)
        unit_mid = mid * r_mid
        h2 = (unit_mid * g_ref[2:3, :]).astype(BF)
        h2t[:, rows] = h2.T
        for c in range(4):
            cols = slice(c * fc, (c + 1) * fc)
            gate = dot(h2, gu_ref[:, cols])
            up = dot(h2, gu_ref[:, ff + c * fc : ff + (c + 1) * fc])
            sq = gate * gate
            th = jnp.tanh(GELU_C * gate * (1.0 + 0.044715 * sq))
            half = 0.5 + 0.5 * th
            act = gate * half
            slope = half + 0.5 * gate * (1.0 - th * th) * (GELU_C * (1.0 + (3 * 0.044715) * sq))
            hid[rows, cols] = (act * up).astype(BF)
            act_s[:, cols] = act
            mul_s[:, cols] = up * slope
        ffn = dot(hid[rows, :], wd_ref[...])
        r_ffn = inv_rms(ffn)
        unit_ffn = ffn * r_ffn
        after = g_ref[3:4, :]
        act_out[...] = (mid + unit_ffn * after).astype(BF)
        row_ids = start + lax.broadcasted_iota(jnp.int32, (rb, 1), 0)
        ups = jnp.where(row_ids < info[1], cot_ref[...].astype(F32), 0.0)
        d_ffn = norm_back(ups, unit_ffn, r_ffn, after).astype(BF)
        dft[:, rows] = d_ffn.T
        for c in range(4):
            cols = slice(c * fc, (c + 1) * fc)
            d_hid = dot_nt(d_ffn, wd_ref[cols, :])
            dgu[rows, cols] = (d_hid * mul_s[:, cols]).astype(BF)
            dgu[rows, ff + c * fc : ff + (c + 1) * fc] = (d_hid * act_s[:, cols]).astype(BF)
        d_h2 = dot_nt(dgu[rows, :], gu_ref[...])
        d_mid = ups + norm_back(d_h2, unit_mid, r_mid, g_ref[2:3, :])
        dmid_out[...] = d_mid
        branch = branch_ref[...]
        r_br = inv_rms(branch)
        unit_br = branch * r_br
        d_br = norm_back(d_mid, unit_br, r_br, g_ref[1:2, :]).astype(BF)
        dbt[:, rows] = d_br.T
        d_att = dot_nt(d_br, wp_ref[...])
        datt_low = d_att.astype(BF)
        prod = datt_low.astype(F32) * att_ref[...].astype(F32)
        spread = []
        for head in range(QH):
            cols = slice(head * HD, (head + 1) * HD)
            datt_out[head] = datt_low[:, cols]
            spread.append(jnp.sum(prod[:, cols], axis=1, keepdims=True))
        wide = jnp.concatenate(spread + [jnp.zeros((rb, 128 - QH), F32)], axis=1)
        spread_out[...] = wide.T[:8, :]
        sums = jnp.concatenate(
            [
                jnp.zeros((1, d), F32),
                column_sum(d_mid * unit_br),
                column_sum(d_h2 * unit_mid),
                column_sum(ups * unit_ffn),
                jnp.zeros((4, d), F32),
            ],
            axis=0,
        )

        @pl.when(i == 0)
        def _():
            gg_out[...] = jnp.zeros_like(gg_out)

        gg_out[...] += sums

    @pl.when(i >= nb)
    def _():
        s = i - nb
        wide = 2 * ff // n_cols
        for c in range(2):
            part = wide // 2
            cols = pl.ds(pl.multiple_of(s * wide + c * part, part), part)
            gu_grad[:, c * part : (c + 1) * part] = dot(h2t[...], dgu[:, cols]).astype(BF)
        cols = pl.ds(pl.multiple_of(s * (ff // n_cols), ff // n_cols), ff // n_cols)
        down_grad[0] = dot(dft[...], hid[:, cols]).astype(BF)
        project_grad[0] = dot(dbt[...], attc_ref[...]).astype(BF)


def feed(info, mid, branch, att, cot, w_gu, w_down, w_project, gains):
    rows, d = mid.shape
    ff = w_down.shape[0]
    qw = att.shape[1]
    rb = RB
    nb = rows // rb
    whole = lambda a: pl.BlockSpec(a.shape, lambda i, *_: (0,) * a.ndim, pipeline_mode=pl.Buffered(1))
    blk = lambda i: jnp.minimum(i, nb - 1)
    col = lambda i: jnp.maximum(i - nb, 0)
    row = lambda width: pl.BlockSpec((rb, width), lambda i, *_: (blk(i), 0))
    nc = COLUMN_STEPS

    return pl.pallas_call(
        functools.partial(feed_kernel, nb, nc),
        grid_spec=pltpu.PrefetchScalarGridSpec(
            num_scalar_prefetch=1,
            grid=(nb + nc,),
            in_specs=[
                row(d), row(d), row(qw), row(d),
                pl.BlockSpec((rows, qw // nc), lambda i, *_: (0, col(i))),
                whole(w_gu), whole(w_down), whole(w_project), whole(gains),
            ],
            out_specs=[
                row(d), row(d),
                pl.BlockSpec((QH, rb, HD), lambda i, *_: (0, blk(i), 0)),
                pl.BlockSpec((8, rb), lambda i, *_: (0, blk(i))),
                pl.BlockSpec((8, d), lambda i, *_: (0, 0)),
                pl.BlockSpec((d, 2 * ff // nc), lambda i, *_: (0, col(i))),
                pl.BlockSpec((1, d, ff // nc), lambda i, *_: (col(i), 0, 0)),
                pl.BlockSpec((1, d, qw // nc), lambda i, *_: (col(i), 0, 0)),
            ],
            scratch_shapes=[
                pltpu.VMEM((rows, ff), BF),
                pltpu.VMEM((rows, 2 * ff), BF),
                pltpu.VMEM((d, rows), BF),
                pltpu.VMEM((d, rows), BF),
                pltpu.VMEM((d, rows), BF),
                pltpu.VMEM((rb, ff), F32),
                pltpu.VMEM((rb, ff), F32),
            ],
        ),
        out_shape=[
            jax.ShapeDtypeStruct((rows, d), BF),
            jax.ShapeDtypeStruct((rows, d), F32),
            jax.ShapeDtypeStruct((QH, rows, HD), BF),
            jax.ShapeDtypeStruct((8, rows), F32),
            jax.ShapeDtypeStruct((8, d), F32),
            jax.ShapeDtypeStruct((d, 2 * ff), BF),
            jax.ShapeDtypeStruct((nc, d, ff // nc), BF),
            jax.ShapeDtypeStruct((nc, d, qw // nc), BF),
        ],
        compiler_params=pltpu.CompilerParams(vmem_limit_bytes=60 * 2**20),
        cost_estimate=pl.CostEstimate(flops=42 * 10**9, bytes_accessed=50 * 10**6, transcendentals=4 * 10**6),
        name="feed",
    )(info, mid, branch, att, cot, att, w_gu, w_down, w_project, gains)


def back_kernel(
    nb, info, x_ref, q_ref, k_ref, v_ref, raw_ref, datt_ref, lse_ref, spread_ref, dmid_ref, w_ref, g_ref, cos_ref, sin_ref,
    din_out, gg_out, w_grad,
    kt_all, dk, dv, dqt, ht, dqkv,
):
    step_id = pl.program_id(0)
    i = nb - 1 - step_id
    bound = info[0]
    rb, d = x_ref.shape
    qw = QH * HD

    @pl.when(step_id == 0)
    def _():
        for j in range(nb):
            kt_all[j] = k_ref[j * rb : (j + 1) * rb, :].T
        dk[...] = jnp.zeros_like(dk)
        dv[...] = jnp.zeros_like(dv)
        gg_out[...] = jnp.zeros_like(gg_out)

    dqt[...] = jnp.zeros_like(dqt)

    def step(j, carry):
        rows = pl.ds(pl.multiple_of(j * rb, rb), rb)
        mask = seen_mask(bound, i, j, rb)
        keys = k_ref[rows, :]
        values = v_ref[rows, :]
        d_keys = dk[j]
        d_values = dv[j]
        for head in range(QH):
            cols = slice(head * rb, (head + 1) * rb)
            queries = q_ref[head]
            d_out = datt_ref[head]
            scores = dot_nt(keys, queries)
            probs = jnp.where(mask, jnp.exp2(scores * EXP_SCALE - lse_ref[head : head + 1, :]), 0.0)
            d_probs = dot_nt(values, d_out)
            d_scores = (probs * (d_probs - spread_ref[head : head + 1, :])).astype(BF)
            dqt[:, cols] += dot(kt_all[j], d_scores)
            d_keys = d_keys + dot(d_scores, queries)
            d_values = d_values + dot(probs.astype(BF), d_out)
        dk[j] = d_keys
        dv[j] = d_values
        return carry

    lax.fori_loop(first_block(bound, i, rb), i + 1, step, 0)
    rows = pl.ds(pl.multiple_of(i * rb, rb), rb)
    cosine, sine = cos_ref[...], sin_ref[...]
    scale = HD ** (-0.5)
    qgain, kgain = g_ref[4:5, :HD], g_ref[5:6, :HD]
    q_sum = jnp.zeros((1, HD), F32)
    for head in range(QH):
        grad = rotate(dqt[:, head * rb : (head + 1) * rb].T * scale, cosine, -sine)
        raw = raw_ref[:, head * HD : (head + 1) * HD].astype(F32)
        r = inv_rms(raw)
        unit = raw * r
        q_sum = q_sum + column_sum(grad * unit)
        dqkv[rows, head * HD : (head + 1) * HD] = norm_back(grad, unit, r, qgain).astype(BF)
    grad = rotate(dk[i] * scale, cosine, -sine)
    raw = raw_ref[:, qw : qw + HD].astype(F32)
    r = inv_rms(raw)
    unit = raw * r
    k_sum = column_sum(grad * unit)
    dqkv[rows, qw : qw + HD] = norm_back(grad, unit, r, kgain).astype(BF)
    dqkv[rows, qw + HD :] = dv[i].astype(BF)
    d_h = dot_nt(dqkv[rows, :], w_ref[...])
    x = x_ref[...].astype(F32)
    r = inv_rms(x)
    unit = x * r
    gain = g_ref[0:1, :]
    ht[:, rows] = (unit * gain).astype(BF).T
    din_out[...] = dmid_ref[...] + norm_back(d_h, unit, r, gain)
    rest = jnp.zeros((1, d - HD), F32)
    gg_out[...] += jnp.concatenate(
        [
            column_sum(d_h * unit),
            jnp.zeros((3, d), F32),
            jnp.concatenate([q_sum, rest], axis=1),
            jnp.concatenate([k_sum, rest], axis=1),
            jnp.zeros((2, d), F32),
        ],
        axis=0,
    )

    @pl.when(step_id == nb - 1)
    def _():
        width = w_grad.shape[1]
        for c in range(6):
            cols = slice(c * width // 6, (c + 1) * width // 6)
            w_grad[:, cols] = dot(ht[...], dqkv[:, cols]).astype(BF)


def back(info, x, q, k, v, raw, datt, lse, spread, dmid, w_qkv, gains, cosine, sine):

    rows, d = x.shape
    rb = RB
    nb = rows // rb
    whole = lambda a: pl.BlockSpec(a.shape, lambda i, *_: (0,) * a.ndim, pipeline_mode=pl.Buffered(1))
    row = lambda width: pl.BlockSpec((rb, width), lambda i, *_: (nb - 1 - i, 0))
    heads = pl.BlockSpec((QH, rb, HD), lambda i, *_: (0, nb - 1 - i, 0))
    vec = pl.BlockSpec((8, rb), lambda i, *_: (0, nb - 1 - i))
    qw = QH * HD
    return pl.pallas_call(
        functools.partial(back_kernel, nb),
        grid_spec=pltpu.PrefetchScalarGridSpec(
            num_scalar_prefetch=1,
            grid=(nb,),
            in_specs=[
                row(d), heads, whole(k), whole(v), row(qw + HD), heads, vec, vec, row(d),
                whole(w_qkv), whole(gains), row(HD // 2), row(HD // 2),
            ],
            out_specs=[
                row(d),
                pl.BlockSpec((8, d), lambda i, *_: (0, 0)),
                pl.BlockSpec(w_qkv.shape, lambda i, *_: (0, 0)),
            ],
            scratch_shapes=[
                pltpu.VMEM((nb, HD, rb), BF),
                pltpu.VMEM((nb, rb, HD), F32),
                pltpu.VMEM((nb, rb, HD), F32),
                pltpu.VMEM((HD, QH * rb), F32),
                pltpu.VMEM((d, rows), BF),
                pltpu.VMEM((rows, qw + 2 * HD), BF),
            ],
        ),
        out_shape=[
            jax.ShapeDtypeStruct((rows, d), F32),
            jax.ShapeDtypeStruct((8, d), F32),
            jax.ShapeDtypeStruct(w_qkv.shape, BF),
        ],
        compiler_params=pltpu.CompilerParams(vmem_limit_bytes=56 * 2**20),
        cost_estimate=pl.CostEstimate(flops=20 * 10**9, bytes_accessed=30 * 10**6, transcendentals=4 * 10**6),
        name="back",
    )(info, x, q, k, v, raw, datt, lse, spread, dmid, w_qkv, gains, cosine, sine)


def tables(rows):
    freqs = np.float32(THETA) ** (-(np.arange(HD // 2, dtype=np.float32) * np.float32(2.0 / HD)))
    angles = np.arange(rows, dtype=np.float32)[:, None] * freqs[None, :].astype(np.float32)
    return np.cos(angles).astype(np.float32), np.sin(angles).astype(np.float32)


def packing(seq_lengths, seq_device, device):
    count = seq_lengths.shape[0]
    ids = jnp.arange(count, dtype=jnp.int32)
    mine = seq_device == device
    first = jnp.min(jnp.where(mine, ids, count))
    bound = jnp.sum(jnp.where(ids == first, seq_lengths, 0), dtype=jnp.int32)
    total = jnp.sum(jnp.where(mine, seq_lengths, 0), dtype=jnp.int32)
    return jnp.stack([bound, total]).astype(jnp.int32)


def local_step(info, tokens, cotangent, w_qkv, w_project, w_gu, w_down, gains):
    cosine, sine = (jnp.asarray(t) for t in tables(tokens.shape[0]))
    q, k, v, raw, att, lse, branch, mid = attend(info, tokens, w_qkv, w_project, gains, cosine, sine)
    act, dmid, datt, spread, gg_ff, gu_grad, down_grad, project_grad = feed(
        info, mid, branch, att, cotangent, w_gu, w_down, w_project, gains
    )
    din, gg_at, qkv_grad = back(
        info, tokens, q, k, v, raw, datt, lse, spread, dmid, w_qkv, gains, cosine, sine
    )
    return act, din, gg_ff + gg_at, qkv_grad, project_grad, gu_grad, down_grad


def scatter(grad):
    return lax.psum_scatter(grad, "shard", scatter_dimension=0, tiled=True)


def scatter_columns(grad, n_shard):
    if grad.shape[0] == n_shard:
        return scatter(grad)[0].T
    turned = grad.transpose(0, 2, 1)
    return scatter(turned.reshape(-1, turned.shape[2]))


def rep_sum(part):
    return lax.psum(part.astype(F32), "rep")


def gather(part):
    return lax.all_gather(part, "shard", axis=0, tiled=True)


def shards(
    tokens, seq_lengths, seq_device, w_query, w_keyval, w_project, w_gate, w_upward, w_down,
    gain_input, gain_query, gain_key, gain_attend, gain_before, gain_after, cotangent,
):
    n_shard = lax.axis_size("shard")
    me = lax.axis_index("shard")
    device = me * lax.axis_size("rep") + lax.axis_index("rep")
    info = packing(seq_lengths, seq_device, device)
    part = w_query.shape[0]
    d = part * n_shard
    ff = w_gate.shape[1]
    qw = w_query.shape[1]
    head_part = gain_query.shape[0]
    padded = [
        jnp.pad(g, (0, 128 - g.shape[0]))
        for g in (gain_input, gain_attend, gain_before, gain_after, gain_query, gain_key)
    ]
    own_gains = jnp.stack(padded + [jnp.zeros_like(padded[0])] * 10)
    wide = gather(own_gains).reshape(n_shard, 16, 128)
    full = lambda row, size: wide[:, row, :size].reshape(n_shard * size)
    rest = jnp.zeros((d - HD,), BF)
    gains = jnp.stack(
        [full(0, part), full(1, part), full(2, part), full(3, part)]
        + [jnp.concatenate([full(row, head_part), rest]) for row in (4, 5)]
        + [jnp.zeros((d,), BF)] * 2
    ).astype(F32)
    w_qkv = gather(jnp.concatenate([w_query, w_keyval], axis=1))
    project = gather(w_project)
    w_gu = gather(jnp.concatenate([w_gate, w_upward], axis=1))
    down = gather(w_down)
    act, din, gg, qkv_grad, project_grad, gu_grad, down_grad = local_step(
        info, tokens, cotangent, w_qkv, project, w_gu, down, gains
    )
    sum_gu = rep_sum(scatter(gu_grad))
    sum_down = rep_sum(scatter_columns(down_grad, n_shard))
    sum_project = rep_sum(scatter_columns(project_grad, n_shard))
    sum_qkv = rep_sum(scatter(qkv_grad))
    sums = lax.psum(gg, ("shard", "rep"))
    own = lambda row, size: lax.dynamic_slice(sums, (row, me * size), (1, size))[0]
    return (
        act, din, sum_qkv[:, :qw], sum_qkv[:, qw:], sum_project, sum_gu[:, :ff], sum_gu[:, ff:], sum_down,
        own(0, part), own(4, head_part), own(5, head_part), own(1, part), own(2, part), own(3, part),
    )


def solution(mesh):
    rows, weight, gain = P(("shard", "rep"), None), P("shard", None), P("shard")
    return jax.shard_map(
        shards,
        mesh=mesh,
        in_specs=(rows, P(), P()) + (weight,) * 6 + (gain,) * 6 + (rows,),
        out_specs=(rows, rows) + (weight,) * 6 + (gain,) * 6,
        check_vma=False,
    )
```

```python
import functools
import math

import jax
import jax.numpy as jnp
import numpy as np
from jax import lax
from jax.experimental import pallas as pl
from jax.experimental.pallas import tpu as pltpu
from jax.sharding import PartitionSpec as P

QH = 4
HD = 256
EPS = 1e-06
THETA = 1000000.0
RB = 256
COLUMN_STEPS = 8
F32 = jnp.float32
BF = jnp.bfloat16
EXP_SCALE = HD ** (-0.5) * math.log2(math.e)
MESH = pl.DeviceIdType.MESH
GELU_C = math.sqrt(2.0 / math.pi)


def dot(left, right):
    return lax.dot_general(left, right, (((1,), (0,)), ((), ())), preferred_element_type=F32)


def dot_nt(left, right):
    return lax.dot_general(left, right, (((1,), (1,)), ((), ())), preferred_element_type=F32)


def inv_rms(value):
    return lax.rsqrt(jnp.mean(value * value, axis=-1, keepdims=True) + EPS)


def rotate(value, cosine, sine):
    first, second = value[:, : HD // 2], value[:, HD // 2 :]
    return jnp.concatenate(
        [first * cosine - second * sine, second * cosine + first * sine], axis=-1
    )


def seen_mask(bound, query_block, key_block, rb):
    keys = key_block * rb + lax.broadcasted_iota(jnp.int32, (rb, rb), 0)
    rows = query_block * rb + lax.broadcasted_iota(jnp.int32, (rb, rb), 1)
    return (keys <= rows) & (keys >= jnp.where(rows >= bound, bound, 0))


def first_block(bound, block, rb):
    return jnp.where(block * rb >= bound, bound // rb, 0)

class Places:
    def __init__(self):
        s, r = lax.axis_index("shard"), lax.axis_index("rep")
        z, self.c = lax.div(s, 2), lax.rem(s, 2)
        self.y, self.x = lax.div(r, 2), lax.rem(r, 2)
        self.s, self.r, self.z = s, r, z
        zs = [z, z + 1 - 2 * lax.rem(z, 2), z + 2 - 4 * lax.div(z, 2), 3 - z]
        self.zs = zs
        self.across = r + 1 - 2 * self.x
        self.along = r + 2 - 4 * self.y
        self.shards = [2 * zp + self.c for zp in zs]
        self.core = (s + 1 - 2 * self.c, r)
        self.xdev = (s, self.across)
        self.ydev = (s, self.along)
        self.zdev = [None] + [(self.shards[k], r) for k in (1, 2, 3)]
        self.all = [self.core, self.xdev, self.ydev] + self.zdev[1:]

    def greet(self):
        barrier = pltpu.get_barrier_semaphore()
        for device in self.all:
            pl.semaphore_signal(barrier, inc=1, device_id=device, device_id_type=MESH)
        pl.semaphore_wait(barrier, len(self.all))


class Gather:
    SEMS = 20

    def __init__(self, at, parts, fulls, send, recv):
        self.at, self.parts, self.fulls, self.send, self.recv = at, parts, fulls, send, recv

    def split(self, n):
        rows, cols = self.parts[n].shape
        if cols % 512 == 0:
            width = cols // 4
            return True, width, min(width, (width // 128 + 1) // 2 * 128)
        return False, rows // 4, rows // 8

    def view(self, n, ref, shard, q, half=None):
        by_cols, size, first = self.split(n)
        rows = self.parts[n].shape[0]
        begin, length = q * size, size
        if half == 0:
            length = first
        if half == 1:
            begin, length = begin + first, size - first
        base = 0 if shard is None else shard * rows
        if by_cols:
            return ref.at[pl.ds(pl.multiple_of(base, 16), rows), pl.ds(pl.multiple_of(begin, 128), length)]
        return ref.at[pl.ds(pl.multiple_of(base + begin, 16), length), :]

    def copy(self, n, idx, src, dst, device):
        return pltpu.make_async_remote_copy(
            src_ref=src, dst_ref=dst, send_sem=self.send.at[n, idx], recv_sem=self.recv.at[n, idx],
            device_id=device, device_id_type=MESH,
        )

    def rows_of(self, n, shard):
        rows = self.parts[n].shape[0]
        return self.fulls[n].at[pl.ds(pl.multiple_of(shard * rows, 16), rows), :]

    def out_z(self, n, k):
        at = self.at
        return self.copy(
            n, k - 1, self.view(n, self.parts[n], None, at.r), self.view(n, self.fulls[n], at.s, at.r), at.zdev[k]
        )

    def out_xy(self, n, k, way):
        at = self.at
        piece = self.view(n, self.fulls[n], at.shards[k], at.r)
        return self.copy(n, 3 + 3 * way + k - 1, piece, piece, (at.xdev, at.ydev)[way])

    def halves(self, n):
        _, size, first = self.split(n)
        return (0,) if size == first else (0, 1)

    def out_diag(self, n, k, half):
        at = self.at
        q, device = ((at.across, at.ydev), (at.along, at.xdev))[half]
        piece = self.view(n, self.fulls[n], at.shards[k], q, half)
        return self.copy(n, 9 + 3 * half + k - 1, piece, piece, device)

    def out_core(self, n, k):
        src = self.parts[n] if k == 0 else self.rows_of(n, self.at.shards[k])
        return self.copy(n, 15 + k, src, self.rows_of(n, self.at.shards[k]), self.at.core)

    def own(self, n):
        return pltpu.make_async_copy(self.parts[n], self.rows_of(n, self.at.s), self.send.at[n, 19])

    def first(self):
        for n in range(len(self.parts)):
            for k in (1, 2, 3):
                self.out_z(n, k).start()
        for n in range(len(self.parts)):
            self.out_core(n, 0).start()
            self.own(n).start()

    def second(self, n, k):
        self.out_z(n, k).wait_recv()
        self.out_xy(n, k, 0).start()
        self.out_xy(n, k, 1).start()

    def third(self, n, k):
        self.out_xy(n, k, 0).wait_recv()
        self.out_diag(n, k, 0).start()
        self.out_xy(n, k, 1).wait_recv()
        if 1 in self.halves(n):
            self.out_diag(n, k, 1).start()

    def fourth(self, n, k):
        for half in self.halves(n):
            self.out_diag(n, k, half).wait_recv()
        self.out_core(n, k).start()

    def last(self):
        for n in range(len(self.parts)):
            self.own(n).wait()
            for k in range(4):
                self.out_core(n, k).wait()
            for k in (1, 2, 3):
                self.out_z(n, k).wait_send()
                self.out_xy(n, k, 0).wait_send()
                self.out_xy(n, k, 1).wait_send()
                for half in self.halves(n):
                    self.out_diag(n, k, half).wait_send()

    def middle(self):
        steps = []
        todo = [(n, k) for n in range(len(self.parts)) for k in (1, 2, 3)]
        for t in range(len(todo) + 2):
            for lag, stage in ((0, self.second), (1, self.third), (2, self.fourth)):
                if 0 <= t - lag < len(todo):
                    steps.append((stage, *todo[t - lag]))
        return steps

    @staticmethod
    def sems(count):
        return [pltpu.SemaphoreType.DMA((count, Gather.SEMS)), pltpu.SemaphoreType.DMA((count, Gather.SEMS))]


def gather_kernel(count, *refs):
    parts, fulls = refs[:count], refs[count : 2 * count]
    send, recv = refs[2 * count :]
    at = Places()
    work = Gather(at, parts, fulls, send, recv)
    at.greet()
    work.first()
    for stage, n, k in work.middle():
        stage(n, k)
    work.last()


def gather_all(parts, collective_id):
    count = len(parts)
    size = sum(8 * p.size * 2 for p in parts)
    return pl.pallas_call(
        functools.partial(gather_kernel, count),
        out_shape=[jax.ShapeDtypeStruct((8 * p.shape[0], p.shape[1]), p.dtype) for p in parts],
        in_specs=[pl.BlockSpec(memory_space=pl.ANY)] * count,
        out_specs=[pl.BlockSpec(memory_space=pl.ANY)] * count,
        scratch_shapes=Gather.sems(count),
        compiler_params=pltpu.CompilerParams(collective_id=collective_id, has_side_effects=True),
        cost_estimate=pl.CostEstimate(flops=0, bytes_accessed=size, transcendentals=0),
        name="collect",
    )(*parts)


class Reduce:
    SEMS = 16

    def __init__(self, at, splits, grads, bufs, send, recv):
        self.at, self.splits, self.grads, self.bufs, self.send, self.recv = at, splits, grads, bufs, send, recv

    @staticmethod
    def sizes(a, b, rows, cols):
        piece = (rows, cols)
        shapes = [
            (4, 2, 2, a + b) + piece,
            (4, 2, 2, a + b) + piece,
            (4, 2, a) + piece,
            (4, 2, b) + piece,
            (4, a) + piece,
            (4, b) + piece,
            (3, a + b) + piece,
            (2, 2, a + b) + piece,
        ]
        return [pltpu.VMEM(shape, BF) for shape in shapes]

    def copy(self, n, idx, src, dst, device):
        return pltpu.make_async_remote_copy(
            src_ref=src, dst_ref=dst, send_sem=self.send.at[n, idx], recv_sem=self.recv.at[n, idx],
            device_id=device, device_id_type=MESH,
        )

    def own(self, n):
        return pltpu.make_async_copy(self.grads[n].at[:, self.at.c], self.bufs[n][0], self.send.at[n, 15])

    def out_core(self, n):
        return self.copy(n, 0, self.grads[n].at[:, 1 - self.at.c], self.bufs[n][1], self.at.core)

    def out_1(self, n, way):
        at, (a, b) = self.at, self.splits[n]
        total = self.bufs[n][0]
        if way == 0:
            return self.copy(n, 1, total.at[:, :, 1 - at.x, pl.ds(0, a)], self.bufs[n][2], at.xdev)
        return self.copy(n, 2, total.at[:, 1 - at.y, :, pl.ds(a, b)], self.bufs[n][3], at.ydev)

    def out_2(self, n, way):
        at, (a, b) = self.at, self.splits[n]
        total = self.bufs[n][0]
        if way == 0:
            return self.copy(n, 3, total.at[:, 1 - at.y, at.x, pl.ds(0, a)], self.bufs[n][4], at.ydev)
        return self.copy(n, 4, total.at[:, at.y, 1 - at.x, pl.ds(a, b)], self.bufs[n][5], at.xdev)

    def out_z(self, n, k):
        at = self.at
        return self.copy(n, 4 + k, self.bufs[n][0].at[at.zs[k], at.y, at.x], self.bufs[n][6].at[k - 1], at.zdev[k])

    def out_final(self, n, way):
        at = self.at
        piece = self.bufs[n][7].at[at.y, at.x]
        return self.copy(n, 8 + way, piece, piece, (at.xdev, at.ydev)[way])

    def out_diag(self, n, way):
        at, (a, b) = self.at, self.splits[n]
        result = self.bufs[n][7]
        if way == 0:
            piece = result.at[at.y, 1 - at.x, pl.ds(0, a)]
            return self.copy(n, 10, piece, piece, at.ydev)
        piece = result.at[1 - at.y, at.x, pl.ds(a, b)]
        return self.copy(n, 11, piece, piece, at.xdev)

    def start(self, n):
        self.out_core(n).start()
        self.own(n).start()

    def one(self, n):
        total, other = self.bufs[n][0], self.bufs[n][1]
        a, b = self.splits[n]
        self.own(n).wait()
        self.out_core(n).wait_recv()

        def add(zp, carry):
            for y in range(2):
                for x in range(2):
                    for p in range(a + b):
                        total[zp, y, x, p] = (total[zp, y, x, p].astype(F32) + other[zp, y, x, p].astype(F32)).astype(BF)
            return carry

        lax.fori_loop(0, 4, add, 0)
        self.out_1(n, 0).start()
        self.out_1(n, 1).start()

    def two(self, n):
        total, at, (a, b) = self.bufs[n][0], self.at, self.splits[n]
        self.out_1(n, 0).wait()
        self.out_1(n, 1).wait()
        from_x, from_y = self.bufs[n][2], self.bufs[n][3]

        def add(zp, carry):
            for m in range(2):
                for p in range(a):
                    total[zp, m, at.x, p] = (total[zp, m, at.x, p].astype(F32) + from_x[zp, m, p].astype(F32)).astype(BF)
                for p in range(b):
                    total[zp, at.y, m, a + p] = (
                        total[zp, at.y, m, a + p].astype(F32) + from_y[zp, m, p].astype(F32)
                    ).astype(BF)
            return carry

        lax.fori_loop(0, 4, add, 0)
        self.out_2(n, 0).start()
        self.out_2(n, 1).start()

    def three(self, n):
        total, at, (a, b) = self.bufs[n][0], self.at, self.splits[n]
        self.out_2(n, 0).wait()
        self.out_2(n, 1).wait()
        from_y, from_x = self.bufs[n][4], self.bufs[n][5]

        def add(zp, carry):
            for p in range(a):
                total[zp, at.y, at.x, p] = (total[zp, at.y, at.x, p].astype(F32) + from_y[zp, p].astype(F32)).astype(BF)
            for p in range(b):
                total[zp, at.y, at.x, a + p] = (
                    total[zp, at.y, at.x, a + p].astype(F32) + from_x[zp, p].astype(F32)
                ).astype(BF)
            return carry

        lax.fori_loop(0, 4, add, 0)
        for k in (1, 2, 3):
            self.out_z(n, k).start()

    def four(self, n):
        total, result, from_z, at = self.bufs[n][0], self.bufs[n][7], self.bufs[n][6], self.at
        for k in (1, 2, 3):
            self.out_z(n, k).wait()
        for p in range(sum(self.splits[n])):
            value = total[at.z, at.y, at.x, p].astype(F32)
            for k in range(3):
                value = value + from_z[k, p].astype(F32)
            result[at.y, at.x, p] = value.astype(BF)
        self.out_final(n, 0).start()
        self.out_final(n, 1).start()

    def five(self, n):
        for way in range(2):
            self.out_final(n, way).wait_recv()
            self.out_diag(n, way).start()

    def six(self, n):
        for way in range(2):
            self.out_diag(n, way).wait()
            self.out_final(n, way).wait_send()
        self.out_core(n).wait_send()

    def stages(self):
        return [self.one, self.two, self.three, self.four, self.five, self.six]


class Small:
    SEMS = 6

    def __init__(self, at, value, total, inbox, send, recv):
        self.at, self.value, self.total, self.inbox, self.send, self.recv = at, value, total, inbox, send, recv

    def copy(self, idx):
        at = self.at
        slot, device = idx, at.all[idx]
        return pltpu.make_async_remote_copy(
            src_ref=self.total.at[min(idx, 3)], dst_ref=self.inbox.at[slot], send_sem=self.send.at[idx],
            recv_sem=self.recv.at[idx], device_id=device, device_id_type=MESH,
        )

    def start(self):
        self.total[0] = self.value[...]
        self.copy(0).start()

    def next(self, step):
        if step == 3:
            for idx in (3, 4, 5):
                self.copy(idx).wait()
            self.total[4] = self.total[3] + self.inbox[3] + self.inbox[4] + self.inbox[5]
            return
        self.copy(step).wait()
        self.total[step + 1] = self.total[step] + self.inbox[step]
        for idx in (step + 1,) if step < 2 else (3, 4, 5):
            self.copy(idx).start()


def unpack(result, outs, turned):
    _, _, pieces, rows, cols = result.shape
    if turned:
        for y in range(2):
            for x in range(2):
                for p in range(pieces):
                    turned_rows = (2 * y + x) * pieces + p
                    outs[0][turned_rows * rows : (turned_rows + 1) * rows, :] = result[y, x, p].astype(F32)
        return
    begin = 0
    for y in range(2):
        for x in range(2):
            for p in range(pieces):
                out = outs[0] if begin < outs[0].shape[1] else outs[1]
                col = begin if begin < outs[0].shape[1] else begin - outs[0].shape[1]
                out[:, col : col + cols] = result[y, x, p].astype(F32)
                begin += cols


def reduce_kernel(splits, turned, n_outs, *refs):
    count = len(splits)
    grads, small_in = refs[:count], refs[count]
    outs = refs[count + 1 : count + 1 + sum(n_outs)]
    small_out = refs[count + 1 + sum(n_outs)]
    scratch = list(refs[count + 2 + sum(n_outs) :])
    bufs = [[scratch.pop(0) for _ in range(8)] for _ in range(count)]
    total, inbox, send, recv, small_send, small_recv = scratch
    at = Places()
    work = Reduce(at, splits, grads, bufs, send, recv)
    small = Small(at, small_in, total, inbox, small_send, small_recv)
    at.greet()
    small.start()
    for n in range(count):
        work.start(n)
    for step, stage in enumerate(work.stages()):
        if step < 4:
            small.next(step)
        for n in range(count):
            stage(n)
    small_out[...] = total[4]
    for n in range(count):
        unpack(bufs[n][7], outs[sum(n_outs[:n]) : sum(n_outs[: n + 1])], turned[n])


def reduce_all(grads, splits, turned, out_shapes, small, collective_id):
    count = len(grads)
    shaped = [g.reshape(4, 2, 2, 2, g.shape[1] // 4, *g.shape[2:]) for g in grads]
    flat = [s for shapes in out_shapes for s in shapes]
    bufs = [b for g, (a, c) in zip(shaped, splits) for b in Reduce.sizes(a, c, *g.shape[5:])]
    vmem = pl.BlockSpec(memory_space=pltpu.VMEM)
    return pl.pallas_call(
        functools.partial(reduce_kernel, tuple(splits), tuple(turned), tuple(len(s) for s in out_shapes)),
        out_shape=[jax.ShapeDtypeStruct(s, F32) for s in flat] + [jax.ShapeDtypeStruct(small.shape, F32)],
        in_specs=[pl.BlockSpec(memory_space=pl.ANY)] * count + [vmem],
        out_specs=[vmem] * (len(flat) + 1),
        scratch_shapes=bufs
        + [
            pltpu.VMEM((5, *small.shape), F32),
            pltpu.VMEM((6, *small.shape), F32),
            pltpu.SemaphoreType.DMA((count, Reduce.SEMS)),
            pltpu.SemaphoreType.DMA((count, Reduce.SEMS)),
            pltpu.SemaphoreType.DMA((Small.SEMS,)),
            pltpu.SemaphoreType.DMA((Small.SEMS,)),
        ],
        compiler_params=pltpu.CompilerParams(
            collective_id=collective_id, has_side_effects=True, vmem_limit_bytes=50 * 2**20
        ),
        cost_estimate=pl.CostEstimate(flops=0, bytes_accessed=30 * 10**6, transcendentals=0),
        name="total",
    )(*shaped, small)


def attend_kernel(
    info, x_ref, wq_ref, wkv_ref, wp_ref, g_ref, cos_ref, sin_ref,
    q_out, k_out, v_out, raw_out, att_out, lse_out, branch_out, mid_out,
    k_all, vt_all, acc, den,
):
    i = pl.program_id(0)
    bound = info[0]
    rb = x_ref.shape[0]
    d = x_ref.shape[1]
    x = x_ref[...].astype(F32)
    h = (x * inv_rms(x) * g_ref[0:1, :]).astype(BF)
    cosine, sine = cos_ref[...], sin_ref[...]
    qgain, kgain = g_ref[4:5, :HD], g_ref[5:6, :HD]
    for head in range(QH):
        raw = dot(h, wq_ref[:, head * HD : (head + 1) * HD])
        raw_out[:, head * HD : (head + 1) * HD] = raw.astype(BF)
        q_out[head] = rotate(raw * inv_rms(raw) * qgain, cosine, sine).astype(BF)
    raw = dot(h, wkv_ref[:, :HD])
    raw_out[:, QH * HD :] = raw.astype(BF)
    keys = rotate(raw * inv_rms(raw) * kgain, cosine, sine).astype(BF)
    values = dot(h, wkv_ref[:, HD:]).astype(BF)
    k_out[...] = keys
    v_out[...] = values
    k_all[i] = keys
    vt_all[i] = values.T
    acc[...] = jnp.zeros_like(acc)
    den[...] = jnp.zeros_like(den)

    def step(j, carry):
        mask = seen_mask(bound, i, j, rb)
        for head in range(QH):
            cols = slice(head * rb, (head + 1) * rb)
            scores = dot_nt(k_all[j], q_out[head])
            probs = jnp.where(mask, jnp.exp2(scores * EXP_SCALE), 0.0)
            den[:, cols] += jnp.sum(probs.reshape(rb // 8, 8, rb), axis=0)
            acc[:, cols] += dot(vt_all[j], probs.astype(BF))
        return carry

    lax.fori_loop(first_block(bound, i, rb), i + 1, step, 0)
    lse = []
    for head in range(QH):
        cols = slice(head * rb, (head + 1) * rb)
        total = jnp.sum(den[:, cols], axis=0, keepdims=True)
        lse.append(jnp.log2(total))
        att_out[:, head * HD : (head + 1) * HD] = (acc[:, cols] * (1.0 / total)).T.astype(BF)
    lse_out[...] = jnp.concatenate(lse + lse, axis=0)
    branch = dot(att_out[...], wp_ref[...])
    branch_out[...] = branch
    mid_out[...] = x + branch * inv_rms(branch) * g_ref[1:2, :]


def attend(info, x, w_query, w_keyval, w_project, gains, cosine, sine):
    rows, d = x.shape
    rb = RB
    nb = rows // rb
    whole = lambda a: pl.BlockSpec(a.shape, lambda i, *_: (0,) * a.ndim, pipeline_mode=pl.Buffered(1))
    row = lambda width: pl.BlockSpec((rb, width), lambda i, *_: (i, 0))
    qw = QH * HD
    return pl.pallas_call(
        attend_kernel,
        grid_spec=pltpu.PrefetchScalarGridSpec(
            num_scalar_prefetch=1,
            grid=(nb,),
            in_specs=[row(d), whole(w_query), whole(w_keyval), whole(w_project), whole(gains), row(HD // 2), row(HD // 2)],
            out_specs=[
                pl.BlockSpec((QH, rb, HD), lambda i, *_: (0, i, 0)),
                row(HD), row(HD), row(qw + HD), row(qw),
                pl.BlockSpec((8, rb), lambda i, *_: (0, i)),
                row(d), row(d),
            ],
            scratch_shapes=[
                pltpu.VMEM((nb, rb, HD), BF),
                pltpu.VMEM((nb, HD, rb), BF),
                pltpu.VMEM((HD, QH * rb), F32),
                pltpu.VMEM((8, QH * rb), F32),
            ],
        ),
        out_shape=[
            jax.ShapeDtypeStruct((QH, rows, HD), BF),
            jax.ShapeDtypeStruct((rows, HD), BF),
            jax.ShapeDtypeStruct((rows, HD), BF),
            jax.ShapeDtypeStruct((rows, qw + HD), BF),
            jax.ShapeDtypeStruct((rows, qw), BF),
            jax.ShapeDtypeStruct((8, rows), F32),
            jax.ShapeDtypeStruct((rows, d), F32),
            jax.ShapeDtypeStruct((rows, d), F32),
        ],
        compiler_params=pltpu.CompilerParams(vmem_limit_bytes=56 * 2**20),
        cost_estimate=pl.CostEstimate(flops=14 * 10**9, bytes_accessed=30 * 10**6, transcendentals=4 * 10**6),
        name="attend",
    )(info, x, w_query, w_keyval, w_project, gains, cosine, sine)


def norm_back(grad, unit, r, gain):
    scaled = grad * gain
    return r * (scaled - unit * jnp.mean(scaled * unit, axis=-1, keepdims=True))


def column_sum(value):
    return jnp.sum(value, axis=0, keepdims=True)


def feed_kernel(
    nb, n_cols, info, mid_ref, branch_ref, att_ref, cot_ref, attc_ref, wg_ref, wu_ref, wd_ref, wp_ref, g_ref,
    act_out, dmid_out, datt_out, spread_out, gg_out, gu_grad, down_grad, project_grad,
    hid, dgu, h2t, dft, dbt, act_s, mul_s,
):
    i = pl.program_id(0)
    rb, d = mid_ref.shape
    ff = wd_ref.shape[0]
    fc = ff // 4

    @pl.when(i < nb)
    def _():
        start = pl.multiple_of(i * rb, rb)
        rows = pl.ds(start, rb)
        mid = mid_ref[...]
        r_mid = inv_rms(mid)
        unit_mid = mid * r_mid
        h2 = (unit_mid * g_ref[2:3, :]).astype(BF)
        h2t[:, rows] = h2.T
        for c in range(4):
            cols = slice(c * fc, (c + 1) * fc)
            gate = dot(h2, wg_ref[:, cols])
            up = dot(h2, wu_ref[:, cols])
            sq = gate * gate
            th = jnp.tanh(GELU_C * gate * (1.0 + 0.044715 * sq))
            half = 0.5 + 0.5 * th
            act = gate * half
            slope = half + 0.5 * gate * (1.0 - th * th) * (GELU_C * (1.0 + (3 * 0.044715) * sq))
            hid[rows, cols] = (act * up).astype(BF)
            act_s[:, cols] = act
            mul_s[:, cols] = up * slope
        ffn = dot(hid[rows, :], wd_ref[...])
        r_ffn = inv_rms(ffn)
        unit_ffn = ffn * r_ffn
        after = g_ref[3:4, :]
        act_out[...] = (mid + unit_ffn * after).astype(BF)
        row_ids = start + lax.broadcasted_iota(jnp.int32, (rb, 1), 0)
        ups = jnp.where(row_ids < info[1], cot_ref[...].astype(F32), 0.0)
        d_ffn = norm_back(ups, unit_ffn, r_ffn, after).astype(BF)
        dft[:, rows] = d_ffn.T
        for c in range(4):
            cols = slice(c * fc, (c + 1) * fc)
            d_hid = dot_nt(d_ffn, wd_ref[cols, :])
            dgu[rows, cols] = (d_hid * mul_s[:, cols]).astype(BF)
            dgu[rows, ff + c * fc : ff + (c + 1) * fc] = (d_hid * act_s[:, cols]).astype(BF)
        d_h2 = dot_nt(dgu[rows, :ff], wg_ref[...]) + dot_nt(dgu[rows, ff:], wu_ref[...])
        d_mid = ups + norm_back(d_h2, unit_mid, r_mid, g_ref[2:3, :])
        dmid_out[...] = d_mid
        branch = branch_ref[...]
        r_br = inv_rms(branch)
        unit_br = branch * r_br
        d_br = norm_back(d_mid, unit_br, r_br, g_ref[1:2, :]).astype(BF)
        dbt[:, rows] = d_br.T
        d_att = dot_nt(d_br, wp_ref[...])
        datt_low = d_att.astype(BF)
        prod = datt_low.astype(F32) * att_ref[...].astype(F32)
        spread = []
        for head in range(QH):
            cols = slice(head * HD, (head + 1) * HD)
            datt_out[head] = datt_low[:, cols]
            spread.append(jnp.sum(prod[:, cols], axis=1, keepdims=True))
        wide = jnp.concatenate(spread + [jnp.zeros((rb, 128 - QH), F32)], axis=1)
        spread_out[...] = wide.T[:8, :]
        sums = jnp.concatenate(
            [
                jnp.zeros((1, d), F32),
                column_sum(d_mid * unit_br),
                column_sum(d_h2 * unit_mid),
                column_sum(ups * unit_ffn),
                jnp.zeros((4, d), F32),
            ],
            axis=0,
        )

        @pl.when(i == 0)
        def _():
            gg_out[...] = jnp.zeros_like(gg_out)

        gg_out[...] += sums

    @pl.when(i >= nb)
    def _():
        s = i - nb
        wide = 2 * ff // n_cols
        for c in range(2):
            part = wide // 2
            cols = pl.ds(pl.multiple_of(s * wide + c * part, part), part)
            value = dot(h2t[...], dgu[:, cols]).astype(BF)
            gu_grad[:, 0, :, c * part : (c + 1) * part] = value.reshape(n_cols, d // n_cols, part)
        cols = pl.ds(pl.multiple_of(s * (ff // n_cols), ff // n_cols), ff // n_cols)
        down_grad[0] = dot(dft[...], hid[:, cols]).astype(BF)
        project_grad[0] = dot(dbt[...], attc_ref[...]).astype(BF)


def feed(info, mid, branch, att, cot, w_gate, w_upward, w_down, w_project, gains):
    rows, d = mid.shape
    ff = w_down.shape[0]
    qw = att.shape[1]
    rb = RB
    nb = rows // rb
    whole = lambda a: pl.BlockSpec(a.shape, lambda i, *_: (0,) * a.ndim, pipeline_mode=pl.Buffered(1))
    blk = lambda i: jnp.minimum(i, nb - 1)
    col = lambda i: jnp.maximum(i - nb, 0)
    row = lambda width: pl.BlockSpec((rb, width), lambda i, *_: (blk(i), 0))
    nc = COLUMN_STEPS

    return pl.pallas_call(
        functools.partial(feed_kernel, nb, nc),
        grid_spec=pltpu.PrefetchScalarGridSpec(
            num_scalar_prefetch=1,
            grid=(nb + nc,),
            in_specs=[
                row(d), row(d), row(qw), row(d),
                pl.BlockSpec((rows, qw // nc), lambda i, *_: (0, col(i))),
                whole(w_gate), whole(w_upward), whole(w_down), whole(w_project), whole(gains),
            ],
            out_specs=[
                row(d), row(d),
                pl.BlockSpec((QH, rb, HD), lambda i, *_: (0, blk(i), 0)),
                pl.BlockSpec((8, rb), lambda i, *_: (0, blk(i))),
                pl.BlockSpec((8, d), lambda i, *_: (0, 0)),
                pl.BlockSpec((nc, 1, d // nc, 2 * ff // nc), lambda i, *_: (0, col(i), 0, 0)),
                pl.BlockSpec((1, d, ff // nc), lambda i, *_: (col(i), 0, 0)),
                pl.BlockSpec((1, d, qw // nc), lambda i, *_: (col(i), 0, 0)),
            ],
            scratch_shapes=[
                pltpu.VMEM((rows, ff), BF),
                pltpu.VMEM((rows, 2 * ff), BF),
                pltpu.VMEM((d, rows), BF),
                pltpu.VMEM((d, rows), BF),
                pltpu.VMEM((d, rows), BF),
                pltpu.VMEM((rb, ff), F32),
                pltpu.VMEM((rb, ff), F32),
            ],
        ),
        out_shape=[
            jax.ShapeDtypeStruct((rows, d), BF),
            jax.ShapeDtypeStruct((rows, d), F32),
            jax.ShapeDtypeStruct((QH, rows, HD), BF),
            jax.ShapeDtypeStruct((8, rows), F32),
            jax.ShapeDtypeStruct((8, d), F32),
            jax.ShapeDtypeStruct((nc, nc, d // nc, 2 * ff // nc), BF),
            jax.ShapeDtypeStruct((nc, d, ff // nc), BF),
            jax.ShapeDtypeStruct((nc, d, qw // nc), BF),
        ],
        compiler_params=pltpu.CompilerParams(vmem_limit_bytes=60 * 2**20),
        cost_estimate=pl.CostEstimate(flops=42 * 10**9, bytes_accessed=50 * 10**6, transcendentals=4 * 10**6),
        name="feed",
    )(info, mid, branch, att, cot, att, w_gate, w_upward, w_down, w_project, gains)


def back_kernel(
    nb, info, x_ref, q_ref, k_ref, v_ref, raw_ref, datt_ref, lse_ref, spread_ref, dmid_ref, wq_ref, wkv_ref, g_ref, gg_ref, cos_ref, sin_ref,
    din_out, gg_out, w_grad,
    kt_all, dk, dv, dqt, ht, dqkv,
):
    step_id = pl.program_id(0)
    i = nb - 1 - step_id
    bound = info[0]
    rb, d = x_ref.shape
    qw = QH * HD

    @pl.when(step_id == 0)
    def _():
        for j in range(nb):
            kt_all[j] = k_ref[j * rb : (j + 1) * rb, :].T
        dk[...] = jnp.zeros_like(dk)
        dv[...] = jnp.zeros_like(dv)
        gg_out[...] = gg_ref[...]

    dqt[...] = jnp.zeros_like(dqt)

    def step(j, carry):
        rows = pl.ds(pl.multiple_of(j * rb, rb), rb)
        mask = seen_mask(bound, i, j, rb)
        keys = k_ref[rows, :]
        values = v_ref[rows, :]
        d_keys = dk[j]
        d_values = dv[j]
        for head in range(QH):
            cols = slice(head * rb, (head + 1) * rb)
            queries = q_ref[head]
            d_out = datt_ref[head]
            scores = dot_nt(keys, queries)
            probs = jnp.where(mask, jnp.exp2(scores * EXP_SCALE - lse_ref[head : head + 1, :]), 0.0)
            d_probs = dot_nt(values, d_out)
            d_scores = (probs * (d_probs - spread_ref[head : head + 1, :])).astype(BF)
            dqt[:, cols] += dot(kt_all[j], d_scores)
            d_keys = d_keys + dot(d_scores, queries)
            d_values = d_values + dot(probs.astype(BF), d_out)
        dk[j] = d_keys
        dv[j] = d_values
        return carry

    lax.fori_loop(first_block(bound, i, rb), i + 1, step, 0)
    rows = pl.ds(pl.multiple_of(i * rb, rb), rb)
    cosine, sine = cos_ref[...], sin_ref[...]
    scale = HD ** (-0.5)
    qgain, kgain = g_ref[4:5, :HD], g_ref[5:6, :HD]
    q_sum = jnp.zeros((1, HD), F32)
    for head in range(QH):
        grad = rotate(dqt[:, head * rb : (head + 1) * rb].T * scale, cosine, -sine)
        raw = raw_ref[:, head * HD : (head + 1) * HD].astype(F32)
        r = inv_rms(raw)
        unit = raw * r
        q_sum = q_sum + column_sum(grad * unit)
        dqkv[rows, head * HD : (head + 1) * HD] = norm_back(grad, unit, r, qgain).astype(BF)
    grad = rotate(dk[i] * scale, cosine, -sine)
    raw = raw_ref[:, qw : qw + HD].astype(F32)
    r = inv_rms(raw)
    unit = raw * r
    k_sum = column_sum(grad * unit)
    dqkv[rows, qw : qw + HD] = norm_back(grad, unit, r, kgain).astype(BF)
    dqkv[rows, qw + HD :] = dv[i].astype(BF)
    d_h = dot_nt(dqkv[rows, :qw], wq_ref[...]) + dot_nt(dqkv[rows, qw:], wkv_ref[...])
    x = x_ref[...].astype(F32)
    r = inv_rms(x)
    unit = x * r
    gain = g_ref[0:1, :]
    ht[:, rows] = (unit * gain).astype(BF).T
    din_out[...] = dmid_ref[...] + norm_back(d_h, unit, r, gain)
    rest = jnp.zeros((1, d - HD), F32)
    gg_out[...] += jnp.concatenate(
        [
            column_sum(d_h * unit),
            jnp.zeros((3, d), F32),
            jnp.concatenate([q_sum, rest], axis=1),
            jnp.concatenate([k_sum, rest], axis=1),
            jnp.zeros((2, d), F32),
        ],
        axis=0,
    )

    @pl.when(step_id == nb - 1)
    def _():
        parts, pieces, part_rows, width = w_grad.shape
        for c in range(pieces // 2):
            value = dot(ht[...], dqkv[:, 2 * c * width : 2 * (c + 1) * width]).astype(BF)
            value = value.reshape(parts, part_rows, 2 * width)
            w_grad[:, 2 * c] = value[:, :, :width]
            w_grad[:, 2 * c + 1] = value[:, :, width:]


def back(info, x, q, k, v, raw, datt, lse, spread, dmid, w_query, w_keyval, gains, gg, cosine, sine):

    rows, d = x.shape
    rb = RB
    nb = rows // rb
    whole = lambda a: pl.BlockSpec(a.shape, lambda i, *_: (0,) * a.ndim, pipeline_mode=pl.Buffered(1))
    row = lambda width: pl.BlockSpec((rb, width), lambda i, *_: (nb - 1 - i, 0))
    heads = pl.BlockSpec((QH, rb, HD), lambda i, *_: (0, nb - 1 - i, 0))
    vec = pl.BlockSpec((8, rb), lambda i, *_: (0, nb - 1 - i))
    qw = QH * HD
    nc = COLUMN_STEPS
    grad_shape = (nc, (qw + 2 * HD) // 128, d // nc, 128)
    return pl.pallas_call(
        functools.partial(back_kernel, nb),
        grid_spec=pltpu.PrefetchScalarGridSpec(
            num_scalar_prefetch=1,
            grid=(nb,),
            in_specs=[
                row(d), heads, whole(k), whole(v), row(qw + HD), heads, vec, vec, row(d),
                whole(w_query), whole(w_keyval), whole(gains), whole(gg), row(HD // 2), row(HD // 2),
            ],
            out_specs=[
                row(d),
                pl.BlockSpec((8, d), lambda i, *_: (0, 0)),
                pl.BlockSpec(grad_shape, lambda i, *_: (0,) * 4),
            ],
            scratch_shapes=[
                pltpu.VMEM((nb, HD, rb), BF),
                pltpu.VMEM((nb, rb, HD), F32),
                pltpu.VMEM((nb, rb, HD), F32),
                pltpu.VMEM((HD, QH * rb), F32),
                pltpu.VMEM((d, rows), BF),
                pltpu.VMEM((rows, qw + 2 * HD), BF),
            ],
        ),
        out_shape=[
            jax.ShapeDtypeStruct((rows, d), F32),
            jax.ShapeDtypeStruct((8, d), F32),
            jax.ShapeDtypeStruct(grad_shape, BF),
        ],
        compiler_params=pltpu.CompilerParams(vmem_limit_bytes=56 * 2**20),
        cost_estimate=pl.CostEstimate(flops=20 * 10**9, bytes_accessed=30 * 10**6, transcendentals=4 * 10**6),
        name="back",
    )(info, x, q, k, v, raw, datt, lse, spread, dmid, w_query, w_keyval, gains, gg, cosine, sine)


def tables(rows):
    freqs = np.float32(THETA) ** (-(np.arange(HD // 2, dtype=np.float32) * np.float32(2.0 / HD)))
    angles = np.arange(rows, dtype=np.float32)[:, None] * freqs[None, :].astype(np.float32)
    return np.cos(angles).astype(np.float32), np.sin(angles).astype(np.float32)


def packing(seq_lengths, seq_device, device):
    count = seq_lengths.shape[0]
    ids = jnp.arange(count, dtype=jnp.int32)
    mine = seq_device == device
    first = jnp.min(jnp.where(mine, ids, count))
    bound = jnp.sum(jnp.where(ids == first, seq_lengths, 0), dtype=jnp.int32)
    total = jnp.sum(jnp.where(mine, seq_lengths, 0), dtype=jnp.int32)
    return jnp.stack([bound, total]).astype(jnp.int32)


def local_step(info, tokens, cotangent, w_query, w_keyval, w_project, w_gate, w_upward, w_down, gains):
    cosine, sine = (jnp.asarray(t) for t in tables(tokens.shape[0]))
    q, k, v, raw, att, lse, branch, mid = attend(
        info, tokens, w_query, w_keyval, w_project, gains, cosine, sine
    )
    act, dmid, datt, spread, gg, gu_grad, down_grad, project_grad = feed(
        info, mid, branch, att, cotangent, w_gate, w_upward, w_down, w_project, gains
    )
    din, gg, qkv_grad = back(
        info, tokens, q, k, v, raw, datt, lse, spread, dmid, w_query, w_keyval, gains, gg, cosine, sine
    )
    return act, din, gg, qkv_grad, project_grad, gu_grad, down_grad


def scatter(grad):
    return lax.psum(lax.psum_scatter(grad, "shard", scatter_dimension=0, tiled=True).astype(F32), "rep")


def by_rows(grad):
    return grad.transpose(0, 2, 1, 3).reshape(-1, grad.shape[1] * grad.shape[3])


def by_columns(grad):
    parts, d, cols = grad.shape
    return grad.transpose(0, 2, 1).reshape(parts * cols, d)


def shards(
    tokens, seq_lengths, seq_device, w_query, w_keyval, w_project, w_gate, w_upward, w_down,
    gain_input, gain_query, gain_key, gain_attend, gain_before, gain_after, cotangent,
):
    n_shard, n_rep = lax.axis_size("shard"), lax.axis_size("rep")
    own_kernels = (n_shard, n_rep) == (8, 4)
    me = lax.axis_index("shard")
    info = packing(seq_lengths, seq_device, me * n_rep + lax.axis_index("rep"))
    part = w_query.shape[0]
    d = part * n_shard
    ff = w_gate.shape[1]
    qw = w_query.shape[1]
    head_part = gain_query.shape[0]
    wide = lambda g: jnp.pad(g, (0, 128 - g.shape[0]))
    own_gains = jnp.stack(
        [
            jnp.concatenate([wide(g) for g in (gain_input, gain_attend, gain_before, gain_after)]),
            jnp.concatenate([wide(gain_query), wide(gain_key), jnp.zeros((256,), BF)]),
        ]
        + [jnp.zeros((512,), BF)] * 14
    )
    parts = [own_gains, w_query, w_keyval, w_project, w_gate, w_upward, w_down]
    if own_kernels:
        fulls = gather_all(parts, 1)
    else:
        fulls = [lax.all_gather(p, "shard", axis=0, tiled=True) for p in parts]
    table = fulls[0].reshape(n_shard, 16, 4, 128)
    full = lambda row, lane, size: table[:, row, lane, :size].reshape(n_shard * size)
    rest = jnp.zeros((d - HD,), BF)
    gains = jnp.stack(
        [full(0, lane, part) for lane in range(4)]
        + [jnp.concatenate([full(1, lane, head_part), rest]) for lane in range(2)]
        + [jnp.zeros((d,), BF)] * 2
    ).astype(F32)
    act, din, gg, qkv_grad, project_grad, gu_grad, down_grad = local_step(
        info, tokens, cotangent, *fulls[1:], gains
    )
    if own_kernels:
        pieces = lambda g: g.reshape(n_shard, 8, d // 8, g.shape[2])
        gate, upward, down, project, query, keyval, sums = reduce_all(
            [gu_grad, pieces(down_grad), pieces(project_grad), qkv_grad],
            [(1, 1), (1, 1), (1, 1), (2, 1)],
            [False, True, True, False],
            [[w_gate.shape, w_upward.shape], [w_down.shape[::-1]], [w_project.shape[::-1]], [w_query.shape, w_keyval.shape]],
            gg,
            2,
        )
        down, project = down.T, project.T
    else:
        both = scatter(by_rows(gu_grad))
        gate, upward = both[:, :ff], both[:, ff:]
        both = scatter(by_rows(qkv_grad))
        query, keyval = both[:, :qw], both[:, qw:]
        down, project = scatter(by_columns(down_grad)), scatter(by_columns(project_grad))
        sums = lax.psum(gg, ("shard", "rep"))
    own = lambda row, size: lax.dynamic_slice(sums, (row, me * size), (1, size))[0]
    return (
        act, din, query, keyval, project, gate, upward, down,
        own(0, part), own(4, head_part), own(5, head_part), own(1, part), own(2, part), own(3, part),
    )


def solution(mesh):
    rows, weight, gain = P(("shard", "rep"), None), P("shard", None), P("shard")
    return jax.shard_map(
        shards,
        mesh=mesh,
        in_specs=(rows, P(), P()) + (weight,) * 6 + (gain,) * 6 + (rows,),
        out_specs=(rows, rows) + (weight,) * 6 + (gain,) * 6,
        check_vma=False,
    )
```

```python
import functools
import math

import jax
import jax.numpy as jnp
import numpy as np
from jax import lax
from jax.experimental import pallas as pl
from jax.experimental.pallas import tpu as pltpu
from jax.sharding import PartitionSpec as P

QH = 4
HD = 256
EPS = 1e-06
THETA = 1000000.0
RB = 256
COLUMN_STEPS = 8
F32 = jnp.float32
BF = jnp.bfloat16
EXP_SCALE = HD ** (-0.5) * math.log2(math.e)
MESH = pl.DeviceIdType.MESH
GELU_C = math.sqrt(2.0 / math.pi)


def dot(left, right):
    return lax.dot_general(left, right, (((1,), (0,)), ((), ())), preferred_element_type=F32)


def dot_nt(left, right):
    return lax.dot_general(left, right, (((1,), (1,)), ((), ())), preferred_element_type=F32)


def inv_rms(value):
    return lax.rsqrt(jnp.mean(value * value, axis=-1, keepdims=True) + EPS)


def rotate(value, cosine, sine):
    first, second = value[:, : HD // 2], value[:, HD // 2 :]
    return jnp.concatenate(
        [first * cosine - second * sine, second * cosine + first * sine], axis=-1
    )


def extents(lens_ref, owner_ref):
    device = lax.axis_index("shard") * lax.axis_size("rep") + lax.axis_index("rep")
    count = lens_ref.shape[1]
    ids = lax.broadcasted_iota(jnp.int32, (1, count), 1).astype(F32)
    mine = owner_ref[...] == device
    lens = lens_ref[...].astype(F32)
    first = jnp.min(jnp.where(mine, ids, float(count)), axis=1, keepdims=True)
    bound = jnp.sum(jnp.where(ids == first, lens, 0.0), axis=1, keepdims=True)
    total = jnp.sum(jnp.where(mine, lens, 0.0), axis=1, keepdims=True)
    return bound.astype(jnp.int32), total.astype(jnp.int32)


def seen_mask(bound, query_block, key_block, rb):
    keys = key_block * rb + lax.broadcasted_iota(jnp.int32, (rb, rb), 0)
    rows = query_block * rb + lax.broadcasted_iota(jnp.int32, (rb, rb), 1)
    return (keys <= rows) & (keys >= jnp.where(rows >= bound, bound, 0))


class Places:
    def __init__(self):
        s, r = lax.axis_index("shard"), lax.axis_index("rep")
        z, self.c = lax.div(s, 2), lax.rem(s, 2)
        self.y, self.x = lax.div(r, 2), lax.rem(r, 2)
        self.s, self.r, self.z = s, r, z
        zs = [z, z + 1 - 2 * lax.rem(z, 2), z + 2 - 4 * lax.div(z, 2), 3 - z]
        self.zs = zs
        self.across = r + 1 - 2 * self.x
        self.along = r + 2 - 4 * self.y
        self.shards = [2 * zp + self.c for zp in zs]
        self.core = (s + 1 - 2 * self.c, r)
        self.xdev = (s, self.across)
        self.ydev = (s, self.along)
        self.zdev = [None] + [(self.shards[k], r) for k in (1, 2, 3)]
        self.all = [self.core, self.xdev, self.ydev] + self.zdev[1:]

    def greet(self):
        barrier = pltpu.get_barrier_semaphore()
        for device in self.all:
            pl.semaphore_signal(barrier, inc=1, device_id=device, device_id_type=MESH)
        pl.semaphore_wait(barrier, len(self.all))


class Gather:
    SEMS = 20

    def __init__(self, at, parts, fulls, send, recv):
        self.at, self.parts, self.fulls, self.send, self.recv = at, parts, fulls, send, recv

    def split(self, n):
        rows, cols = self.parts[n].shape
        if cols % 512 == 0:
            width = cols // 4
            return True, width, min(width, (width // 128 + 1) // 2 * 128)
        return False, rows // 4, rows // 8

    def view(self, n, ref, shard, q, half=None):
        by_cols, size, first = self.split(n)
        rows = self.parts[n].shape[0]
        begin, length = q * size, size
        if half == 0:
            length = first
        if half == 1:
            begin, length = begin + first, size - first
        base = 0 if shard is None else shard * rows
        if by_cols:
            return ref.at[pl.ds(pl.multiple_of(base, 16), rows), pl.ds(pl.multiple_of(begin, 128), length)]
        return ref.at[pl.ds(pl.multiple_of(base + begin, 16), length), :]

    def copy(self, n, idx, src, dst, device):
        return pltpu.make_async_remote_copy(
            src_ref=src, dst_ref=dst, send_sem=self.send.at[n, idx], recv_sem=self.recv.at[n, idx],
            device_id=device, device_id_type=MESH,
        )

    def rows_of(self, n, shard):
        rows = self.parts[n].shape[0]
        return self.fulls[n].at[pl.ds(pl.multiple_of(shard * rows, 16), rows), :]

    def out_z(self, n, k):
        at = self.at
        return self.copy(
            n, k - 1, self.view(n, self.parts[n], None, at.r), self.view(n, self.fulls[n], at.s, at.r), at.zdev[k]
        )

    def out_xy(self, n, k, way):
        at = self.at
        piece = self.view(n, self.fulls[n], at.shards[k], at.r)
        return self.copy(n, 3 + 3 * way + k - 1, piece, piece, (at.xdev, at.ydev)[way])

    def halves(self, n):
        _, size, first = self.split(n)
        return (0,) if size == first else (0, 1)

    def out_diag(self, n, k, half):
        at = self.at
        q, device = ((at.across, at.ydev), (at.along, at.xdev))[half]
        piece = self.view(n, self.fulls[n], at.shards[k], q, half)
        return self.copy(n, 9 + 3 * half + k - 1, piece, piece, device)

    def out_core(self, n, k):
        src = self.parts[n] if k == 0 else self.rows_of(n, self.at.shards[k])
        return self.copy(n, 15 + k, src, self.rows_of(n, self.at.shards[k]), self.at.core)

    def own(self, n):
        return pltpu.make_async_copy(self.parts[n], self.rows_of(n, self.at.s), self.send.at[n, 19])

    AHEAD = 2

    def first(self):
        for n, k in self.items()[: self.AHEAD]:
            self.out_z(n, k).start()
        for n in range(len(self.parts)):
            self.out_core(n, 0).start()
            self.own(n).start()

    def items(self):
        return [(n, k) for n in range(len(self.parts)) for k in (1, 2, 3)]

    def second(self, n, k):
        self.out_z(n, k).wait_recv()
        self.out_xy(n, k, 0).start()
        self.out_xy(n, k, 1).start()
        items = self.items()
        later = items.index((n, k)) + self.AHEAD
        if later < len(items):
            self.out_z(*items[later]).start()

    def third(self, n, k):
        self.out_xy(n, k, 0).wait_recv()
        self.out_diag(n, k, 0).start()
        self.out_xy(n, k, 1).wait_recv()
        if 1 in self.halves(n):
            self.out_diag(n, k, 1).start()

    def fourth(self, n, k):
        for half in self.halves(n):
            self.out_diag(n, k, half).wait_recv()
        self.out_core(n, k).start()

    def last(self):
        for n in range(len(self.parts)):
            self.own(n).wait()
            for k in range(4):
                self.out_core(n, k).wait()
            for k in (1, 2, 3):
                self.out_z(n, k).wait_send()
                self.out_xy(n, k, 0).wait_send()
                self.out_xy(n, k, 1).wait_send()
                for half in self.halves(n):
                    self.out_diag(n, k, half).wait_send()

    def middle(self):
        steps = []
        todo = self.items()
        for t in range(len(todo) + 3):
            for lag, stage in ((0, self.second), (1, self.third), (3, self.fourth)):
                if 0 <= t - lag < len(todo):
                    steps.append((t, stage, *todo[t - lag]))
        return steps

    @staticmethod
    def sems(count):
        return [pltpu.SemaphoreType.DMA((count, Gather.SEMS)), pltpu.SemaphoreType.DMA((count, Gather.SEMS))]


def gather_kernel(count, *refs):
    parts, fulls = refs[:count], refs[count : 2 * count]
    send, recv = refs[2 * count :]
    at = Places()
    work = Gather(at, parts, fulls, send, recv)
    at.greet()
    work.first()
    for _, stage, n, k in work.middle():
        stage(n, k)
    work.last()


def gather_all(parts, collective_id):
    count = len(parts)
    size = sum(8 * p.size * 2 for p in parts)
    return pl.pallas_call(
        functools.partial(gather_kernel, count),
        out_shape=[jax.ShapeDtypeStruct((8 * p.shape[0], p.shape[1]), p.dtype) for p in parts],
        in_specs=[pl.BlockSpec(memory_space=pl.ANY)] * count,
        out_specs=[pl.BlockSpec(memory_space=pl.ANY)] * count,
        scratch_shapes=Gather.sems(count),
        compiler_params=pltpu.CompilerParams(collective_id=collective_id, has_side_effects=True),
        cost_estimate=pl.CostEstimate(flops=0, bytes_accessed=size, transcendentals=0),
        name="collect",
    )(*parts)


class Reduce:
    SEMS = 16

    def __init__(self, at, splits, grads, bufs, send, recv):
        self.at, self.splits, self.grads, self.bufs, self.send, self.recv = at, splits, grads, bufs, send, recv

    @staticmethod
    def sizes(a, b, rows, cols):
        piece = (rows, cols)
        shapes = [
            (4, 2, 2, a + b) + piece,
            (4, 2, 2, a + b) + piece,
            (4, 2, a) + piece,
            (4, 2, b) + piece,
            (4, a) + piece,
            (4, b) + piece,
            (3, a + b) + piece,
            (2, 2, a + b) + piece,
        ]
        return [pltpu.VMEM(shape, BF) for shape in shapes]

    def copy(self, n, idx, src, dst, device):
        return pltpu.make_async_remote_copy(
            src_ref=src, dst_ref=dst, send_sem=self.send.at[n, idx], recv_sem=self.recv.at[n, idx],
            device_id=device, device_id_type=MESH,
        )

    def own(self, n):
        return pltpu.make_async_copy(self.grads[n].at[:, self.at.c], self.bufs[n][0], self.send.at[n, 15])

    def out_core(self, n):
        return self.copy(n, 0, self.grads[n].at[:, 1 - self.at.c], self.bufs[n][1], self.at.core)

    def out_1(self, n, way):
        at, (a, b) = self.at, self.splits[n]
        total = self.bufs[n][0]
        if way == 0:
            return self.copy(n, 1, total.at[:, :, 1 - at.x, pl.ds(0, a)], self.bufs[n][2], at.xdev)
        return self.copy(n, 2, total.at[:, 1 - at.y, :, pl.ds(a, b)], self.bufs[n][3], at.ydev)

    def out_2(self, n, way):
        at, (a, b) = self.at, self.splits[n]
        total = self.bufs[n][0]
        if way == 0:
            return self.copy(n, 3, total.at[:, 1 - at.y, at.x, pl.ds(0, a)], self.bufs[n][4], at.ydev)
        return self.copy(n, 4, total.at[:, at.y, 1 - at.x, pl.ds(a, b)], self.bufs[n][5], at.xdev)

    def out_z(self, n, k):
        at = self.at
        return self.copy(n, 4 + k, self.bufs[n][0].at[at.zs[k], at.y, at.x], self.bufs[n][6].at[k - 1], at.zdev[k])

    def out_final(self, n, way):
        at = self.at
        piece = self.bufs[n][7].at[at.y, at.x]
        return self.copy(n, 8 + way, piece, piece, (at.xdev, at.ydev)[way])

    def out_diag(self, n, way):
        at, (a, b) = self.at, self.splits[n]
        result = self.bufs[n][7]
        if way == 0:
            piece = result.at[at.y, 1 - at.x, pl.ds(0, a)]
            return self.copy(n, 10, piece, piece, at.ydev)
        piece = result.at[1 - at.y, at.x, pl.ds(a, b)]
        return self.copy(n, 11, piece, piece, at.xdev)

    def start(self, n):
        self.out_core(n).start()
        self.own(n).start()

    def one(self, n):
        total, other = self.bufs[n][0], self.bufs[n][1]
        a, b = self.splits[n]
        self.own(n).wait()
        self.out_core(n).wait_recv()

        def add(zp, carry):
            for y in range(2):
                for x in range(2):
                    for p in range(a + b):
                        total[zp, y, x, p] = total[zp, y, x, p] + other[zp, y, x, p]
            return carry

        lax.fori_loop(0, 4, add, 0)
        self.out_1(n, 0).start()
        self.out_1(n, 1).start()

    def two(self, n):
        total, at, (a, b) = self.bufs[n][0], self.at, self.splits[n]
        self.out_1(n, 0).wait()
        self.out_1(n, 1).wait()
        from_x, from_y = self.bufs[n][2], self.bufs[n][3]

        def add(zp, carry):
            for m in range(2):
                for p in range(a):
                    total[zp, m, at.x, p] = total[zp, m, at.x, p] + from_x[zp, m, p]
                for p in range(b):
                    total[zp, at.y, m, a + p] = total[zp, at.y, m, a + p] + from_y[zp, m, p]
            return carry

        lax.fori_loop(0, 4, add, 0)
        self.out_2(n, 0).start()
        self.out_2(n, 1).start()

    def three(self, n):
        total, at, (a, b) = self.bufs[n][0], self.at, self.splits[n]
        self.out_2(n, 0).wait()
        self.out_2(n, 1).wait()
        from_y, from_x = self.bufs[n][4], self.bufs[n][5]

        def add(zp, carry):
            for p in range(a):
                total[zp, at.y, at.x, p] = total[zp, at.y, at.x, p] + from_y[zp, p]
            for p in range(b):
                total[zp, at.y, at.x, a + p] = total[zp, at.y, at.x, a + p] + from_x[zp, p]
            return carry

        lax.fori_loop(0, 4, add, 0)
        for k in (1, 2, 3):
            self.out_z(n, k).start()

    def four(self, n):
        total, result, from_z, at = self.bufs[n][0], self.bufs[n][7], self.bufs[n][6], self.at
        for k in (1, 2, 3):
            self.out_z(n, k).wait()
        for p in range(sum(self.splits[n])):
            value = total[at.z, at.y, at.x, p].astype(F32)
            for k in range(3):
                value = value + from_z[k, p].astype(F32)
            result[at.y, at.x, p] = value.astype(BF)
        self.out_final(n, 0).start()
        self.out_final(n, 1).start()

    def five(self, n):
        for way in range(2):
            self.out_final(n, way).wait_recv()
            self.out_diag(n, way).start()

    def six(self, n):
        for way in range(2):
            self.out_diag(n, way).wait()
            self.out_final(n, way).wait_send()
        self.out_core(n).wait_send()

    def stages(self):
        return [self.one, self.two, self.three, self.four, self.five, self.six]

    def waves(self):
        stages, count = self.stages(), len(self.grads)
        return [
            (t, stages[t - n], n)
            for t in range(count + len(stages) - 1)
            for n in range(count)
            if 0 <= t - n < len(stages)
        ]


class Small:
    SEMS = 6

    def __init__(self, at, value, total, inbox, send, recv):
        self.at, self.value, self.total, self.inbox, self.send, self.recv = at, value, total, inbox, send, recv

    def copy(self, idx):
        at = self.at
        slot, device = idx, at.all[idx]
        return pltpu.make_async_remote_copy(
            src_ref=self.total.at[min(idx, 3)], dst_ref=self.inbox.at[slot], send_sem=self.send.at[idx],
            recv_sem=self.recv.at[idx], device_id=device, device_id_type=MESH,
        )

    def start(self):
        self.total[0] = self.value[...]
        self.copy(0).start()

    def next(self, step):
        if step == 3:
            for idx in (3, 4, 5):
                self.copy(idx).wait()
            self.total[4] = self.total[3] + self.inbox[3] + self.inbox[4] + self.inbox[5]
            return
        self.copy(step).wait()
        self.total[step + 1] = self.total[step] + self.inbox[step]
        for idx in (step + 1,) if step < 2 else (3, 4, 5):
            self.copy(idx).start()


def unpack(result, outs, turned):
    _, _, pieces, rows, cols = result.shape
    if turned:
        for y in range(2):
            for x in range(2):
                for p in range(pieces):
                    turned_rows = (2 * y + x) * pieces + p
                    outs[0][turned_rows * rows : (turned_rows + 1) * rows, :] = result[y, x, p].astype(F32)
        return
    begin = 0
    for y in range(2):
        for x in range(2):
            for p in range(pieces):
                out = outs[0] if begin < outs[0].shape[1] else outs[1]
                col = begin if begin < outs[0].shape[1] else begin - outs[0].shape[1]
                out[:, col : col + cols] = result[y, x, p].astype(F32)
                begin += cols


def reduce_kernel(splits, turned, n_outs, *refs):
    count = len(splits)
    grads, small_in = refs[:count], refs[count]
    outs = refs[count + 1 : count + 1 + sum(n_outs)]
    small_out = refs[count + 1 + sum(n_outs)]
    scratch = list(refs[count + 2 + sum(n_outs) :])
    bufs = [[scratch.pop(0) for _ in range(8)] for _ in range(count)]
    total, inbox, send, recv, small_send, small_recv = scratch
    at = Places()
    work = Reduce(at, splits, grads, bufs, send, recv)
    small = Small(at, small_in, total, inbox, small_send, small_recv)
    at.greet()
    small.start()
    for n in range(count):
        work.start(n)
    for _, stage, n in work.waves():
        stage(n)
        if n == 0 and stage in work.stages()[:4]:
            small.next(work.stages().index(stage))
    small_out[...] = total[4]
    for n in range(count):
        unpack(bufs[n][7], outs[sum(n_outs[:n]) : sum(n_outs[: n + 1])], turned[n])


def reduce_all(grads, splits, turned, out_shapes, small, collective_id):
    count = len(grads)
    shaped = [g.reshape(4, 2, 2, 2, g.shape[1] // 4, *g.shape[2:]) for g in grads]
    flat = [s for shapes in out_shapes for s in shapes]
    bufs = [b for g, (a, c) in zip(shaped, splits) for b in Reduce.sizes(a, c, *g.shape[5:])]
    vmem = pl.BlockSpec(memory_space=pltpu.VMEM)
    return pl.pallas_call(
        functools.partial(reduce_kernel, tuple(splits), tuple(turned), tuple(len(s) for s in out_shapes)),
        out_shape=[jax.ShapeDtypeStruct(s, F32) for s in flat] + [jax.ShapeDtypeStruct(small.shape, F32)],
        in_specs=[pl.BlockSpec(memory_space=pl.ANY)] * count + [vmem],
        out_specs=[vmem] * (len(flat) + 1),
        scratch_shapes=bufs
        + [
            pltpu.VMEM((5, *small.shape), F32),
            pltpu.VMEM((6, *small.shape), F32),
            pltpu.SemaphoreType.DMA((count, Reduce.SEMS)),
            pltpu.SemaphoreType.DMA((count, Reduce.SEMS)),
            pltpu.SemaphoreType.DMA((Small.SEMS,)),
            pltpu.SemaphoreType.DMA((Small.SEMS,)),
        ],
        compiler_params=pltpu.CompilerParams(
            collective_id=collective_id, has_side_effects=True, vmem_limit_bytes=50 * 2**20
        ),
        cost_estimate=pl.CostEstimate(flops=0, bytes_accessed=30 * 10**6, transcendentals=0),
        name="total",
    )(*shaped, small)


def attend_kernel(
    nb, count, lens_ref, owner_ref, x_ref, wq_ref, wkv_ref, g_ref, cos_ref, sin_ref, *refs
):
    parts, refs = refs[:count], refs[count:]
    q_out, k_out, v_out, raw_out, att_out, lse_out = refs[:6]
    fulls, refs = refs[6 : 6 + count], refs[6 + count :]
    k_all, vt_all, acc, den = refs[:4]
    i = pl.program_id(0)
    if count:
        at = Places()
        work = Gather(at, parts, fulls, *refs[4:])

        @pl.when(i == 0)
        def _():
            at.greet()
            work.first()

        steps = work.middle()
        slots = max(t for t, _, _, _ in steps) + 1
        places = [(b, p) for b in range(nb) for p in range(3)][2:]
        plan = {}
        for t, *step in steps:
            plan.setdefault(places[t * len(places) // slots], []).append(step)

    def travel(place):
        if count:
            for b in range(nb):
                if (b, place) in plan:

                    @pl.when(i == b)
                    def _(todo=plan[b, place]):
                        for stage, n, k in todo:
                            stage(n, k)

    travel(0)
    bound, _ = extents(lens_ref, owner_ref)
    rb = x_ref.shape[0]
    d = x_ref.shape[1]
    x = x_ref[...].astype(F32)
    h = (x * inv_rms(x) * g_ref[0:1, :]).astype(BF)
    cosine, sine = cos_ref[...], sin_ref[...]
    qgain, kgain = g_ref[4:5, :HD], g_ref[5:6, :HD]
    for head in range(QH):
        raw = dot(h, wq_ref[:, head * HD : (head + 1) * HD])
        raw_out[:, head * HD : (head + 1) * HD] = raw.astype(BF)
        q_out[head] = rotate(raw * inv_rms(raw) * qgain, cosine, sine).astype(BF)
    raw = dot(h, wkv_ref[:, :HD])
    raw_out[:, QH * HD :] = raw.astype(BF)
    keys = rotate(raw * inv_rms(raw) * kgain, cosine, sine).astype(BF)
    values = dot(h, wkv_ref[:, HD:]).astype(BF)
    k_out[...] = keys
    v_out[...] = values
    k_all[i] = keys
    vt_all[i] = values.T
    travel(1)
    acc[...] = jnp.zeros_like(acc)
    den[...] = jnp.zeros_like(den)

    def step(j, carry):
        mask = seen_mask(bound, i, j, rb)
        for head in range(QH):
            cols = slice(head * rb, (head + 1) * rb)
            scores = dot_nt(k_all[j], q_out[head])
            probs = jnp.where(mask, jnp.exp2(scores * EXP_SCALE), 0.0)
            den[:, cols] += jnp.sum(probs.reshape(rb // 8, 8, rb), axis=0)
            acc[:, cols] += dot(vt_all[j], probs.astype(BF))
        return carry

    lax.fori_loop(0, i + 1, step, 0)
    travel(2)
    lse = []
    for head in range(QH):
        cols = slice(head * rb, (head + 1) * rb)
        total = jnp.sum(den[:, cols], axis=0, keepdims=True)
        lse.append(jnp.log2(total))
        att_out[:, head * HD : (head + 1) * HD] = (acc[:, cols] * (1.0 / total)).T.astype(BF)
    lse_out[...] = jnp.concatenate(lse + lse, axis=0)
    if count:

        @pl.when(i == nb - 1)
        def _():
            work.last()


def attend(packing, x, w_query, w_keyval, gains, cosine, sine, parts, collective_id):
    rows, d = x.shape
    rb = RB
    nb = rows // rb
    whole = lambda a: pl.BlockSpec(a.shape, lambda i: (0,) * a.ndim, pipeline_mode=pl.Buffered(1))
    row = lambda width: pl.BlockSpec((rb, width), lambda i: (i, 0))
    far = [pl.BlockSpec(memory_space=pl.ANY)] * len(parts)
    qw = QH * HD
    params = dict(vmem_limit_bytes=56 * 2**20)
    if parts:
        params.update(collective_id=collective_id, has_side_effects=True)
    return pl.pallas_call(
        functools.partial(attend_kernel, nb, len(parts)),
        grid=(nb,),
        in_specs=[whole(packing[0]), whole(packing[1]), row(d), whole(w_query), whole(w_keyval), whole(gains)]
        + [row(HD // 2), row(HD // 2)]
        + far,
        out_specs=[
            pl.BlockSpec((QH, rb, HD), lambda i: (0, i, 0)),
            row(HD), row(HD), row(qw + HD), row(qw),
            pl.BlockSpec((8, rb), lambda i: (0, i)),
        ]
        + far,
        scratch_shapes=[
            pltpu.VMEM((nb, rb, HD), BF),
            pltpu.VMEM((nb, HD, rb), BF),
            pltpu.VMEM((HD, QH * rb), F32),
            pltpu.VMEM((8, QH * rb), F32),
        ]
        + (Gather.sems(len(parts)) if parts else []),
        out_shape=[
            jax.ShapeDtypeStruct((QH, rows, HD), BF),
            jax.ShapeDtypeStruct((rows, HD), BF),
            jax.ShapeDtypeStruct((rows, HD), BF),
            jax.ShapeDtypeStruct((rows, qw + HD), BF),
            jax.ShapeDtypeStruct((rows, qw), BF),
            jax.ShapeDtypeStruct((8, rows), F32),
        ]
        + [jax.ShapeDtypeStruct((8 * p.shape[0], p.shape[1]), p.dtype) for p in parts],
        compiler_params=pltpu.CompilerParams(**params),
        cost_estimate=pl.CostEstimate(flops=14 * 10**9, bytes_accessed=30 * 10**6, transcendentals=4 * 10**6),
        name="attend",
    )(*packing, x, w_query, w_keyval, gains, cosine, sine, *parts)


def norm_back(grad, unit, r, gain):
    scaled = grad * gain
    return r * (scaled - unit * jnp.mean(scaled * unit, axis=-1, keepdims=True))


def column_sum(value):
    return jnp.sum(value, axis=0, keepdims=True)


def feed_kernel(
    nb, n_cols, lens_ref, owner_ref, x_ref, att_ref, cot_ref, attc_ref, wg_ref, wu_ref, wd_ref, wp_ref, g_ref,
    act_out, dmid_out, datt_out, spread_out, gg_out, gate_grad, up_grad, down_grad, project_grad,
    hid, dgu, h2t, dft, dbt, act_s, mul_s,
):
    i = pl.program_id(0)
    rb, d = x_ref.shape
    ff = wd_ref.shape[0]
    fc = ff // 4

    @pl.when(i < nb)
    def _():
        start = pl.multiple_of(i * rb, rb)
        rows = pl.ds(start, rb)
        branch = dot(att_ref[...], wp_ref[...])
        r_br = inv_rms(branch)
        unit_br = branch * r_br
        mid = x_ref[...].astype(F32) + unit_br * g_ref[1:2, :]
        r_mid = inv_rms(mid)
        unit_mid = mid * r_mid
        h2 = (unit_mid * g_ref[2:3, :]).astype(BF)
        h2t[:, rows] = h2.T
        for c in range(4):
            cols = slice(c * fc, (c + 1) * fc)
            gate = dot(h2, wg_ref[:, cols])
            up = dot(h2, wu_ref[:, cols])
            sq = gate * gate
            th = jnp.tanh(GELU_C * gate * (1.0 + 0.044715 * sq))
            half = 0.5 + 0.5 * th
            act = gate * half
            slope = half + 0.5 * gate * (1.0 - th * th) * (GELU_C * (1.0 + (3 * 0.044715) * sq))
            hid[rows, cols] = (act * up).astype(BF)
            act_s[:, cols] = act
            mul_s[:, cols] = up * slope
        ffn = dot(hid[rows, :], wd_ref[...])
        r_ffn = inv_rms(ffn)
        unit_ffn = ffn * r_ffn
        after = g_ref[3:4, :]
        act_out[...] = (mid + unit_ffn * after).astype(BF)
        row_ids = start + lax.broadcasted_iota(jnp.int32, (rb, 1), 0)
        _, total = extents(lens_ref, owner_ref)
        ups = jnp.where(row_ids < total, cot_ref[...].astype(F32), 0.0)
        d_ffn = norm_back(ups, unit_ffn, r_ffn, after).astype(BF)
        dft[:, rows] = d_ffn.T
        for c in range(4):
            cols = slice(c * fc, (c + 1) * fc)
            d_hid = dot_nt(d_ffn, wd_ref[cols, :])
            dgu[rows, cols] = (d_hid * mul_s[:, cols]).astype(BF)
            dgu[rows, ff + c * fc : ff + (c + 1) * fc] = (d_hid * act_s[:, cols]).astype(BF)
        d_h2 = dot_nt(dgu[rows, :ff], wg_ref[...]) + dot_nt(dgu[rows, ff:], wu_ref[...])
        d_mid = ups + norm_back(d_h2, unit_mid, r_mid, g_ref[2:3, :])
        dmid_out[...] = d_mid
        d_br = norm_back(d_mid, unit_br, r_br, g_ref[1:2, :]).astype(BF)
        dbt[:, rows] = d_br.T
        d_att = dot_nt(d_br, wp_ref[...])
        datt_low = d_att.astype(BF)
        prod = datt_low.astype(F32) * att_ref[...].astype(F32)
        spread = []
        for head in range(QH):
            cols = slice(head * HD, (head + 1) * HD)
            datt_out[head] = datt_low[:, cols]
            spread.append(jnp.sum(prod[:, cols], axis=1, keepdims=True))
        wide = jnp.concatenate(spread + [jnp.zeros((rb, 128 - QH), F32)], axis=1)
        spread_out[...] = wide.T[:8, :]
        sums = jnp.concatenate(
            [
                jnp.zeros((1, d), F32),
                column_sum(d_mid * unit_br),
                column_sum(d_h2 * unit_mid),
                column_sum(ups * unit_ffn),
                jnp.zeros((4, d), F32),
            ],
            axis=0,
        )

        @pl.when(i == 0)
        def _():
            gg_out[...] = jnp.zeros_like(gg_out)

        gg_out[...] += sums

    @pl.when(i >= nb)
    def _():
        s = i - nb
        width = ff // n_cols
        for grad, base in ((gate_grad, 0), (up_grad, ff)):
            cols = pl.ds(pl.multiple_of(base + s * width, width), width)
            grad[:, 0] = dot(h2t[...], dgu[:, cols]).astype(BF).reshape(n_cols, d // n_cols, width)
        cols = pl.ds(pl.multiple_of(s * width, width), width)
        down_grad[0] = dot(dft[...], hid[:, cols]).astype(BF)
        project_grad[0] = dot(dbt[...], attc_ref[...]).astype(BF)


def feed(packing, x, att, cot, w_gate, w_upward, w_down, w_project, gains):
    rows, d = x.shape
    ff = w_down.shape[0]
    qw = att.shape[1]
    rb = RB
    nb = rows // rb
    whole = lambda a: pl.BlockSpec(a.shape, lambda i, *_: (0,) * a.ndim, pipeline_mode=pl.Buffered(1))
    blk = lambda i: jnp.minimum(i, nb - 1)
    col = lambda i: jnp.maximum(i - nb, 0)
    row = lambda width: pl.BlockSpec((rb, width), lambda i, *_: (blk(i), 0))
    nc = COLUMN_STEPS

    return pl.pallas_call(
        functools.partial(feed_kernel, nb, nc),
        grid_spec=pltpu.PrefetchScalarGridSpec(
            num_scalar_prefetch=0,
            grid=(nb + nc,),
            in_specs=[
                whole(packing[0]), whole(packing[1]), row(d), row(qw), row(d),
                pl.BlockSpec((rows, qw // nc), lambda i, *_: (0, col(i))),
                whole(w_gate), whole(w_upward), whole(w_down), whole(w_project), whole(gains),
            ],
            out_specs=[
                row(d), row(d),
                pl.BlockSpec((QH, rb, HD), lambda i, *_: (0, blk(i), 0)),
                pl.BlockSpec((8, rb), lambda i, *_: (0, blk(i))),
                pl.BlockSpec((8, d), lambda i, *_: (0, 0)),
                pl.BlockSpec((nc, 1, d // nc, ff // nc), lambda i, *_: (0, col(i), 0, 0)),
                pl.BlockSpec((nc, 1, d // nc, ff // nc), lambda i, *_: (0, col(i), 0, 0)),
                pl.BlockSpec((1, d, ff // nc), lambda i, *_: (col(i), 0, 0)),
                pl.BlockSpec((1, d, qw // nc), lambda i, *_: (col(i), 0, 0)),
            ],
            scratch_shapes=[
                pltpu.VMEM((rows, ff), BF),
                pltpu.VMEM((rows, 2 * ff), BF),
                pltpu.VMEM((d, rows), BF),
                pltpu.VMEM((d, rows), BF),
                pltpu.VMEM((d, rows), BF),
                pltpu.VMEM((rb, ff), F32),
                pltpu.VMEM((rb, ff), F32),
            ],
        ),
        out_shape=[
            jax.ShapeDtypeStruct((rows, d), BF),
            jax.ShapeDtypeStruct((rows, d), F32),
            jax.ShapeDtypeStruct((QH, rows, HD), BF),
            jax.ShapeDtypeStruct((8, rows), F32),
            jax.ShapeDtypeStruct((8, d), F32),
            jax.ShapeDtypeStruct((nc, nc, d // nc, ff // nc), BF),
            jax.ShapeDtypeStruct((nc, nc, d // nc, ff // nc), BF),
            jax.ShapeDtypeStruct((nc, d, ff // nc), BF),
            jax.ShapeDtypeStruct((nc, d, qw // nc), BF),
        ],
        compiler_params=pltpu.CompilerParams(vmem_limit_bytes=60 * 2**20),
        cost_estimate=pl.CostEstimate(flops=42 * 10**9, bytes_accessed=50 * 10**6, transcendentals=4 * 10**6),
        name="feed",
    )(*packing, x, att, cot, att, w_gate, w_upward, w_down, w_project, gains)


TRAVEL = (
    (0, 1, 1, 0),
    (0, 2, 1, 1),
    (1, 0, 2, 0),
    (1, 0, 1, 2),
    (1, 3, 3, 0),
    (1, 3, 2, 1),
    (2, 0, 1, 3),
    (2, 2, 3, 1),
    (2, 2, 2, 2),
    (2, 3, 4, 0),
    (3, 0, 2, 3),
    (3, 1, 5, 0),
    (3, 2, 4, 1),
    (3, 2, 3, 2),
    (3, 3, 6, 0),
    (3, 3, 3, 3),
    (3, 3, 5, 1),
    (4, 2, 4, 2),
    (4, 3, 6, 1),
    (4, 3, 4, 3),
    (5, 0, 5, 2),
    (5, 3, 5, 3),
    (5, 4, 6, 2),
    (5, 4, 6, 3),
)


def back_kernel(
    nb, splits, turned, lens_ref, owner_ref, x_ref, q_ref, k_ref, v_ref, raw_ref, datt_ref, lse_ref, spread_ref, dmid_ref,
    wq_ref, wkv_ref, g_ref, gg_ref, cos_ref, sin_ref, *refs
):
    count = len(splits)
    grads, (din_out, gg_out, w_grad) = refs[:count], refs[count : count + 3]
    sums, refs = refs[count + 3 : 2 * count + 3], refs[2 * count + 3 :]
    kt_all, dk, dv, dqt, ht, dqkv = refs[:6]
    step_id = pl.program_id(0)
    if count:
        refs = list(refs[6:])
        bufs = [[refs.pop(0) for _ in range(8)] for _ in range(count)]
        at = Places()
        work = Reduce(at, splits, grads, bufs, *refs)

        @pl.when(step_id == 0)
        def _():
            at.greet()
            for n in range(count):
                work.start(n)

    def travel(place):
        for block, where, stage, n in TRAVEL if count else ():
            if where == place:

                @pl.when(step_id == block)
                def _(stage=stage, n=n):
                    work.stages()[stage - 1](n)

    i = nb - 1 - step_id
    bound, _ = extents(lens_ref, owner_ref)
    rb, d = x_ref.shape
    qw = QH * HD

    @pl.when(step_id == 0)
    def _():
        for j in range(nb):
            kt_all[j] = k_ref[j * rb : (j + 1) * rb, :].T
        dk[...] = jnp.zeros_like(dk)
        dv[...] = jnp.zeros_like(dv)
        gg_out[...] = gg_ref[...]

    travel(0)
    dqt[...] = jnp.zeros_like(dqt)

    def step(j, carry):
        rows = pl.ds(pl.multiple_of(j * rb, rb), rb)
        mask = seen_mask(bound, i, j, rb)
        keys = k_ref[rows, :]
        values = v_ref[rows, :]
        d_keys = dk[j]
        d_values = dv[j]
        for head in range(QH):
            cols = slice(head * rb, (head + 1) * rb)
            queries = q_ref[head]
            d_out = datt_ref[head]
            scores = dot_nt(keys, queries)
            probs = jnp.where(mask, jnp.exp2(scores * EXP_SCALE - lse_ref[head : head + 1, :]), 0.0)
            d_probs = dot_nt(values, d_out)
            d_scores = (probs * (d_probs - spread_ref[head : head + 1, :])).astype(BF)
            dqt[:, cols] += dot(kt_all[j], d_scores)
            d_keys = d_keys + dot(d_scores, queries)
            d_values = d_values + dot(probs.astype(BF), d_out)
        dk[j] = d_keys
        dv[j] = d_values
        return carry

    for third in range(3):
        lax.fori_loop(lax.div((i + 1) * third, 3), lax.div((i + 1) * (third + 1), 3), step, 0)
        travel(third + 1)
    rows = pl.ds(pl.multiple_of(i * rb, rb), rb)
    cosine, sine = cos_ref[...], sin_ref[...]
    scale = HD ** (-0.5)
    qgain, kgain = g_ref[4:5, :HD], g_ref[5:6, :HD]
    q_sum = jnp.zeros((1, HD), F32)
    for head in range(QH):
        grad = rotate(dqt[:, head * rb : (head + 1) * rb].T * scale, cosine, -sine)
        raw = raw_ref[:, head * HD : (head + 1) * HD].astype(F32)
        r = inv_rms(raw)
        unit = raw * r
        q_sum = q_sum + column_sum(grad * unit)
        dqkv[rows, head * HD : (head + 1) * HD] = norm_back(grad, unit, r, qgain).astype(BF)
    grad = rotate(dk[i] * scale, cosine, -sine)
    raw = raw_ref[:, qw : qw + HD].astype(F32)
    r = inv_rms(raw)
    unit = raw * r
    k_sum = column_sum(grad * unit)
    dqkv[rows, qw : qw + HD] = norm_back(grad, unit, r, kgain).astype(BF)
    dqkv[rows, qw + HD :] = dv[i].astype(BF)
    d_h = dot_nt(dqkv[rows, :qw], wq_ref[...]) + dot_nt(dqkv[rows, qw:], wkv_ref[...])
    x = x_ref[...].astype(F32)
    r = inv_rms(x)
    unit = x * r
    gain = g_ref[0:1, :]
    ht[:, rows] = (unit * gain).astype(BF).T
    din_out[...] = dmid_ref[...] + norm_back(d_h, unit, r, gain)
    rest = jnp.zeros((1, d - HD), F32)
    gg_out[...] += jnp.concatenate(
        [
            column_sum(d_h * unit),
            jnp.zeros((3, d), F32),
            jnp.concatenate([q_sum, rest], axis=1),
            jnp.concatenate([k_sum, rest], axis=1),
            jnp.zeros((2, d), F32),
        ],
        axis=0,
    )

    @pl.when(step_id == nb - 1)
    def _():
        parts, pieces, part_rows, width = w_grad.shape
        for c in range(pieces // 2):
            value = dot(ht[...], dqkv[:, 2 * c * width : 2 * (c + 1) * width]).astype(BF)
            value = value.reshape(parts, part_rows, 2 * width)
            w_grad[:, 2 * c] = value[:, :, :width]
            w_grad[:, 2 * c + 1] = value[:, :, width:]
        for n in range(count):
            if (nb - 1, 4, 6, n) in TRAVEL:
                work.six(n)
            unpack(bufs[n][7], sums[n : n + 1], turned[n])


def back(packing, x, q, k, v, raw, datt, lse, spread, dmid, w_query, w_keyval, gains, gg, cosine, sine, grads, splits, turned, out_shapes, collective_id):
    rows, d = x.shape
    rb = RB
    nb = rows // rb
    whole = lambda a: pl.BlockSpec(a.shape, lambda i, *_: (0,) * a.ndim, pipeline_mode=pl.Buffered(1))
    row = lambda width: pl.BlockSpec((rb, width), lambda i, *_: (nb - 1 - i, 0))
    heads = pl.BlockSpec((QH, rb, HD), lambda i, *_: (0, nb - 1 - i, 0))
    vec = pl.BlockSpec((8, rb), lambda i, *_: (0, nb - 1 - i))
    qw = QH * HD
    nc = COLUMN_STEPS
    grad_shape = (nc, (qw + 2 * HD) // 128, d // nc, 128)
    shaped = [g.reshape(4, 2, 2, 2, g.shape[1] // 4, *g.shape[2:]) for g in grads]
    far = [pl.BlockSpec(memory_space=pl.ANY)] * len(grads)
    scratch = [
        pltpu.VMEM((nb, HD, rb), BF),
        pltpu.VMEM((nb, rb, HD), F32),
        pltpu.VMEM((nb, rb, HD), F32),
        pltpu.VMEM((HD, QH * rb), F32),
        pltpu.VMEM((d, rows), BF),
        pltpu.VMEM((rows, qw + 2 * HD), BF),
    ]
    params = dict(vmem_limit_bytes=58 * 2**20)
    if grads:
        scratch += [b for g, (a, c) in zip(shaped, splits) for b in Reduce.sizes(a, c, *g.shape[5:])]
        scratch += [pltpu.SemaphoreType.DMA((len(grads), Reduce.SEMS))] * 2
        params.update(collective_id=collective_id, has_side_effects=True)
    return pl.pallas_call(
        functools.partial(back_kernel, nb, tuple(splits), tuple(turned)),
        grid=(nb,),
        in_specs=[
            whole(packing[0]), whole(packing[1]), row(d), heads, whole(k), whole(v), row(qw + HD), heads, vec, vec, row(d),
            whole(w_query), whole(w_keyval), whole(gains), whole(gg), row(HD // 2), row(HD // 2),
        ]
        + far,
        out_specs=[
            row(d),
            pl.BlockSpec((8, d), lambda i: (0, 0)),
            pl.BlockSpec(grad_shape, lambda i: (0,) * 4),
        ]
        + [pl.BlockSpec(s, lambda i: (0, 0)) for s in out_shapes],
        scratch_shapes=scratch,
        out_shape=[
            jax.ShapeDtypeStruct((rows, d), F32),
            jax.ShapeDtypeStruct((8, d), F32),
            jax.ShapeDtypeStruct(grad_shape, BF),
        ]
        + [jax.ShapeDtypeStruct(s, F32) for s in out_shapes],
        compiler_params=pltpu.CompilerParams(**params),
        cost_estimate=pl.CostEstimate(flops=20 * 10**9, bytes_accessed=30 * 10**6, transcendentals=4 * 10**6),
        name="back",
    )(*packing, x, q, k, v, raw, datt, lse, spread, dmid, w_query, w_keyval, gains, gg, cosine, sine, *shaped)


def tables(rows):
    freqs = np.float32(THETA) ** (-(np.arange(HD // 2, dtype=np.float32) * np.float32(2.0 / HD)))
    angles = np.arange(rows, dtype=np.float32)[:, None] * freqs[None, :].astype(np.float32)
    return np.cos(angles).astype(np.float32), np.sin(angles).astype(np.float32)


def scatter(grad):
    return lax.psum(lax.psum_scatter(grad, "shard", scatter_dimension=0, tiled=True).astype(F32), "rep")


def by_rows(grad):
    return grad.transpose(0, 2, 1, 3).reshape(-1, grad.shape[1] * grad.shape[3])


def by_columns(grad):
    parts, d, cols = grad.shape
    return grad.transpose(0, 2, 1).reshape(parts * cols, d)


def shards(
    tokens, seq_lengths, seq_device, w_query, w_keyval, w_project, w_gate, w_upward, w_down,
    gain_input, gain_query, gain_key, gain_attend, gain_before, gain_after, cotangent,
):
    n_shard = lax.axis_size("shard")
    own_kernels = (n_shard, lax.axis_size("rep")) == (8, 4)
    me = lax.axis_index("shard")
    packing = (seq_lengths[None, :], seq_device[None, :])
    part = w_query.shape[0]
    d = part * n_shard
    ff = w_gate.shape[1]
    qw = w_query.shape[1]
    head_part = gain_query.shape[0]
    wide = lambda g: jnp.pad(g, (0, 128 - g.shape[0]))
    own_gains = jnp.stack(
        [
            jnp.concatenate([wide(g) for g in (gain_input, gain_attend, gain_before, gain_after)]),
            jnp.concatenate([wide(gain_query), wide(gain_key), jnp.zeros((256,), BF)]),
        ]
        + [jnp.zeros((512,), BF)] * 14
    )
    early = [w_query, w_keyval, own_gains]
    late = [w_project, w_gate, w_upward, w_down]
    if own_kernels:
        fulls = gather_all(early, 1)
    else:
        fulls = [lax.all_gather(p, "shard", axis=0, tiled=True) for p in early]
    *fulls, table = fulls
    table = table.reshape(n_shard, 16, 4, 128)
    full = lambda row, lane, size: table[:, row, lane, :size].reshape(n_shard * size)
    rest = jnp.zeros((d - HD,), BF)
    gains = jnp.stack(
        [full(0, lane, part) for lane in range(4)]
        + [jnp.concatenate([full(1, lane, head_part), rest]) for lane in range(2)]
        + [jnp.zeros((d,), BF)] * 2
    ).astype(F32)
    cosine, sine = (jnp.asarray(t) for t in tables(tokens.shape[0]))
    query_full, keyval_full = fulls
    q, k, v, raw, att, lse, *rest = attend(
        packing, tokens, query_full, keyval_full, gains, cosine, sine, late if own_kernels else [], 3
    )
    if not own_kernels:
        rest = [lax.all_gather(p, "shard", axis=0, tiled=True) for p in late]
    act, dmid, datt, spread, gg, gate_grad, up_grad, down_grad, project_grad = feed(
        packing, tokens, att, cotangent, *rest[1:], rest[0], gains
    )
    pieces = lambda g: g.reshape(COLUMN_STEPS, 8, d // 8, g.shape[2])
    late_sums = ([], [], [], [])
    if own_kernels:
        late_sums = (
            [gate_grad, up_grad, pieces(down_grad), pieces(project_grad)],
            [(1, 1)] * 4,
            [False, False, True, True],
            [w_gate.shape, w_upward.shape, w_down.shape[::-1], w_project.shape[::-1]],
        )
    din, gg, qkv_grad, *rest = back(
        packing, tokens, q, k, v, raw, datt, lse, spread, dmid, query_full, keyval_full, gains, gg, cosine, sine,
        *late_sums, 4,
    )
    if own_kernels:
        gate, upward, down, project = rest
        query, keyval, sums = reduce_all(
            [qkv_grad], [(2, 1)], [False], [[w_query.shape, w_keyval.shape]], gg, 2
        )
        down, project = down.T, project.T
    else:
        gate, upward = scatter(by_rows(gate_grad)), scatter(by_rows(up_grad))
        both = scatter(by_rows(qkv_grad))
        query, keyval = both[:, :qw], both[:, qw:]
        down, project = scatter(by_columns(down_grad)), scatter(by_columns(project_grad))
        sums = lax.psum(gg, ("shard", "rep"))
    own = lambda row, size: lax.dynamic_slice(sums, (row, me * size), (1, size))[0]
    return (
        act, din, query, keyval, project, gate, upward, down,
        own(0, part), own(4, head_part), own(5, head_part), own(1, part), own(2, part), own(3, part),
    )


def solution(mesh):
    rows, weight, gain = P(("shard", "rep"), None), P("shard", None), P("shard")
    return jax.shard_map(
        shards,
        mesh=mesh,
        in_specs=(rows, P(), P()) + (weight,) * 6 + (gain,) * 6 + (rows,),
        out_specs=(rows, rows) + (weight,) * 6 + (gain,) * 6,
        check_vma=False,
    )
```

```python
import functools
import math

import jax
import jax.numpy as jnp
import numpy as np
from jax import lax
from jax.experimental import pallas as pl
from jax.experimental.pallas import tpu as pltpu
from jax.sharding import PartitionSpec as P

QH = 4
HD = 256
EPS = 1e-06
THETA = 1000000.0
RB = 256
FEED_ROWS = 512
COLUMN_STEPS = 8
F32 = jnp.float32
BF = jnp.bfloat16
EXP_SCALE = HD ** (-0.5) * math.log2(math.e)
MESH = pl.DeviceIdType.MESH
GELU_C = math.sqrt(2.0 / math.pi)


def dot(left, right):
    return lax.dot_general(left, right, (((1,), (0,)), ((), ())), preferred_element_type=F32)


def dot_nt(left, right):
    return lax.dot_general(left, right, (((1,), (1,)), ((), ())), preferred_element_type=F32)


def inv_rms(value):
    return lax.rsqrt(jnp.mean(value * value, axis=-1, keepdims=True) + EPS)


def rotate(value, cosine, sine):
    first, second = value[:, : HD // 2], value[:, HD // 2 :]
    return jnp.concatenate(
        [first * cosine - second * sine, second * cosine + first * sine], axis=-1
    )


def extents(lens_ref, owner_ref):
    device = lax.axis_index("shard") * lax.axis_size("rep") + lax.axis_index("rep")
    count = lens_ref.shape[1]
    ids = lax.broadcasted_iota(jnp.int32, (1, count), 1).astype(F32)
    mine = owner_ref[...] == device
    lens = lens_ref[...].astype(F32)
    first = jnp.min(jnp.where(mine, ids, float(count)), axis=1, keepdims=True)
    bound = jnp.sum(jnp.where(ids == first, lens, 0.0), axis=1, keepdims=True)
    total = jnp.sum(jnp.where(mine, lens, 0.0), axis=1, keepdims=True)
    return bound.astype(jnp.int32), total.astype(jnp.int32)


def seen_mask(bound, query_block, key_block, rb):
    keys = key_block * rb + lax.broadcasted_iota(jnp.int32, (rb, rb), 0)
    rows = query_block * rb + lax.broadcasted_iota(jnp.int32, (rb, rb), 1)
    return (keys <= rows) & (keys >= jnp.where(rows >= bound, bound, 0))


class Places:
    def __init__(self):
        s, r = lax.axis_index("shard"), lax.axis_index("rep")
        z, self.c = lax.div(s, 2), lax.rem(s, 2)
        self.y, self.x = lax.div(r, 2), lax.rem(r, 2)
        self.s, self.r, self.z = s, r, z
        zs = [z, z + 1 - 2 * lax.rem(z, 2), z + 2 - 4 * lax.div(z, 2), 3 - z]
        self.zs = zs
        self.across = r + 1 - 2 * self.x
        self.along = r + 2 - 4 * self.y
        self.shards = [2 * zp + self.c for zp in zs]
        self.core = (s + 1 - 2 * self.c, r)
        self.xdev = (s, self.across)
        self.ydev = (s, self.along)
        self.zdev = [None] + [(self.shards[k], r) for k in (1, 2, 3)]
        self.all = [self.core, self.xdev, self.ydev] + self.zdev[1:]

    def greet(self):
        barrier = pltpu.get_barrier_semaphore()
        for device in self.all:
            pl.semaphore_signal(barrier, inc=1, device_id=device, device_id_type=MESH)
        pl.semaphore_wait(barrier, len(self.all))


class Gather:
    SEMS = 20

    def __init__(self, at, parts, fulls, groups, send, recv):
        self.at, self.parts, self.fulls, self.groups, self.send, self.recv = at, parts, fulls, groups, send, recv

    def split(self, n):
        rows, cols = self.parts[n].shape
        if cols % 512 == 0:
            width = cols // 4
            return True, width, min(width, (width // 128 + 1) // 2 * 128)
        return False, rows // 4, rows // 8

    def view(self, n, ref, shard, q, half=None):
        by_cols, size, first = self.split(n)
        rows = self.parts[n].shape[0]
        begin, length = q * size, size
        if half == 0:
            length = first
        if half == 1:
            begin, length = begin + first, size - first
        base = 0 if shard is None else shard * rows
        if by_cols:
            return ref.at[pl.ds(pl.multiple_of(base, 16), rows), pl.ds(pl.multiple_of(begin, 128), length)]
        return ref.at[pl.ds(pl.multiple_of(base + begin, 16), length), :]

    def copy(self, n, idx, src, dst, device):
        return pltpu.make_async_remote_copy(
            src_ref=src, dst_ref=dst, send_sem=self.send.at[n, idx], recv_sem=self.recv.at[n, idx],
            device_id=device, device_id_type=MESH,
        )

    def rows_of(self, n, shard):
        rows = self.parts[n].shape[0]
        return self.fulls[n].at[pl.ds(pl.multiple_of(shard * rows, 16), rows), :]

    def out_z(self, n, k):
        at = self.at
        return self.copy(
            n, k - 1, self.view(n, self.parts[n], None, at.r), self.view(n, self.fulls[n], at.s, at.r), at.zdev[k]
        )

    def out_xy(self, n, k, way):
        at = self.at
        piece = self.view(n, self.fulls[n], at.shards[k], at.r)
        return self.copy(n, 3 + 3 * way + k - 1, piece, piece, (at.xdev, at.ydev)[way])

    def halves(self, n):
        _, size, first = self.split(n)
        return (0,) if size == first else (0, 1)

    def out_diag(self, n, k, half):
        at = self.at
        q, device = ((at.across, at.ydev), (at.along, at.xdev))[half]
        piece = self.view(n, self.fulls[n], at.shards[k], q, half)
        return self.copy(n, 9 + 3 * half + k - 1, piece, piece, device)

    def out_core(self, n, k):
        src = self.parts[n] if k == 0 else self.rows_of(n, self.at.shards[k])
        return self.copy(n, 15 + k, src, self.rows_of(n, self.at.shards[k]), self.at.core)

    def own(self, n):
        return pltpu.make_async_copy(self.parts[n], self.rows_of(n, self.at.s), self.send.at[n, 19])

    AHEAD = 2

    def items(self):
        return [(group, k) for group in self.groups for k in (1, 2, 3)]

    def first(self):
        for group, k in self.items()[: self.AHEAD]:
            for n in group:
                self.out_z(n, k).start()
        for group in self.groups:
            for n in group:
                self.out_core(n, 0).start()
                self.own(n).start()

    def second(self, slot):
        items = self.items()
        group, k = items[slot]
        for n in group:
            self.out_z(n, k).wait_recv()
            self.out_xy(n, k, 0).start()
            self.out_xy(n, k, 1).start()
        if slot + self.AHEAD < len(items):
            group, k = items[slot + self.AHEAD]
            for n in group:
                self.out_z(n, k).start()

    def third(self, slot):
        group, k = self.items()[slot]
        for n in group:
            self.out_xy(n, k, 0).wait_recv()
            self.out_diag(n, k, 0).start()
            self.out_xy(n, k, 1).wait_recv()
            if 1 in self.halves(n):
                self.out_diag(n, k, 1).start()

    def fourth(self, slot):
        group, k = self.items()[slot]
        for n in group:
            for half in self.halves(n):
                self.out_diag(n, k, half).wait_recv()
            self.out_core(n, k).start()

    def slots(self):
        return len(self.items()) + 3

    def advance(self, slot):
        for lag, stage in ((0, self.second), (1, self.third), (3, self.fourth)):
            if 0 <= slot - lag < len(self.items()):
                stage(slot - lag)

    def ready(self, n):
        self.own(n).wait()
        for k in range(4):
            self.out_core(n, k).wait_recv()

    def sent(self, n):
        for k in range(4):
            self.out_core(n, k).wait_send()
        for k in (1, 2, 3):
            self.out_z(n, k).wait_send()
            self.out_xy(n, k, 0).wait_send()
            self.out_xy(n, k, 1).wait_send()
            for half in self.halves(n):
                self.out_diag(n, k, half).wait_send()

    @staticmethod
    def sems(count):
        return [pltpu.SemaphoreType.DMA((count, Gather.SEMS)), pltpu.SemaphoreType.DMA((count, Gather.SEMS))]


class Reduce:
    SEMS = 16

    def __init__(self, at, splits, grads, bufs, send, recv):
        self.at, self.splits, self.grads, self.bufs, self.send, self.recv = at, splits, grads, bufs, send, recv

    @staticmethod
    def sizes(a, b, rows, cols):
        piece = (rows, cols)
        shapes = [
            (4, 2, 2, a + b) + piece,
            (4, 2, 2, a + b) + piece,
            (4, 2, a) + piece,
            (4, 2, b) + piece,
            (4, a) + piece,
            (4, b) + piece,
            (3, a + b) + piece,
            (2, 2, a + b) + piece,
        ]
        return [pltpu.VMEM(shape, BF) for shape in shapes]

    def copy(self, n, idx, src, dst, device):
        return pltpu.make_async_remote_copy(
            src_ref=src, dst_ref=dst, send_sem=self.send.at[n, idx], recv_sem=self.recv.at[n, idx],
            device_id=device, device_id_type=MESH,
        )

    def own(self, n):
        return pltpu.make_async_copy(self.grads[n].at[:, self.at.c], self.bufs[n][0], self.send.at[n, 15])

    def out_core(self, n):
        return self.copy(n, 0, self.grads[n].at[:, 1 - self.at.c], self.bufs[n][1], self.at.core)

    def out_1(self, n, way):
        at, (a, b) = self.at, self.splits[n]
        total = self.bufs[n][0]
        if way == 0:
            return self.copy(n, 1, total.at[:, :, 1 - at.x, pl.ds(0, a)], self.bufs[n][2], at.xdev)
        return self.copy(n, 2, total.at[:, 1 - at.y, :, pl.ds(a, b)], self.bufs[n][3], at.ydev)

    def out_2(self, n, way):
        at, (a, b) = self.at, self.splits[n]
        total = self.bufs[n][0]
        if way == 0:
            return self.copy(n, 3, total.at[:, 1 - at.y, at.x, pl.ds(0, a)], self.bufs[n][4], at.ydev)
        return self.copy(n, 4, total.at[:, at.y, 1 - at.x, pl.ds(a, b)], self.bufs[n][5], at.xdev)

    def out_z(self, n, k):
        at = self.at
        return self.copy(n, 4 + k, self.bufs[n][0].at[at.zs[k], at.y, at.x], self.bufs[n][6].at[k - 1], at.zdev[k])

    def out_final(self, n, way):
        at = self.at
        piece = self.bufs[n][7].at[at.y, at.x]
        return self.copy(n, 8 + way, piece, piece, (at.xdev, at.ydev)[way])

    def out_diag(self, n, way):
        at, (a, b) = self.at, self.splits[n]
        result = self.bufs[n][7]
        if way == 0:
            piece = result.at[at.y, 1 - at.x, pl.ds(0, a)]
            return self.copy(n, 10, piece, piece, at.ydev)
        piece = result.at[1 - at.y, at.x, pl.ds(a, b)]
        return self.copy(n, 11, piece, piece, at.xdev)

    def start(self, n):
        self.out_core(n).start()
        self.own(n).start()

    def one(self, n):
        total, other = self.bufs[n][0], self.bufs[n][1]
        a, b = self.splits[n]
        self.own(n).wait()
        self.out_core(n).wait_recv()

        def add(zp, carry):
            for y in range(2):
                for x in range(2):
                    for p in range(a + b):
                        total[zp, y, x, p] = total[zp, y, x, p] + other[zp, y, x, p]
            return carry

        lax.fori_loop(0, 4, add, 0)
        self.out_1(n, 0).start()
        self.out_1(n, 1).start()

    def two(self, n):
        total, at, (a, b) = self.bufs[n][0], self.at, self.splits[n]
        self.out_1(n, 0).wait()
        self.out_1(n, 1).wait()
        from_x, from_y = self.bufs[n][2], self.bufs[n][3]

        def add(zp, carry):
            for m in range(2):
                for p in range(a):
                    total[zp, m, at.x, p] = total[zp, m, at.x, p] + from_x[zp, m, p]
                for p in range(b):
                    total[zp, at.y, m, a + p] = total[zp, at.y, m, a + p] + from_y[zp, m, p]
            return carry

        lax.fori_loop(0, 4, add, 0)
        self.out_2(n, 0).start()
        self.out_2(n, 1).start()

    def three(self, n):
        total, at, (a, b) = self.bufs[n][0], self.at, self.splits[n]
        self.out_2(n, 0).wait()
        self.out_2(n, 1).wait()
        from_y, from_x = self.bufs[n][4], self.bufs[n][5]

        def add(zp, carry):
            for p in range(a):
                total[zp, at.y, at.x, p] = total[zp, at.y, at.x, p] + from_y[zp, p]
            for p in range(b):
                total[zp, at.y, at.x, a + p] = total[zp, at.y, at.x, a + p] + from_x[zp, p]
            return carry

        lax.fori_loop(0, 4, add, 0)
        for k in (1, 2, 3):
            self.out_z(n, k).start()

    def four(self, n):
        total, result, from_z, at = self.bufs[n][0], self.bufs[n][7], self.bufs[n][6], self.at
        for k in (1, 2, 3):
            self.out_z(n, k).wait()
        for p in range(sum(self.splits[n])):
            value = total[at.z, at.y, at.x, p].astype(F32)
            for k in range(3):
                value = value + from_z[k, p].astype(F32)
            result[at.y, at.x, p] = value.astype(BF)
        self.out_final(n, 0).start()
        self.out_final(n, 1).start()

    def five(self, n):
        for way in range(2):
            self.out_final(n, way).wait_recv()
            self.out_diag(n, way).start()

    def six(self, n):
        for way in range(2):
            self.out_diag(n, way).wait()
            self.out_final(n, way).wait_send()
        self.out_core(n).wait_send()

    def stages(self):
        return [self.one, self.two, self.three, self.four, self.five, self.six]

    def waves(self):
        stages, count = self.stages(), len(self.grads)
        return [
            (t, stages[t - n], n)
            for t in range(count + len(stages) - 1)
            for n in range(count)
            if 0 <= t - n < len(stages)
        ]


class Small:
    SEMS = 6

    def __init__(self, at, value, total, inbox, send, recv):
        self.at, self.value, self.total, self.inbox, self.send, self.recv = at, value, total, inbox, send, recv

    def copy(self, idx):
        at = self.at
        slot, device = idx, at.all[idx]
        return pltpu.make_async_remote_copy(
            src_ref=self.total.at[min(idx, 3)], dst_ref=self.inbox.at[slot], send_sem=self.send.at[idx],
            recv_sem=self.recv.at[idx], device_id=device, device_id_type=MESH,
        )

    def start(self):
        self.total[0] = self.value[...]
        self.copy(0).start()

    def next(self, step):
        if step == 3:
            for idx in (3, 4, 5):
                self.copy(idx).wait()
            self.total[4] = self.total[3] + self.inbox[3] + self.inbox[4] + self.inbox[5]
            return
        self.copy(step).wait()
        self.total[step + 1] = self.total[step] + self.inbox[step]
        for idx in (step + 1,) if step < 2 else (3, 4, 5):
            self.copy(idx).start()


def unpack(result, outs, turned):
    _, _, pieces, rows, cols = result.shape
    if turned:
        for y in range(2):
            for x in range(2):
                for p in range(pieces):
                    turned_rows = (2 * y + x) * pieces + p
                    outs[0][turned_rows * rows : (turned_rows + 1) * rows, :] = result[y, x, p].astype(F32)
        return
    begin = 0
    for y in range(2):
        for x in range(2):
            for p in range(pieces):
                out = outs[0] if begin < outs[0].shape[1] else outs[1]
                col = begin if begin < outs[0].shape[1] else begin - outs[0].shape[1]
                out[:, col : col + cols] = result[y, x, p].astype(F32)
                begin += cols


EARLY = 3
GROUPS = ((0, 1, 2), (4,), (5,), (6, 3))
BEFORE = 6
PLACES = ((0, 2), (1, 1), (1, 2), (2, 1), (2, 2), (3, 1), (3, 2), (4, 1), (4, 2))


def spread_gains(table_ref, g_ref, n_shard):
    d, size = g_ref.shape[1], g_ref.shape[1] // n_shard
    g_ref[...] = jnp.zeros_like(g_ref)
    step = table_ref.shape[0] // n_shard
    for row, slot, width, to in [(0, lane, size, lane) for lane in range(4)] + [
        (1, lane, HD // n_shard, 4 + lane) for lane in range(2)
    ]:
        lanes = lax.broadcasted_iota(jnp.int32, (128, d), 0)
        cols = lax.broadcasted_iota(jnp.int32, (128, d), 1)
        total = jnp.zeros((16, d), F32)
        for shard in range(n_shard):
            here = ((cols == lanes + shard * width) & (lanes < width)).astype(F32).astype(BF)
            total = total + dot(table_ref[shard * step : shard * step + 16, slot * 128 : (slot + 1) * 128], here)
        g_ref[to : to + 1, :] = total[row : row + 1, :]


def attend_kernel(
    nb, n_shard, count, lens_ref, owner_ref, x_ref, cos_ref, sin_ref, *refs
):
    i = pl.program_id(0)
    if count:
        parts, refs = refs[:count], refs[count:]
        q_out, k_out, v_out, raw_out, att_out, lse_out, g_ref = refs[:7]
        fulls, refs = refs[7 : 7 + count - 1], refs[7 + count - 1 :]
        k_all, vt_all, acc, den, wq_ref, wkv_ref, table_ref, send, recv, keep = refs
        at = Places()
        work = Gather(at, parts, (wq_ref, wkv_ref, table_ref) + fulls[2:], GROUPS, send, recv)
        kept = [
            pltpu.make_async_copy(wq_ref, fulls[0], keep.at[0]),
            pltpu.make_async_copy(wkv_ref, fulls[1], keep.at[1]),
        ]

        @pl.when(i == 0)
        def _():
            at.greet()
            work.first()
            for slot in range(BEFORE):
                work.advance(slot)
            for n in range(EARLY):
                work.ready(n)
            for copy in kept:
                copy.start()
            spread_gains(table_ref, g_ref, n_shard)

    else:
        wq_ref, wkv_ref, table_ref, q_out, k_out, v_out, raw_out, att_out, lse_out, g_ref, k_all, vt_all, acc, den = refs

        @pl.when(i == 0)
        def _():
            spread_gains(table_ref, g_ref, n_shard)

    def travel(place):
        for slot, (block, where) in enumerate(PLACES if count else ()):
            if where == place:

                @pl.when(i == block)
                def _(slot=slot):
                    work.advance(BEFORE + slot)

    bound, _ = extents(lens_ref, owner_ref)
    rb = x_ref.shape[0]
    d = x_ref.shape[1]
    x = x_ref[...].astype(F32)
    h = (x * inv_rms(x) * g_ref[0:1, :]).astype(BF)
    cosine, sine = cos_ref[...], sin_ref[...]
    qgain, kgain = g_ref[4:5, :HD], g_ref[5:6, :HD]
    for head in range(QH):
        raw = dot(h, wq_ref[:, head * HD : (head + 1) * HD])
        raw_out[:, head * HD : (head + 1) * HD] = raw.astype(BF)
        q_out[head] = rotate(raw * inv_rms(raw) * qgain, cosine, sine).astype(BF)
    raw = dot(h, wkv_ref[:, :HD])
    raw_out[:, QH * HD :] = raw.astype(BF)
    keys = rotate(raw * inv_rms(raw) * kgain, cosine, sine).astype(BF)
    values = dot(h, wkv_ref[:, HD:]).astype(BF)
    k_out[...] = keys
    v_out[...] = values
    k_all[i] = keys
    vt_all[i] = values.T
    travel(1)
    acc[...] = jnp.zeros_like(acc)
    den[...] = jnp.zeros_like(den)

    def step(j, carry):
        mask = seen_mask(bound, i, j, rb)
        for head in range(QH):
            cols = slice(head * rb, (head + 1) * rb)
            scores = dot_nt(k_all[j], q_out[head])
            probs = jnp.where(mask, jnp.exp2(scores * EXP_SCALE), 0.0)
            den[:, cols] += jnp.sum(probs.reshape(rb // 8, 8, rb), axis=0)
            acc[:, cols] += dot(vt_all[j], probs.astype(BF))
        return carry

    lax.fori_loop(0, i + 1, step, 0)
    travel(2)
    lse = []
    for head in range(QH):
        cols = slice(head * rb, (head + 1) * rb)
        total = jnp.sum(den[:, cols], axis=0, keepdims=True)
        lse.append(jnp.log2(total))
        att_out[:, head * HD : (head + 1) * HD] = (acc[:, cols] * (1.0 / total)).T.astype(BF)
    lse_out[...] = jnp.concatenate(lse + lse, axis=0)
    if count:

        @pl.when(i == nb - 1)
        def _():
            for copy in kept:
                copy.wait()
            for n in range(EARLY, count):
                work.ready(n)
            for n in range(count):
                work.sent(n)


def attend(packing, x, cosine, sine, n_shard, parts, gathered, collective_id):
    rows, d = x.shape
    rb = RB
    nb = rows // rb
    whole = lambda a: pl.BlockSpec(a.shape, lambda i: (0,) * a.ndim, pipeline_mode=pl.Buffered(1))
    row = lambda width: pl.BlockSpec((rb, width), lambda i: (i, 0))
    far = pl.BlockSpec(memory_space=pl.ANY)
    qw = QH * HD
    params = dict(vmem_limit_bytes=56 * 2**20)
    scratch = [
        pltpu.VMEM((nb, rb, HD), BF),
        pltpu.VMEM((nb, HD, rb), BF),
        pltpu.VMEM((HD, QH * rb), F32),
        pltpu.VMEM((8, QH * rb), F32),
    ]
    fulls = [jax.ShapeDtypeStruct((8 * p.shape[0], p.shape[1]), p.dtype) for p in parts]
    if parts:
        params.update(collective_id=collective_id, has_side_effects=True)
        scratch += [pltpu.VMEM(f.shape, f.dtype) for f in fulls[:EARLY]] + Gather.sems(len(parts))
        scratch += [pltpu.SemaphoreType.DMA((2,))]
    kept = fulls[:2] + fulls[EARLY:]
    return pl.pallas_call(
        functools.partial(attend_kernel, nb, n_shard, len(parts)),
        grid=(nb,),
        in_specs=[whole(packing[0]), whole(packing[1]), row(d), row(HD // 2), row(HD // 2)]
        + [far] * len(parts)
        + [whole(w) for w in gathered],
        out_specs=[
            pl.BlockSpec((QH, rb, HD), lambda i: (0, i, 0)),
            row(HD), row(HD), row(qw + HD), row(qw),
            pl.BlockSpec((8, rb), lambda i: (0, i)),
            pl.BlockSpec((8, d), lambda i: (0, 0)),
        ]
        + [far] * len(kept),
        scratch_shapes=scratch,
        out_shape=[
            jax.ShapeDtypeStruct((QH, rows, HD), BF),
            jax.ShapeDtypeStruct((rows, HD), BF),
            jax.ShapeDtypeStruct((rows, HD), BF),
            jax.ShapeDtypeStruct((rows, qw + HD), BF),
            jax.ShapeDtypeStruct((rows, qw), BF),
            jax.ShapeDtypeStruct((8, rows), F32),
            jax.ShapeDtypeStruct((8, d), F32),
        ]
        + kept,
        compiler_params=pltpu.CompilerParams(**params),
        cost_estimate=pl.CostEstimate(flops=14 * 10**9, bytes_accessed=30 * 10**6, transcendentals=4 * 10**6),
        name="attend",
    )(*packing, x, cosine, sine, *parts, *gathered)


def norm_back(grad, unit, r, gain):
    scaled = grad * gain
    return r * (scaled - unit * jnp.mean(scaled * unit, axis=-1, keepdims=True))


def column_sum(value):
    return jnp.sum(value, axis=0, keepdims=True)


def feed_kernel(
    nb, n_cols, lens_ref, owner_ref, x_ref, att_ref, cot_ref, attc_ref, wg_ref, wu_ref, wd_ref, wp_ref, g_ref,
    act_out, dmid_out, datt_out, spread_out, gg_out, gate_grad, up_grad, down_grad, project_grad,
    hid, dgu, h2t, dft, dbt, act_s, mul_s,
):
    i = pl.program_id(0)
    rb, d = x_ref.shape
    ff = wd_ref.shape[0]
    fc = ff // 4

    @pl.when(i < nb)
    def _():
        start = pl.multiple_of(i * rb, rb)
        rows = pl.ds(start, rb)
        branch = dot(att_ref[...], wp_ref[...])
        r_br = inv_rms(branch)
        unit_br = branch * r_br
        mid = x_ref[...].astype(F32) + unit_br * g_ref[1:2, :]
        r_mid = inv_rms(mid)
        unit_mid = mid * r_mid
        h2 = (unit_mid * g_ref[2:3, :]).astype(BF)
        h2t[:, rows] = h2.T
        for c in range(4):
            cols = slice(c * fc, (c + 1) * fc)
            gate = dot(h2, wg_ref[:, cols])
            up = dot(h2, wu_ref[:, cols])
            sq = gate * gate
            th = jnp.tanh(GELU_C * gate * (1.0 + 0.044715 * sq))
            half = 0.5 + 0.5 * th
            act = gate * half
            slope = half + 0.5 * gate * (1.0 - th * th) * (GELU_C * (1.0 + (3 * 0.044715) * sq))
            hid[rows, cols] = (act * up).astype(BF)
            act_s[:, cols] = act.astype(BF)
            mul_s[:, cols] = (up * slope).astype(BF)
        ffn = dot(hid[rows, :], wd_ref[...])
        r_ffn = inv_rms(ffn)
        unit_ffn = ffn * r_ffn
        after = g_ref[3:4, :]
        act_out[...] = (mid + unit_ffn * after).astype(BF)
        row_ids = start + lax.broadcasted_iota(jnp.int32, (rb, 1), 0)
        _, total = extents(lens_ref, owner_ref)
        ups = jnp.where(row_ids < total, cot_ref[...].astype(F32), 0.0)
        d_ffn = norm_back(ups, unit_ffn, r_ffn, after).astype(BF)
        dft[:, rows] = d_ffn.T
        for c in range(4):
            cols = slice(c * fc, (c + 1) * fc)
            d_hid = dot_nt(d_ffn, wd_ref[cols, :])
            dgu[rows, cols] = (d_hid * mul_s[:, cols]).astype(BF)
            dgu[rows, ff + c * fc : ff + (c + 1) * fc] = (d_hid * act_s[:, cols]).astype(BF)
        d_h2 = dot_nt(dgu[rows, :ff], wg_ref[...]) + dot_nt(dgu[rows, ff:], wu_ref[...])
        d_mid = ups + norm_back(d_h2, unit_mid, r_mid, g_ref[2:3, :])
        dmid_out[...] = d_mid
        d_br = norm_back(d_mid, unit_br, r_br, g_ref[1:2, :]).astype(BF)
        dbt[:, rows] = d_br.T
        d_att = dot_nt(d_br, wp_ref[...])
        datt_low = d_att.astype(BF)
        prod = datt_low.astype(F32) * att_ref[...].astype(F32)
        spread = []
        for head in range(QH):
            cols = slice(head * HD, (head + 1) * HD)
            datt_out[head] = datt_low[:, cols]
            spread.append(jnp.sum(prod[:, cols], axis=1, keepdims=True))
        wide = jnp.concatenate(spread + [jnp.zeros((rb, 128 - QH), F32)], axis=1)
        spread_out[...] = wide.T[:8, :]
        sums = jnp.concatenate(
            [
                jnp.zeros((1, d), F32),
                column_sum(d_mid * unit_br),
                column_sum(d_h2 * unit_mid),
                column_sum(ups * unit_ffn),
                jnp.zeros((4, d), F32),
            ],
            axis=0,
        )

        @pl.when(i == 0)
        def _():
            gg_out[...] = jnp.zeros_like(gg_out)

        gg_out[...] += sums

    @pl.when(i >= nb)
    def _():
        s = i - nb
        width = ff // n_cols
        for grad, base in ((gate_grad, 0), (up_grad, ff)):
            cols = pl.ds(pl.multiple_of(base + s * width, width), width)
            grad[:, 0] = dot(h2t[...], dgu[:, cols]).astype(BF).reshape(n_cols, d // n_cols, width)
        cols = pl.ds(pl.multiple_of(s * width, width), width)
        down_grad[0] = dot(dft[...], hid[:, cols]).astype(BF)
        project_grad[0] = dot(dbt[...], attc_ref[...]).astype(BF)


def feed(packing, x, att, cot, w_gate, w_upward, w_down, w_project, gains):
    rows, d = x.shape
    ff = w_down.shape[0]
    qw = att.shape[1]
    rb = FEED_ROWS
    nb = rows // rb
    whole = lambda a: pl.BlockSpec(a.shape, lambda i, *_: (0,) * a.ndim, pipeline_mode=pl.Buffered(1))
    blk = lambda i: jnp.minimum(i, nb - 1)
    col = lambda i: jnp.maximum(i - nb, 0)
    row = lambda width: pl.BlockSpec((rb, width), lambda i, *_: (blk(i), 0))
    nc = COLUMN_STEPS

    return pl.pallas_call(
        functools.partial(feed_kernel, nb, nc),
        grid_spec=pltpu.PrefetchScalarGridSpec(
            num_scalar_prefetch=0,
            grid=(nb + nc,),
            in_specs=[
                whole(packing[0]), whole(packing[1]), row(d), row(qw), row(d),
                pl.BlockSpec((rows, qw // nc), lambda i, *_: (0, col(i))),
                whole(w_gate), whole(w_upward), whole(w_down), whole(w_project), whole(gains),
            ],
            out_specs=[
                row(d), row(d),
                pl.BlockSpec((QH, rb, HD), lambda i, *_: (0, blk(i), 0)),
                pl.BlockSpec((8, rb), lambda i, *_: (0, blk(i))),
                pl.BlockSpec((8, d), lambda i, *_: (0, 0)),
                pl.BlockSpec((nc, 1, d // nc, ff // nc), lambda i, *_: (0, col(i), 0, 0)),
                pl.BlockSpec((nc, 1, d // nc, ff // nc), lambda i, *_: (0, col(i), 0, 0)),
                pl.BlockSpec((1, d, ff // nc), lambda i, *_: (col(i), 0, 0)),
                pl.BlockSpec((1, d, qw // nc), lambda i, *_: (col(i), 0, 0)),
            ],
            scratch_shapes=[
                pltpu.VMEM((rows, ff), BF),
                pltpu.VMEM((rows, 2 * ff), BF),
                pltpu.VMEM((d, rows), BF),
                pltpu.VMEM((d, rows), BF),
                pltpu.VMEM((d, rows), BF),
                pltpu.VMEM((rb, ff), BF),
                pltpu.VMEM((rb, ff), BF),
            ],
        ),
        out_shape=[
            jax.ShapeDtypeStruct((rows, d), BF),
            jax.ShapeDtypeStruct((rows, d), F32),
            jax.ShapeDtypeStruct((QH, rows, HD), BF),
            jax.ShapeDtypeStruct((8, rows), F32),
            jax.ShapeDtypeStruct((8, d), F32),
            jax.ShapeDtypeStruct((nc, nc, d // nc, ff // nc), BF),
            jax.ShapeDtypeStruct((nc, nc, d // nc, ff // nc), BF),
            jax.ShapeDtypeStruct((nc, d, ff // nc), BF),
            jax.ShapeDtypeStruct((nc, d, qw // nc), BF),
        ],
        compiler_params=pltpu.CompilerParams(vmem_limit_bytes=60 * 2**20),
        cost_estimate=pl.CostEstimate(flops=42 * 10**9, bytes_accessed=50 * 10**6, transcendentals=4 * 10**6),
        name="feed",
    )(*packing, x, att, cot, att, w_gate, w_upward, w_down, w_project, gains)


TRAVEL = ((0, 1, 1, 0), (0, 2, 1, 1), (1, 0, 2, 0), (1, 0, 1, 2), (1, 3, 3, 0), (1, 3, 2, 1), (2, 0, 1, 3), (2, 2, 3, 1), (2, 2, 2, 2), (2, 3, 4, 0), (3, 0, 2, 3), (3, 1, 5, 0), (3, 2, 4, 1), (3, 2, 3, 2), (3, 3, 6, 0), (3, 3, 3, 3), (3, 3, 5, 1), (4, 2, 4, 2), (4, 3, 6, 1), (4, 3, 4, 3), (5, 0, 5, 2), (5, 3, 5, 3), (6, 0, 6, 2), (6, 0, 6, 3), (8, 0, 1, 4))
LAST = ((2, 4), (3, 4), (4, 4), (5, 4), (6, 4))
SPLITS = ((1, 1), (1, 1), (1, 1), (1, 1), (2, 1))
TURNED = (False, False, True, True, False)


def back_kernel(
    nb, count, lens_ref, owner_ref, x_ref, q_ref, k_ref, v_ref, raw_ref, datt_ref, lse_ref, spread_ref, dmid_ref,
    wq_ref, wkv_ref, g_ref, gg_ref, cos_ref, sin_ref, *refs
):
    grads, (din_out, gg_out), refs = refs[:count], refs[count : count + 2], list(refs[count + 2 :])
    sums = [refs.pop(0) for _ in range(count + 3)] if count else []
    w_grad = refs.pop(0)
    kt_all, dk, dv, dqt, ht, dqkv = refs[:6]
    step_id = pl.program_id(0)
    if count:
        refs = refs[6:]
        bufs = [[refs.pop(0) for _ in range(8)] for _ in range(count + 1)]
        total, inbox, send, recv, small_send, small_recv = refs
        at = Places()
        work = Reduce(at, SPLITS, list(grads) + [w_grad], bufs, send, recv)
        small = Small(at, gg_out, total, inbox, small_send, small_recv)

        @pl.when(step_id == 0)
        def _():
            at.greet()
            for n in range(count):
                work.start(n)

    def advance(stage, n):
        work.stages()[stage - 1](n)
        if n == count and stage <= 4:
            small.next(stage - 1)

    def travel(place):
        for block, where, stage, n in TRAVEL if count else ():
            if where == place:

                @pl.when(step_id == block)
                def _(stage=stage, n=n):
                    advance(stage, n)

    travel(0)

    @pl.when(step_id < nb)
    def _():
        attend_back(
            nb, travel, lens_ref, owner_ref, x_ref, q_ref, k_ref, v_ref, raw_ref, datt_ref, lse_ref, spread_ref,
            wq_ref, wkv_ref, g_ref, gg_ref, cos_ref, sin_ref, gg_out, w_grad, kt_all, dk, dv, dqt, ht, dqkv,
        )

    if count:

        @pl.when(step_id == nb - 1)
        def _():
            work.start(count)
            small.start()

    @pl.when(step_id >= nb)
    def _():
        rb = x_ref.shape[0]
        qw = wq_ref.shape[1]
        rows = pl.ds(pl.multiple_of((step_id - nb) * rb, rb), rb)
        d_h = dot_nt(dqkv[rows, :qw], wq_ref[...]) + dot_nt(dqkv[rows, qw:], wkv_ref[...])
        x = x_ref[...].astype(F32)
        r = inv_rms(x)
        din_out[...] = dmid_ref[...] + norm_back(d_h, x * r, r, g_ref[0:1, :])

    if count:

        @pl.when(step_id == 2 * nb - 1)
        def _():
            for stage, n in LAST:
                advance(stage, n)
            for n in range(count + 1):
                unpack(bufs[n][7], sums[n : n + 1] if n < count else sums[n : n + 2], TURNED[n])
            sums[-1][...] = total[4]


def attend_back(
    nb, travel, lens_ref, owner_ref, x_ref, q_ref, k_ref, v_ref, raw_ref, datt_ref, lse_ref, spread_ref,
    wq_ref, wkv_ref, g_ref, gg_ref, cos_ref, sin_ref, gg_out, w_grad, kt_all, dk, dv, dqt, ht, dqkv,
):
    step_id = pl.program_id(0)
    i = nb - 1 - step_id
    bound, _ = extents(lens_ref, owner_ref)
    rb, d = x_ref.shape
    qw = QH * HD

    @pl.when(step_id == 0)
    def _():
        for j in range(nb):
            kt_all[j] = k_ref[j * rb : (j + 1) * rb, :].T
        dk[...] = jnp.zeros_like(dk)
        dv[...] = jnp.zeros_like(dv)
        gg_out[...] = gg_ref[...]

    dqt[...] = jnp.zeros_like(dqt)

    def step(j, carry):
        rows = pl.ds(pl.multiple_of(j * rb, rb), rb)
        mask = seen_mask(bound, i, j, rb)
        keys = k_ref[rows, :]
        values = v_ref[rows, :]
        d_keys = dk[j]
        d_values = dv[j]
        for head in range(QH):
            cols = slice(head * rb, (head + 1) * rb)
            queries = q_ref[head]
            d_out = datt_ref[head]
            scores = dot_nt(keys, queries)
            probs = jnp.where(mask, jnp.exp2(scores * EXP_SCALE - lse_ref[head : head + 1, :]), 0.0)
            d_probs = dot_nt(values, d_out)
            d_scores = (probs * (d_probs - spread_ref[head : head + 1, :])).astype(BF)
            dqt[:, cols] += dot(kt_all[j], d_scores)
            d_keys = d_keys + dot(d_scores, queries)
            d_values = d_values + dot(probs.astype(BF), d_out)
        dk[j] = d_keys
        dv[j] = d_values
        return carry

    for third in range(3):
        lax.fori_loop(lax.div((i + 1) * third, 3), lax.div((i + 1) * (third + 1), 3), step, 0)
        travel(third + 1)
    rows = pl.ds(pl.multiple_of(i * rb, rb), rb)
    cosine, sine = cos_ref[...], sin_ref[...]
    scale = HD ** (-0.5)
    qgain, kgain = g_ref[4:5, :HD], g_ref[5:6, :HD]
    q_sum = jnp.zeros((1, HD), F32)
    for head in range(QH):
        grad = rotate(dqt[:, head * rb : (head + 1) * rb].T * scale, cosine, -sine)
        raw = raw_ref[:, head * HD : (head + 1) * HD].astype(F32)
        r = inv_rms(raw)
        unit = raw * r
        q_sum = q_sum + column_sum(grad * unit)
        dqkv[rows, head * HD : (head + 1) * HD] = norm_back(grad, unit, r, qgain).astype(BF)
    grad = rotate(dk[i] * scale, cosine, -sine)
    raw = raw_ref[:, qw : qw + HD].astype(F32)
    r = inv_rms(raw)
    unit = raw * r
    k_sum = column_sum(grad * unit)
    dqkv[rows, qw : qw + HD] = norm_back(grad, unit, r, kgain).astype(BF)
    dqkv[rows, qw + HD :] = dv[i].astype(BF)
    x = x_ref[...].astype(F32)
    ht[:, rows] = (x * inv_rms(x) * g_ref[0:1, :]).astype(BF).T
    rest = jnp.zeros((1, d - HD), F32)
    gg_out[...] += jnp.concatenate(
        [
            jnp.zeros((4, d), F32),
            jnp.concatenate([q_sum, rest], axis=1),
            jnp.concatenate([k_sum, rest], axis=1),
            jnp.zeros((2, d), F32),
        ],
        axis=0,
    )

    @pl.when(step_id == nb - 1)
    def _():
        _, _, _, _, pieces, part_rows, width = w_grad.shape
        gained = jnp.zeros((d, 1), F32)
        for c in range(2 * pieces):
            wide = slice(2 * c * width, 2 * (c + 1) * width)
            value = dot(ht[...], dqkv[:, wide])
            base = 2 * c * width - qw
            weight = wq_ref[:, wide] if base < 0 else wkv_ref[:, base : base + 2 * width]
            gained = gained + jnp.sum(value * weight.astype(F32), axis=1, keepdims=True)
            value = value.astype(BF)
            for side in range(2):
                quarter, p = divmod(2 * c + side, pieces)
                half = value[:, side * width : (side + 1) * width]
                w_grad[:, :, quarter // 2, quarter % 2, p] = half.reshape(4, 2, part_rows, width)
        across = jnp.broadcast_to(gained, (d, 128)).T
        gg_out[0:1, :] = across[0:1, :] / g_ref[0:1, :]


def back(packing, x, q, k, v, raw, datt, lse, spread, dmid, w_query, w_keyval, gains, gg, cosine, sine, grads, out_shapes, collective_id):
    rows, d = x.shape
    rb = RB
    nb = rows // rb
    qw = QH * HD
    nc = COLUMN_STEPS
    count = len(grads)
    first = lambda i: jnp.maximum(nb - 1 - i, 0)
    second = lambda i: jnp.maximum(i - nb, 0)
    whole = lambda a: pl.BlockSpec(a.shape, lambda i: (0,) * a.ndim, pipeline_mode=pl.Buffered(1))
    row = lambda width: pl.BlockSpec((rb, width), lambda i: (first(i), 0))
    late = pl.BlockSpec((rb, d), lambda i: (second(i), 0))
    both = pl.BlockSpec((rb, d), lambda i: (jnp.where(i < nb, nb - 1 - i, i - nb), 0))
    heads = pl.BlockSpec((QH, rb, HD), lambda i: (0, first(i), 0))
    vec = pl.BlockSpec((8, rb), lambda i: (0, first(i)))
    fixed = lambda shape: pl.BlockSpec(shape, lambda i: (0,) * len(shape))
    grad_shape = (4, 2, 2, 2, (qw + 2 * HD) // 512, d // nc, 128)
    shaped = [g.reshape(4, 2, 2, 2, g.shape[1] // 4, *g.shape[2:]) for g in grads]
    scratch = [
        pltpu.VMEM((nb, HD, rb), BF),
        pltpu.VMEM((nb, rb, HD), F32),
        pltpu.VMEM((nb, rb, HD), F32),
        pltpu.VMEM((HD, QH * rb), F32),
        pltpu.VMEM((d, rows), BF),
        pltpu.VMEM((rows, qw + 2 * HD), BF),
    ]
    params = dict(vmem_limit_bytes=58 * 2**20)
    outs = [((rows, d), F32, late), ((8, d), F32, fixed((8, d)))]
    if grads:
        outs += [(s, F32, fixed(s)) for s in (*out_shapes, (8, d))]
        sizes = [g.shape[4:] for g in shaped] + [grad_shape[4:]]
        scratch = [pltpu.VMEM(grad_shape, BF)] + scratch
        scratch += [b for split, shape in zip(SPLITS, sizes) for b in Reduce.sizes(*split, *shape[1:])]
        scratch += [pltpu.VMEM((5, 8, d), F32), pltpu.VMEM((6, 8, d), F32)]
        scratch += [pltpu.SemaphoreType.DMA((count + 1, Reduce.SEMS))] * 2 + [pltpu.SemaphoreType.DMA((Small.SEMS,))] * 2
        params.update(collective_id=collective_id, has_side_effects=True)
    else:
        outs += [(grad_shape, BF, fixed(grad_shape))]
    return pl.pallas_call(
        functools.partial(back_kernel, nb, count),
        grid=(2 * nb,),
        in_specs=[
            whole(packing[0]), whole(packing[1]), both, heads, whole(k), whole(v), row(qw + HD), heads, vec, vec, late,
            whole(w_query), whole(w_keyval), whole(gains), whole(gg), row(HD // 2), row(HD // 2),
        ]
        + [pl.BlockSpec(memory_space=pl.ANY)] * count,
        out_specs=[spec for _, _, spec in outs],
        scratch_shapes=scratch,
        out_shape=[jax.ShapeDtypeStruct(shape, dtype) for shape, dtype, _ in outs],
        compiler_params=pltpu.CompilerParams(**params),
        cost_estimate=pl.CostEstimate(flops=20 * 10**9, bytes_accessed=30 * 10**6, transcendentals=4 * 10**6),
        name="back",
    )(*packing, x, q, k, v, raw, datt, lse, spread, dmid, w_query, w_keyval, gains, gg, cosine, sine, *shaped)


def tables(rows):
    freqs = np.float32(THETA) ** (-(np.arange(HD // 2, dtype=np.float32) * np.float32(2.0 / HD)))
    angles = np.arange(rows, dtype=np.float32)[:, None] * freqs[None, :].astype(np.float32)
    return np.cos(angles).astype(np.float32), np.sin(angles).astype(np.float32)


def scatter(grad):
    return lax.psum(lax.psum_scatter(grad, "shard", scatter_dimension=0, tiled=True).astype(F32), "rep")


def by_rows(grad):
    return grad.transpose(0, 2, 1, 3).reshape(-1, grad.shape[1] * grad.shape[3])


def by_columns(grad):
    parts, d, cols = grad.shape
    return grad.transpose(0, 2, 1).reshape(parts * cols, d)


def shards(
    tokens, seq_lengths, seq_device, w_query, w_keyval, w_project, w_gate, w_upward, w_down,
    gain_input, gain_query, gain_key, gain_attend, gain_before, gain_after, cotangent,
):
    n_shard = lax.axis_size("shard")
    own_kernels = (n_shard, lax.axis_size("rep")) == (8, 4)
    me = lax.axis_index("shard")
    packing = (seq_lengths[None, :], seq_device[None, :])
    part = w_query.shape[0]
    d = part * n_shard
    ff = w_gate.shape[1]
    qw = w_query.shape[1]
    head_part = gain_query.shape[0]
    wide = lambda g: jnp.pad(g, (0, 128 - g.shape[0]))
    own_gains = jnp.stack(
        [
            jnp.concatenate([wide(g) for g in (gain_input, gain_attend, gain_before, gain_after)]),
            jnp.concatenate([wide(gain_query), wide(gain_key), jnp.zeros((256,), BF)]),
        ]
        + [jnp.zeros((512,), BF)] * 14
    )
    early = [w_query, w_keyval, own_gains]
    late = [w_project, w_gate, w_upward, w_down]
    cosine, sine = (jnp.asarray(t) for t in tables(tokens.shape[0]))
    collect = lambda parts: [lax.all_gather(p, "shard", axis=0, tiled=True) for p in parts]
    if own_kernels:
        q, k, v, raw, att, lse, gains, query_full, keyval_full, *rest = attend(
            packing, tokens, cosine, sine, n_shard, early + late, [], 3
        )
    else:
        fulls = collect(early)
        q, k, v, raw, att, lse, gains = attend(packing, tokens, cosine, sine, n_shard, [], fulls, 3)
        query_full, keyval_full = fulls[:2]
        rest = collect(late)
    act, dmid, datt, spread, gg, gate_grad, up_grad, down_grad, project_grad = feed(
        packing, tokens, att, cotangent, *rest[1:], rest[0], gains
    )
    pieces = lambda g: g.reshape(COLUMN_STEPS, 8, d // 8, g.shape[2])
    late_sums = ([], [])
    if own_kernels:
        late_sums = (
            [gate_grad, up_grad, pieces(down_grad), pieces(project_grad)],
            [w_gate.shape, w_upward.shape, w_down.shape[::-1], w_project.shape[::-1], w_query.shape, w_keyval.shape],
        )
    din, gg, *rest = back(
        packing, tokens, q, k, v, raw, datt, lse, spread, dmid, query_full, keyval_full, gains, gg, cosine, sine,
        *late_sums, 4,
    )
    if own_kernels:
        gate, upward, down, project, query, keyval, sums = rest
        down, project = down.T, project.T
    else:
        gate, upward = scatter(by_rows(gate_grad)), scatter(by_rows(up_grad))
        both = scatter(by_rows(rest[0].reshape(COLUMN_STEPS, -1, *rest[0].shape[5:])))
        query, keyval = both[:, :qw], both[:, qw:]
        down, project = scatter(by_columns(down_grad)), scatter(by_columns(project_grad))
        sums = lax.psum(gg, ("shard", "rep"))
    own = lambda row, size: lax.dynamic_slice(sums, (row, me * size), (1, size))[0]
    return (
        act, din, query, keyval, project, gate, upward, down,
        own(0, part), own(4, head_part), own(5, head_part), own(1, part), own(2, part), own(3, part),
    )


def solution(mesh):
    rows, weight, gain = P(("shard", "rep"), None), P("shard", None), P("shard")
    return jax.shard_map(
        shards,
        mesh=mesh,
        in_specs=(rows, P(), P()) + (weight,) * 6 + (gain,) * 6 + (rows,),
        out_specs=(rows, rows) + (weight,) * 6 + (gain,) * 6,
        check_vma=False,
    )
```

```python
import functools
import math

import jax
import jax.numpy as jnp
import numpy as np
from jax import lax
from jax.experimental import pallas as pl
from jax.experimental.pallas import tpu as pltpu
from jax.sharding import PartitionSpec as P

QH = 4
HD = 256
EPS = 1e-06
THETA = 1000000.0
RB = 256
FEED_ROWS = 512
COLUMN_STEPS = 8
F32 = jnp.float32
BF = jnp.bfloat16
EXP_SCALE = HD ** (-0.5) * math.log2(math.e)
MESH = pl.DeviceIdType.MESH
HIDDEN = -1e30
GELU_C = math.sqrt(2.0 / math.pi)


def dot(left, right):
    return lax.dot_general(left, right, (((1,), (0,)), ((), ())), preferred_element_type=F32)


def dot_nt(left, right):
    return lax.dot_general(left, right, (((1,), (1,)), ((), ())), preferred_element_type=F32)


def inv_rms(value):
    return lax.rsqrt(jnp.mean(value * value, axis=-1, keepdims=True) + EPS)


def rotate(value, cosine, sine):
    first, second = value[:, : HD // 2], value[:, HD // 2 :]
    return jnp.concatenate(
        [first * cosine - second * sine, second * cosine + first * sine], axis=-1
    )


def extents(lens_ref, owner_ref):
    device = lax.axis_index("shard") * lax.axis_size("rep") + lax.axis_index("rep")
    count = lens_ref.shape[1]
    ids = lax.broadcasted_iota(jnp.int32, (1, count), 1).astype(F32)
    mine = owner_ref[...] == device
    lens = lens_ref[...].astype(F32)
    first = jnp.min(jnp.where(mine, ids, float(count)), axis=1, keepdims=True)
    bound = jnp.sum(jnp.where(ids == first, lens, 0.0), axis=1, keepdims=True)
    total = jnp.sum(jnp.where(mine, lens, 0.0), axis=1, keepdims=True)
    return bound.astype(jnp.int32), total.astype(jnp.int32)


def seen_mask(bound, query_block, key_block, rb):
    keys = key_block * rb + lax.broadcasted_iota(jnp.int32, (rb, rb), 0)
    rows = query_block * rb + lax.broadcasted_iota(jnp.int32, (rb, rb), 1)
    return (keys <= rows) & (keys >= jnp.where(rows >= bound, bound, 0))


class Places:
    def __init__(self):
        s, r = lax.axis_index("shard"), lax.axis_index("rep")
        z, self.c = lax.div(s, 2), lax.rem(s, 2)
        self.y, self.x = lax.div(r, 2), lax.rem(r, 2)
        self.s, self.r, self.z = s, r, z
        zs = [z, z + 1 - 2 * lax.rem(z, 2), z + 2 - 4 * lax.div(z, 2), 3 - z]
        self.zs = zs
        self.across = r + 1 - 2 * self.x
        self.along = r + 2 - 4 * self.y
        self.shards = [2 * zp + self.c for zp in zs]
        self.core = (s + 1 - 2 * self.c, r)
        self.xdev = (s, self.across)
        self.ydev = (s, self.along)
        self.zdev = [None] + [(self.shards[k], r) for k in (1, 2, 3)]
        self.all = [self.core, self.xdev, self.ydev] + self.zdev[1:]

    def greet(self):
        barrier = pltpu.get_barrier_semaphore()
        for device in self.all:
            pl.semaphore_signal(barrier, inc=1, device_id=device, device_id_type=MESH)
        pl.semaphore_wait(barrier, len(self.all))


class Gather:
    SEMS = 20

    def __init__(self, at, parts, fulls, groups, send, recv):
        self.at, self.parts, self.fulls, self.groups, self.send, self.recv = at, parts, fulls, groups, send, recv

    def split(self, n):
        rows, cols = self.parts[n].shape
        if cols % 512 == 0:
            width = cols // 4
            return True, width, min(width, (width // 128 + 1) // 2 * 128)
        return False, rows // 4, rows // 8

    def view(self, n, ref, shard, q, half=None):
        by_cols, size, first = self.split(n)
        rows = self.parts[n].shape[0]
        begin, length = q * size, size
        if half == 0:
            length = first
        if half == 1:
            begin, length = begin + first, size - first
        base = 0 if shard is None else shard * rows
        if by_cols:
            return ref.at[pl.ds(pl.multiple_of(base, 16), rows), pl.ds(pl.multiple_of(begin, 128), length)]
        return ref.at[pl.ds(pl.multiple_of(base + begin, 16), length), :]

    def copy(self, n, idx, src, dst, device):
        return pltpu.make_async_remote_copy(
            src_ref=src, dst_ref=dst, send_sem=self.send.at[n, idx], recv_sem=self.recv.at[n, idx],
            device_id=device, device_id_type=MESH,
        )

    def rows_of(self, n, shard):
        rows = self.parts[n].shape[0]
        return self.fulls[n].at[pl.ds(pl.multiple_of(shard * rows, 16), rows), :]

    def out_z(self, n, k):
        at = self.at
        return self.copy(
            n, k - 1, self.view(n, self.parts[n], None, at.r), self.view(n, self.fulls[n], at.s, at.r), at.zdev[k]
        )

    def out_xy(self, n, k, way):
        at = self.at
        piece = self.view(n, self.fulls[n], at.shards[k], at.r)
        return self.copy(n, 3 + 3 * way + k - 1, piece, piece, (at.xdev, at.ydev)[way])

    def halves(self, n):
        _, size, first = self.split(n)
        return (0,) if size == first else (0, 1)

    def out_diag(self, n, k, half):
        at = self.at
        q, device = ((at.across, at.ydev), (at.along, at.xdev))[half]
        piece = self.view(n, self.fulls[n], at.shards[k], q, half)
        return self.copy(n, 9 + 3 * half + k - 1, piece, piece, device)

    def out_core(self, n, k):
        src = self.parts[n] if k == 0 else self.rows_of(n, self.at.shards[k])
        return self.copy(n, 15 + k, src, self.rows_of(n, self.at.shards[k]), self.at.core)

    def own(self, n):
        return pltpu.make_async_copy(self.parts[n], self.rows_of(n, self.at.s), self.send.at[n, 19])

    AHEAD = 3

    def items(self):
        return [(group, k) for group in self.groups for k in (1, 2, 3)]

    def first(self):
        for group, k in self.items()[: self.AHEAD]:
            for n in group:
                self.out_z(n, k).start()
        for group in self.groups:
            for n in group:
                self.out_core(n, 0).start()
                self.own(n).start()

    def second(self, slot):
        items = self.items()
        group, k = items[slot]
        for n in group:
            self.out_z(n, k).wait_recv()
            self.out_xy(n, k, 0).start()
            self.out_xy(n, k, 1).start()
        if slot + self.AHEAD < len(items):
            group, k = items[slot + self.AHEAD]
            for n in group:
                self.out_z(n, k).start()

    def third(self, slot):
        group, k = self.items()[slot]
        for n in group:
            self.out_xy(n, k, 0).wait_recv()
            self.out_diag(n, k, 0).start()
            self.out_xy(n, k, 1).wait_recv()
            if 1 in self.halves(n):
                self.out_diag(n, k, 1).start()

    def fourth(self, slot):
        group, k = self.items()[slot]
        for n in group:
            for half in self.halves(n):
                self.out_diag(n, k, half).wait_recv()
            self.out_core(n, k).start()

    def slots(self):
        return len(self.items()) + 3

    def advance(self, slot):
        for lag, stage in ((0, self.second), (1, self.third), (3, self.fourth)):
            if 0 <= slot - lag < len(self.items()):
                stage(slot - lag)

    def ready(self, n):
        self.own(n).wait()
        for k in range(4):
            self.out_core(n, k).wait_recv()

    def sent(self, n):
        for k in range(4):
            self.out_core(n, k).wait_send()
        for k in (1, 2, 3):
            self.out_z(n, k).wait_send()
            self.out_xy(n, k, 0).wait_send()
            self.out_xy(n, k, 1).wait_send()
            for half in self.halves(n):
                self.out_diag(n, k, half).wait_send()

    @staticmethod
    def sems(count):
        return [pltpu.SemaphoreType.DMA((count, Gather.SEMS)), pltpu.SemaphoreType.DMA((count, Gather.SEMS))]


class Reduce:
    SEMS = 16

    def __init__(self, at, splits, grads, bufs, send, recv):
        self.at, self.splits, self.grads, self.bufs, self.send, self.recv = at, splits, grads, bufs, send, recv

    @staticmethod
    def sizes(a, b, rows, cols):
        piece = (rows, cols)
        shapes = [
            (4, 2, 2, a + b) + piece,
            (4, 2, 2, a + b) + piece,
            (4, 2, a) + piece,
            (4, 2, b) + piece,
            (4, a) + piece,
            (4, b) + piece,
            (3, a + b) + piece,
            (2, 2, a + b) + piece,
        ]
        return [pltpu.VMEM(shape, BF) for shape in shapes]

    def copy(self, n, idx, src, dst, device):
        return pltpu.make_async_remote_copy(
            src_ref=src, dst_ref=dst, send_sem=self.send.at[n, idx], recv_sem=self.recv.at[n, idx],
            device_id=device, device_id_type=MESH,
        )

    def own(self, n):
        return pltpu.make_async_copy(self.grads[n].at[:, self.at.c], self.bufs[n][0], self.send.at[n, 15])

    def out_core(self, n):
        return self.copy(n, 0, self.grads[n].at[:, 1 - self.at.c], self.bufs[n][1], self.at.core)

    def out_1(self, n, way):
        at, (a, b) = self.at, self.splits[n]
        total = self.bufs[n][0]
        if way == 0:
            return self.copy(n, 1, total.at[:, :, 1 - at.x, pl.ds(0, a)], self.bufs[n][2], at.xdev)
        return self.copy(n, 2, total.at[:, 1 - at.y, :, pl.ds(a, b)], self.bufs[n][3], at.ydev)

    def out_2(self, n, way):
        at, (a, b) = self.at, self.splits[n]
        total = self.bufs[n][0]
        if way == 0:
            return self.copy(n, 3, total.at[:, 1 - at.y, at.x, pl.ds(0, a)], self.bufs[n][4], at.ydev)
        return self.copy(n, 4, total.at[:, at.y, 1 - at.x, pl.ds(a, b)], self.bufs[n][5], at.xdev)

    def out_z(self, n, k):
        at = self.at
        return self.copy(n, 4 + k, self.bufs[n][0].at[at.zs[k], at.y, at.x], self.bufs[n][6].at[k - 1], at.zdev[k])

    def out_final(self, n, way):
        at = self.at
        piece = self.bufs[n][7].at[at.y, at.x]
        return self.copy(n, 8 + way, piece, piece, (at.xdev, at.ydev)[way])

    def out_diag(self, n, way):
        at, (a, b) = self.at, self.splits[n]
        result = self.bufs[n][7]
        if way == 0:
            piece = result.at[at.y, 1 - at.x, pl.ds(0, a)]
            return self.copy(n, 10, piece, piece, at.ydev)
        piece = result.at[1 - at.y, at.x, pl.ds(a, b)]
        return self.copy(n, 11, piece, piece, at.xdev)

    def start(self, n):
        self.out_core(n).start()
        self.own(n).start()

    def one(self, n):
        total, other = self.bufs[n][0], self.bufs[n][1]
        a, b = self.splits[n]
        self.own(n).wait()
        self.out_core(n).wait_recv()

        def add(zp, carry):
            for y in range(2):
                for x in range(2):
                    for p in range(a + b):
                        total[zp, y, x, p] = total[zp, y, x, p] + other[zp, y, x, p]
            return carry

        lax.fori_loop(0, 4, add, 0)
        self.out_1(n, 0).start()
        self.out_1(n, 1).start()

    def two(self, n):
        total, at, (a, b) = self.bufs[n][0], self.at, self.splits[n]
        self.out_1(n, 0).wait()
        self.out_1(n, 1).wait()
        from_x, from_y = self.bufs[n][2], self.bufs[n][3]

        def add(zp, carry):
            for m in range(2):
                for p in range(a):
                    total[zp, m, at.x, p] = total[zp, m, at.x, p] + from_x[zp, m, p]
                for p in range(b):
                    total[zp, at.y, m, a + p] = total[zp, at.y, m, a + p] + from_y[zp, m, p]
            return carry

        lax.fori_loop(0, 4, add, 0)
        self.out_2(n, 0).start()
        self.out_2(n, 1).start()

    def three(self, n):
        total, at, (a, b) = self.bufs[n][0], self.at, self.splits[n]
        self.out_2(n, 0).wait()
        self.out_2(n, 1).wait()
        from_y, from_x = self.bufs[n][4], self.bufs[n][5]

        def add(zp, carry):
            for p in range(a):
                total[zp, at.y, at.x, p] = total[zp, at.y, at.x, p] + from_y[zp, p]
            for p in range(b):
                total[zp, at.y, at.x, a + p] = total[zp, at.y, at.x, a + p] + from_x[zp, p]
            return carry

        lax.fori_loop(0, 4, add, 0)
        for k in (1, 2, 3):
            self.out_z(n, k).start()

    def four(self, n):
        total, result, from_z, at = self.bufs[n][0], self.bufs[n][7], self.bufs[n][6], self.at
        for k in (1, 2, 3):
            self.out_z(n, k).wait()
        for p in range(sum(self.splits[n])):
            value = total[at.z, at.y, at.x, p].astype(F32)
            for k in range(3):
                value = value + from_z[k, p].astype(F32)
            result[at.y, at.x, p] = value.astype(BF)
        self.out_final(n, 0).start()
        self.out_final(n, 1).start()

    def five(self, n):
        for way in range(2):
            self.out_final(n, way).wait_recv()
            self.out_diag(n, way).start()

    def six(self, n):
        for way in range(2):
            self.out_diag(n, way).wait()
            self.out_final(n, way).wait_send()
        self.out_core(n).wait_send()

    def stages(self):
        return [self.one, self.two, self.three, self.four, self.five, self.six]

    def waves(self):
        stages, count = self.stages(), len(self.grads)
        return [
            (t, stages[t - n], n)
            for t in range(count + len(stages) - 1)
            for n in range(count)
            if 0 <= t - n < len(stages)
        ]


class Small:
    SEMS = 6

    def __init__(self, at, value, total, inbox, send, recv):
        self.at, self.value, self.total, self.inbox, self.send, self.recv = at, value, total, inbox, send, recv

    def copy(self, idx):
        at = self.at
        slot, device = idx, at.all[idx]
        return pltpu.make_async_remote_copy(
            src_ref=self.total.at[min(idx, 3)], dst_ref=self.inbox.at[slot], send_sem=self.send.at[idx],
            recv_sem=self.recv.at[idx], device_id=device, device_id_type=MESH,
        )

    def start(self):
        self.total[0] = self.value[...]
        self.copy(0).start()

    def next(self, step):
        if step == 3:
            for idx in (3, 4, 5):
                self.copy(idx).wait()
            self.total[4] = self.total[3] + self.inbox[3] + self.inbox[4] + self.inbox[5]
            return
        self.copy(step).wait()
        self.total[step + 1] = self.total[step] + self.inbox[step]
        for idx in (step + 1,) if step < 2 else (3, 4, 5):
            self.copy(idx).start()


def unpack(result, outs, turned):
    _, _, pieces, rows, cols = result.shape
    if turned:
        for y in range(2):
            for x in range(2):
                for p in range(pieces):
                    turned_rows = (2 * y + x) * pieces + p
                    outs[0][turned_rows * rows : (turned_rows + 1) * rows, :] = result[y, x, p].astype(F32)
        return
    begin = 0
    for y in range(2):
        for x in range(2):
            for p in range(pieces):
                out = outs[0] if begin < outs[0].shape[1] else outs[1]
                col = begin if begin < outs[0].shape[1] else begin - outs[0].shape[1]
                out[:, col : col + cols] = result[y, x, p].astype(F32)
                begin += cols


EARLY = 3
GROUPS = ((0, 1, 2), (4,), (5,), (6, 3))
BEFORE = 6
PLACES = ((0, 2), (1, 1), (1, 2), (2, 1), (2, 2), (3, 1), (3, 2), (4, 1), (4, 2))


def spread_gains(table_ref, g_ref, n_shard):
    d, size = g_ref.shape[1], g_ref.shape[1] // n_shard
    g_ref[...] = jnp.zeros_like(g_ref)
    step = table_ref.shape[0] // n_shard
    for row, slot, width, to in [(0, lane, size, lane) for lane in range(4)] + [
        (1, lane, HD // n_shard, 4 + lane) for lane in range(2)
    ]:
        lanes = lax.broadcasted_iota(jnp.int32, (128, d), 0)
        cols = lax.broadcasted_iota(jnp.int32, (128, d), 1)
        total = jnp.zeros((16, d), F32)
        for shard in range(n_shard):
            here = ((cols == lanes + shard * width) & (lanes < width)).astype(F32).astype(BF)
            total = total + dot(table_ref[shard * step : shard * step + 16, slot * 128 : (slot + 1) * 128], here)
        g_ref[to : to + 1, :] = total[row : row + 1, :]


def attend_kernel(
    nb, n_shard, count, lens_ref, owner_ref, x_ref, cos_ref, sin_ref, *refs
):
    i = pl.program_id(0)
    if count:
        parts, refs = refs[:count], refs[count:]
        q_out, k_out, v_out, raw_out, att_out, lse_out, g_ref = refs[:7]
        fulls, refs = refs[7 : 7 + count - 1], refs[7 + count - 1 :]
        k_all, vt_all, acc, den, wq_ref, wkv_ref, table_ref, send, recv, keep = refs
        at = Places()
        work = Gather(at, parts, (wq_ref, wkv_ref, table_ref) + fulls[2:], GROUPS, send, recv)
        kept = [
            pltpu.make_async_copy(wq_ref, fulls[0], keep.at[0]),
            pltpu.make_async_copy(wkv_ref, fulls[1], keep.at[1]),
        ]

        @pl.when(i == 0)
        def _():
            at.greet()
            work.first()
            for slot in range(BEFORE):
                work.advance(slot)
            for n in range(EARLY):
                work.ready(n)
            for copy in kept:
                copy.start()
            spread_gains(table_ref, g_ref, n_shard)

    else:
        wq_ref, wkv_ref, table_ref, q_out, k_out, v_out, raw_out, att_out, lse_out, g_ref, k_all, vt_all, acc, den = refs

        @pl.when(i == 0)
        def _():
            spread_gains(table_ref, g_ref, n_shard)

    def travel(place):
        for slot, (block, where) in enumerate(PLACES if count else ()):
            if where == place:

                @pl.when(i == block)
                def _(slot=slot):
                    work.advance(BEFORE + slot)

    bound, _ = extents(lens_ref, owner_ref)
    rb = x_ref.shape[0]
    d = x_ref.shape[1]
    x = x_ref[...].astype(F32)
    h = (x * inv_rms(x) * g_ref[0:1, :]).astype(BF)
    cosine, sine = cos_ref[...], sin_ref[...]
    qgain, kgain = g_ref[4:5, :HD], g_ref[5:6, :HD]
    for head in range(QH):
        raw = dot(h, wq_ref[:, head * HD : (head + 1) * HD])
        raw_out[:, head * HD : (head + 1) * HD] = raw.astype(BF)
        q_out[head] = rotate(raw * inv_rms(raw) * qgain, cosine, sine).astype(BF)
    raw = dot(h, wkv_ref[:, :HD])
    raw_out[:, QH * HD :] = raw.astype(BF)
    keys = rotate(raw * inv_rms(raw) * kgain, cosine, sine).astype(BF)
    values = dot(h, wkv_ref[:, HD:]).astype(BF)
    k_out[...] = keys
    v_out[...] = values
    k_all[i] = keys
    vt_all[i] = values.T
    travel(1)
    acc[...] = jnp.zeros_like(acc)
    den[...] = jnp.zeros_like(den)

    def step(j, carry):
        hide = jnp.where(seen_mask(bound, i, j, rb), 0.0, HIDDEN)
        scores = dot_nt(k_all[j], q_out[...].reshape(QH * rb, HD))
        probs = jnp.exp2(scores * EXP_SCALE + jnp.concatenate([hide] * QH, axis=1))
        den[...] += jnp.sum(probs.reshape(rb // 8, 8, QH * rb), axis=0)
        acc[...] += dot(vt_all[j], probs.astype(BF))
        return carry

    lax.fori_loop(0, i + 1, step, 0)
    travel(2)
    lse = []
    for head in range(QH):
        cols = slice(head * rb, (head + 1) * rb)
        total = jnp.sum(den[:, cols], axis=0, keepdims=True)
        lse.append(jnp.log2(total))
        att_out[:, head * HD : (head + 1) * HD] = (acc[:, cols] * (1.0 / total)).T.astype(BF)
    lse_out[...] = jnp.concatenate(lse + lse, axis=0)
    if count:

        @pl.when(i == nb - 1)
        def _():
            for copy in kept:
                copy.wait()
            for n in range(EARLY, count):
                work.ready(n)
            for n in range(count):
                work.sent(n)


def attend(packing, x, cosine, sine, n_shard, parts, gathered, collective_id):
    rows, d = x.shape
    rb = RB
    nb = rows // rb
    whole = lambda a: pl.BlockSpec(a.shape, lambda i: (0,) * a.ndim, pipeline_mode=pl.Buffered(1))
    row = lambda width: pl.BlockSpec((rb, width), lambda i: (i, 0))
    far = pl.BlockSpec(memory_space=pl.ANY)
    qw = QH * HD
    params = dict(vmem_limit_bytes=56 * 2**20)
    scratch = [
        pltpu.VMEM((nb, rb, HD), BF),
        pltpu.VMEM((nb, HD, rb), BF),
        pltpu.VMEM((HD, QH * rb), F32),
        pltpu.VMEM((8, QH * rb), F32),
    ]
    fulls = [jax.ShapeDtypeStruct((8 * p.shape[0], p.shape[1]), p.dtype) for p in parts]
    if parts:
        params.update(collective_id=collective_id, has_side_effects=True)
        scratch += [pltpu.VMEM(f.shape, f.dtype) for f in fulls[:EARLY]] + Gather.sems(len(parts))
        scratch += [pltpu.SemaphoreType.DMA((2,))]
    kept = fulls[:2] + fulls[EARLY:]
    return pl.pallas_call(
        functools.partial(attend_kernel, nb, n_shard, len(parts)),
        grid=(nb,),
        in_specs=[whole(packing[0]), whole(packing[1]), row(d), row(HD // 2), row(HD // 2)]
        + [far] * len(parts)
        + [whole(w) for w in gathered],
        out_specs=[
            pl.BlockSpec((QH, rb, HD), lambda i: (0, i, 0)),
            row(HD), row(HD), row(qw + HD), row(qw),
            pl.BlockSpec((8, rb), lambda i: (0, i)),
            pl.BlockSpec((8, d), lambda i: (0, 0)),
        ]
        + [far] * len(kept),
        scratch_shapes=scratch,
        out_shape=[
            jax.ShapeDtypeStruct((QH, rows, HD), BF),
            jax.ShapeDtypeStruct((rows, HD), BF),
            jax.ShapeDtypeStruct((rows, HD), BF),
            jax.ShapeDtypeStruct((rows, qw + HD), BF),
            jax.ShapeDtypeStruct((rows, qw), BF),
            jax.ShapeDtypeStruct((8, rows), F32),
            jax.ShapeDtypeStruct((8, d), F32),
        ]
        + kept,
        compiler_params=pltpu.CompilerParams(**params),
        cost_estimate=pl.CostEstimate(flops=14 * 10**9, bytes_accessed=30 * 10**6, transcendentals=4 * 10**6),
        name="attend",
    )(*packing, x, cosine, sine, *parts, *gathered)


def norm_back(grad, unit, r, gain):
    scaled = grad * gain
    return r * (scaled - unit * jnp.mean(scaled * unit, axis=-1, keepdims=True))


def column_sum(value):
    return jnp.sum(value, axis=0, keepdims=True)


def feed_kernel(
    nb, n_cols, lens_ref, owner_ref, x_ref, att_ref, cot_ref, attc_ref, wg_ref, wu_ref, wd_ref, wp_ref, g_ref,
    act_out, dmid_out, datt_out, spread_out, gg_out, gate_grad, up_grad, down_grad, project_grad,
    hid, dgu, h2t, dft, dbt, act_s, mul_s,
):
    i = pl.program_id(0)
    rb, d = x_ref.shape
    ff = wd_ref.shape[0]
    fc = ff // 4

    @pl.when(i < nb)
    def _():
        start = pl.multiple_of(i * rb, rb)
        rows = pl.ds(start, rb)
        branch = dot(att_ref[...], wp_ref[...])
        r_br = inv_rms(branch)
        unit_br = branch * r_br
        mid = x_ref[...].astype(F32) + unit_br * g_ref[1:2, :]
        r_mid = inv_rms(mid)
        unit_mid = mid * r_mid
        h2 = (unit_mid * g_ref[2:3, :]).astype(BF)
        h2t[:, rows] = h2.T
        for c in range(4):
            cols = slice(c * fc, (c + 1) * fc)
            gate = dot(h2, wg_ref[:, cols])
            up = dot(h2, wu_ref[:, cols])
            sq = gate * gate
            th = jnp.tanh(GELU_C * gate * (1.0 + 0.044715 * sq))
            half = 0.5 + 0.5 * th
            act = gate * half
            slope = half + 0.5 * gate * (1.0 - th * th) * (GELU_C * (1.0 + (3 * 0.044715) * sq))
            hid[rows, cols] = (act * up).astype(BF)
            act_s[:, cols] = act.astype(BF)
            mul_s[:, cols] = (up * slope).astype(BF)
        ffn = dot(hid[rows, :], wd_ref[...])
        r_ffn = inv_rms(ffn)
        unit_ffn = ffn * r_ffn
        after = g_ref[3:4, :]
        act_out[...] = (mid + unit_ffn * after).astype(BF)
        row_ids = start + lax.broadcasted_iota(jnp.int32, (rb, 1), 0)
        _, total = extents(lens_ref, owner_ref)
        ups = jnp.where(row_ids < total, cot_ref[...].astype(F32), 0.0)
        d_ffn = norm_back(ups, unit_ffn, r_ffn, after).astype(BF)
        dft[:, rows] = d_ffn.T
        for c in range(4):
            cols = slice(c * fc, (c + 1) * fc)
            d_hid = dot_nt(d_ffn, wd_ref[cols, :])
            dgu[rows, cols] = (d_hid * mul_s[:, cols]).astype(BF)
            dgu[rows, ff + c * fc : ff + (c + 1) * fc] = (d_hid * act_s[:, cols]).astype(BF)
        d_h2 = dot_nt(dgu[rows, :ff], wg_ref[...]) + dot_nt(dgu[rows, ff:], wu_ref[...])
        d_mid = ups + norm_back(d_h2, unit_mid, r_mid, g_ref[2:3, :])
        dmid_out[...] = d_mid
        d_br = norm_back(d_mid, unit_br, r_br, g_ref[1:2, :]).astype(BF)
        dbt[:, rows] = d_br.T
        d_att = dot_nt(d_br, wp_ref[...])
        datt_low = d_att.astype(BF)
        prod = datt_low.astype(F32) * att_ref[...].astype(F32)
        spread = []
        for head in range(QH):
            cols = slice(head * HD, (head + 1) * HD)
            datt_out[head] = datt_low[:, cols]
            spread.append(jnp.sum(prod[:, cols], axis=1, keepdims=True))
        wide = jnp.concatenate(spread + [jnp.zeros((rb, 128 - QH), F32)], axis=1)
        spread_out[...] = wide.T[:8, :]
        sums = jnp.concatenate(
            [
                jnp.zeros((1, d), F32),
                column_sum(d_mid * unit_br),
                column_sum(d_h2 * unit_mid),
                column_sum(ups * unit_ffn),
                jnp.zeros((4, d), F32),
            ],
            axis=0,
        )

        @pl.when(i == 0)
        def _():
            gg_out[...] = jnp.zeros_like(gg_out)

        gg_out[...] += sums

    @pl.when(i >= nb)
    def _():
        s = i - nb
        width = ff // n_cols
        for grad, base in ((gate_grad, 0), (up_grad, ff)):
            cols = pl.ds(pl.multiple_of(base + s * width, width), width)
            grad[:, 0] = dot(h2t[...], dgu[:, cols]).astype(BF).reshape(n_cols, d // n_cols, width)
        cols = pl.ds(pl.multiple_of(s * width, width), width)
        down_grad[0] = dot(dft[...], hid[:, cols]).astype(BF)
        project_grad[0] = dot(dbt[...], attc_ref[...]).astype(BF)


def feed(packing, x, att, cot, w_gate, w_upward, w_down, w_project, gains):
    rows, d = x.shape
    ff = w_down.shape[0]
    qw = att.shape[1]
    rb = FEED_ROWS
    nb = rows // rb
    whole = lambda a: pl.BlockSpec(a.shape, lambda i, *_: (0,) * a.ndim, pipeline_mode=pl.Buffered(1))
    blk = lambda i: jnp.minimum(i, nb - 1)
    col = lambda i: jnp.maximum(i - nb, 0)
    row = lambda width: pl.BlockSpec((rb, width), lambda i, *_: (blk(i), 0))
    nc = COLUMN_STEPS

    return pl.pallas_call(
        functools.partial(feed_kernel, nb, nc),
        grid_spec=pltpu.PrefetchScalarGridSpec(
            num_scalar_prefetch=0,
            grid=(nb + nc,),
            in_specs=[
                whole(packing[0]), whole(packing[1]), row(d), row(qw), row(d),
                pl.BlockSpec((rows, qw // nc), lambda i, *_: (0, col(i))),
                whole(w_gate), whole(w_upward), whole(w_down), whole(w_project), whole(gains),
            ],
            out_specs=[
                row(d), row(d),
                pl.BlockSpec((QH, rb, HD), lambda i, *_: (0, blk(i), 0)),
                pl.BlockSpec((8, rb), lambda i, *_: (0, blk(i))),
                pl.BlockSpec((8, d), lambda i, *_: (0, 0)),
                pl.BlockSpec((nc, 1, d // nc, ff // nc), lambda i, *_: (0, col(i), 0, 0)),
                pl.BlockSpec((nc, 1, d // nc, ff // nc), lambda i, *_: (0, col(i), 0, 0)),
                pl.BlockSpec((1, d, ff // nc), lambda i, *_: (col(i), 0, 0)),
                pl.BlockSpec((1, d, qw // nc), lambda i, *_: (col(i), 0, 0)),
            ],
            scratch_shapes=[
                pltpu.VMEM((rows, ff), BF),
                pltpu.VMEM((rows, 2 * ff), BF),
                pltpu.VMEM((d, rows), BF),
                pltpu.VMEM((d, rows), BF),
                pltpu.VMEM((d, rows), BF),
                pltpu.VMEM((rb, ff), BF),
                pltpu.VMEM((rb, ff), BF),
            ],
        ),
        out_shape=[
            jax.ShapeDtypeStruct((rows, d), BF),
            jax.ShapeDtypeStruct((rows, d), F32),
            jax.ShapeDtypeStruct((QH, rows, HD), BF),
            jax.ShapeDtypeStruct((8, rows), F32),
            jax.ShapeDtypeStruct((8, d), F32),
            jax.ShapeDtypeStruct((nc, nc, d // nc, ff // nc), BF),
            jax.ShapeDtypeStruct((nc, nc, d // nc, ff // nc), BF),
            jax.ShapeDtypeStruct((nc, d, ff // nc), BF),
            jax.ShapeDtypeStruct((nc, d, qw // nc), BF),
        ],
        compiler_params=pltpu.CompilerParams(vmem_limit_bytes=60 * 2**20),
        cost_estimate=pl.CostEstimate(flops=42 * 10**9, bytes_accessed=50 * 10**6, transcendentals=4 * 10**6),
        name="feed",
    )(*packing, x, att, cot, att, w_gate, w_upward, w_down, w_project, gains)


TRAVEL = ((0, 1, 1, 0), (0, 2, 1, 1), (1, 0, 2, 0), (1, 0, 1, 2), (1, 3, 3, 0), (1, 3, 2, 1), (2, 0, 1, 3), (2, 2, 3, 1), (2, 2, 2, 2), (2, 3, 4, 0), (3, 0, 2, 3), (3, 1, 5, 0), (3, 2, 4, 1), (3, 2, 3, 2), (3, 3, 6, 0), (3, 3, 3, 3), (3, 3, 5, 1), (6, 0, 4, 2), (6, 0, 6, 1), (6, 0, 4, 3), (7, 0, 1, 4), (9, 0, 5, 2), (9, 0, 5, 3))
LAST = ((2, 4), (6, 2), (6, 3), (3, 4), (4, 4), (5, 4), (6, 4))
SPLITS = ((1, 1), (1, 1), (1, 1), (1, 1), (2, 1))
TURNED = (False, False, True, True, False)


def back_kernel(
    nb, count, lens_ref, owner_ref, x_ref, q_ref, k_ref, v_ref, raw_ref, datt_ref, lse_ref, spread_ref, dmid_ref,
    wq_ref, wkv_ref, g_ref, gg_ref, cos_ref, sin_ref, *refs
):
    grads, (din_out, gg_out), refs = refs[:count], refs[count : count + 2], list(refs[count + 2 :])
    sums = [refs.pop(0) for _ in range(count + 3)] if count else []
    w_grad = refs.pop(0)
    kt_all, dk, dv, dqt, ht, dqkv = refs[:6]
    step_id = pl.program_id(0)
    if count:
        refs = refs[6:]
        bufs = [[refs.pop(0) for _ in range(8)] for _ in range(count + 1)]
        total, inbox, send, recv, small_send, small_recv = refs
        at = Places()
        work = Reduce(at, SPLITS, list(grads) + [w_grad], bufs, send, recv)
        small = Small(at, gg_out, total, inbox, small_send, small_recv)

        @pl.when(step_id == 0)
        def _():
            at.greet()
            for n in range(count):
                work.start(n)

    def advance(stage, n):
        work.stages()[stage - 1](n)
        if n == count and stage <= 4:
            small.next(stage - 1)

    def travel(place):
        for block, where, stage, n in TRAVEL if count else ():
            if where == place:

                @pl.when(step_id == block)
                def _(stage=stage, n=n):
                    advance(stage, n)

    travel(0)

    @pl.when(step_id < nb)
    def _():
        attend_back(
            nb, travel, lens_ref, owner_ref, x_ref, q_ref, k_ref, v_ref, raw_ref, datt_ref, lse_ref, spread_ref,
            wq_ref, wkv_ref, g_ref, gg_ref, cos_ref, sin_ref, gg_out, w_grad, kt_all, dk, dv, dqt, ht, dqkv,
        )

    if count:

        @pl.when(step_id == nb - 1)
        def _():
            work.start(count)
            small.start()

    @pl.when(step_id >= nb)
    def _():
        rb = x_ref.shape[0]
        qw = wq_ref.shape[1]
        rows = pl.ds(pl.multiple_of((step_id - nb) * rb, rb), rb)
        d_h = dot_nt(dqkv[rows, :qw], wq_ref[...]) + dot_nt(dqkv[rows, qw:], wkv_ref[...])
        x = x_ref[...].astype(F32)
        r = inv_rms(x)
        din_out[...] = dmid_ref[...] + norm_back(d_h, x * r, r, g_ref[0:1, :])

    if count:

        @pl.when(step_id == 2 * nb - 1)
        def _():
            for stage, n in LAST:
                advance(stage, n)
            for n in range(count + 1):
                unpack(bufs[n][7], sums[n : n + 1] if n < count else sums[n : n + 2], TURNED[n])
            sums[-1][...] = total[4]


def attend_back(
    nb, travel, lens_ref, owner_ref, x_ref, q_ref, k_ref, v_ref, raw_ref, datt_ref, lse_ref, spread_ref,
    wq_ref, wkv_ref, g_ref, gg_ref, cos_ref, sin_ref, gg_out, w_grad, kt_all, dk, dv, dqt, ht, dqkv,
):
    step_id = pl.program_id(0)
    i = nb - 1 - step_id
    bound, _ = extents(lens_ref, owner_ref)
    rb, d = x_ref.shape
    qw = QH * HD

    @pl.when(step_id == 0)
    def _():
        for j in range(nb):
            kt_all[j] = k_ref[j * rb : (j + 1) * rb, :].T
        dk[...] = jnp.zeros_like(dk)
        dv[...] = jnp.zeros_like(dv)
        gg_out[...] = gg_ref[...]

    dqt[...] = jnp.zeros_like(dqt)

    def step(j, carry):
        rows = pl.ds(pl.multiple_of(j * rb, rb), rb)
        hide = jnp.where(seen_mask(bound, i, j, rb), 0.0, HIDDEN)
        keys = k_ref[rows, :]
        queries = q_ref[...].reshape(QH * rb, HD)
        d_out = datt_ref[...].reshape(QH * rb, HD)
        by_head = lambda ref: jnp.concatenate([ref[head : head + 1, :] for head in range(QH)], axis=1)
        scores = dot_nt(keys, queries)
        d_probs = dot_nt(v_ref[rows, :], d_out)
        probs = jnp.exp2(scores * EXP_SCALE - by_head(lse_ref) + jnp.concatenate([hide] * QH, axis=1))
        d_scores = (probs * (d_probs - by_head(spread_ref))).astype(BF)
        dv[j] += dot(probs.astype(BF), d_out)
        dk[j] += dot(d_scores, queries)
        dqt[...] += dot(kt_all[j], d_scores)
        return carry

    for third in range(3):
        lax.fori_loop(lax.div((i + 1) * third, 3), lax.div((i + 1) * (third + 1), 3), step, 0)
        travel(third + 1)
    rows = pl.ds(pl.multiple_of(i * rb, rb), rb)
    cosine, sine = cos_ref[...], sin_ref[...]
    scale = HD ** (-0.5)
    qgain, kgain = g_ref[4:5, :HD], g_ref[5:6, :HD]
    q_sum = jnp.zeros((1, HD), F32)
    for head in range(QH):
        grad = rotate(dqt[:, head * rb : (head + 1) * rb].T * scale, cosine, -sine)
        raw = raw_ref[:, head * HD : (head + 1) * HD].astype(F32)
        r = inv_rms(raw)
        unit = raw * r
        q_sum = q_sum + column_sum(grad * unit)
        dqkv[rows, head * HD : (head + 1) * HD] = norm_back(grad, unit, r, qgain).astype(BF)
    grad = rotate(dk[i] * scale, cosine, -sine)
    raw = raw_ref[:, qw : qw + HD].astype(F32)
    r = inv_rms(raw)
    unit = raw * r
    k_sum = column_sum(grad * unit)
    dqkv[rows, qw : qw + HD] = norm_back(grad, unit, r, kgain).astype(BF)
    dqkv[rows, qw + HD :] = dv[i].astype(BF)
    x = x_ref[...].astype(F32)
    ht[:, rows] = (x * inv_rms(x) * g_ref[0:1, :]).astype(BF).T
    rest = jnp.zeros((1, d - HD), F32)
    gg_out[...] += jnp.concatenate(
        [
            jnp.zeros((4, d), F32),
            jnp.concatenate([q_sum, rest], axis=1),
            jnp.concatenate([k_sum, rest], axis=1),
            jnp.zeros((2, d), F32),
        ],
        axis=0,
    )

    @pl.when(step_id == nb - 1)
    def _():
        _, _, _, _, pieces, part_rows, width = w_grad.shape
        gained = jnp.zeros((d, 1), F32)
        for c in range(2 * pieces):
            wide = slice(2 * c * width, 2 * (c + 1) * width)
            value = dot(ht[...], dqkv[:, wide])
            base = 2 * c * width - qw
            weight = wq_ref[:, wide] if base < 0 else wkv_ref[:, base : base + 2 * width]
            gained = gained + jnp.sum(value * weight.astype(F32), axis=1, keepdims=True)
            value = value.astype(BF)
            for side in range(2):
                quarter, p = divmod(2 * c + side, pieces)
                half = value[:, side * width : (side + 1) * width]
                w_grad[:, :, quarter // 2, quarter % 2, p] = half.reshape(4, 2, part_rows, width)
        across = jnp.broadcast_to(gained, (d, 128)).T
        gg_out[0:1, :] = across[0:1, :] / g_ref[0:1, :]


def back(packing, x, q, k, v, raw, datt, lse, spread, dmid, w_query, w_keyval, gains, gg, cosine, sine, grads, out_shapes, collective_id):
    rows, d = x.shape
    rb = RB
    nb = rows // rb
    qw = QH * HD
    nc = COLUMN_STEPS
    count = len(grads)
    first = lambda i: jnp.maximum(nb - 1 - i, 0)
    second = lambda i: jnp.maximum(i - nb, 0)
    whole = lambda a: pl.BlockSpec(a.shape, lambda i: (0,) * a.ndim, pipeline_mode=pl.Buffered(1))
    row = lambda width: pl.BlockSpec((rb, width), lambda i: (first(i), 0))
    late = pl.BlockSpec((rb, d), lambda i: (second(i), 0))
    both = pl.BlockSpec((rb, d), lambda i: (jnp.where(i < nb, nb - 1 - i, i - nb), 0))
    heads = pl.BlockSpec((QH, rb, HD), lambda i: (0, first(i), 0))
    vec = pl.BlockSpec((8, rb), lambda i: (0, first(i)))
    fixed = lambda shape: pl.BlockSpec(shape, lambda i: (0,) * len(shape))
    grad_shape = (4, 2, 2, 2, (qw + 2 * HD) // 512, d // nc, 128)
    shaped = [g.reshape(4, 2, 2, 2, g.shape[1] // 4, *g.shape[2:]) for g in grads]
    scratch = [
        pltpu.VMEM((nb, HD, rb), BF),
        pltpu.VMEM((nb, rb, HD), F32),
        pltpu.VMEM((nb, rb, HD), F32),
        pltpu.VMEM((HD, QH * rb), F32),
        pltpu.VMEM((d, rows), BF),
        pltpu.VMEM((rows, qw + 2 * HD), BF),
    ]
    params = dict(vmem_limit_bytes=58 * 2**20)
    outs = [((rows, d), F32, late), ((8, d), F32, fixed((8, d)))]
    if grads:
        outs += [(s, F32, fixed(s)) for s in (*out_shapes, (8, d))]
        sizes = [g.shape[4:] for g in shaped] + [grad_shape[4:]]
        scratch = [pltpu.VMEM(grad_shape, BF)] + scratch
        scratch += [b for split, shape in zip(SPLITS, sizes) for b in Reduce.sizes(*split, *shape[1:])]
        scratch += [pltpu.VMEM((5, 8, d), F32), pltpu.VMEM((6, 8, d), F32)]
        scratch += [pltpu.SemaphoreType.DMA((count + 1, Reduce.SEMS))] * 2 + [pltpu.SemaphoreType.DMA((Small.SEMS,))] * 2
        params.update(collective_id=collective_id, has_side_effects=True)
    else:
        outs += [(grad_shape, BF, fixed(grad_shape))]
    return pl.pallas_call(
        functools.partial(back_kernel, nb, count),
        grid=(2 * nb,),
        in_specs=[
            whole(packing[0]), whole(packing[1]), both, heads, whole(k), whole(v), row(qw + HD), heads, vec, vec, late,
            whole(w_query), whole(w_keyval), whole(gains), whole(gg), row(HD // 2), row(HD // 2),
        ]
        + [pl.BlockSpec(memory_space=pl.ANY)] * count,
        out_specs=[spec for _, _, spec in outs],
        scratch_shapes=scratch,
        out_shape=[jax.ShapeDtypeStruct(shape, dtype) for shape, dtype, _ in outs],
        compiler_params=pltpu.CompilerParams(**params),
        cost_estimate=pl.CostEstimate(flops=20 * 10**9, bytes_accessed=30 * 10**6, transcendentals=4 * 10**6),
        name="back",
    )(*packing, x, q, k, v, raw, datt, lse, spread, dmid, w_query, w_keyval, gains, gg, cosine, sine, *shaped)


def tables(rows):
    freqs = np.float32(THETA) ** (-(np.arange(HD // 2, dtype=np.float32) * np.float32(2.0 / HD)))
    angles = np.arange(rows, dtype=np.float32)[:, None] * freqs[None, :].astype(np.float32)
    return np.cos(angles).astype(np.float32), np.sin(angles).astype(np.float32)


def scatter(grad):
    return lax.psum(lax.psum_scatter(grad, "shard", scatter_dimension=0, tiled=True).astype(F32), "rep")


def by_rows(grad):
    return grad.transpose(0, 2, 1, 3).reshape(-1, grad.shape[1] * grad.shape[3])


def by_columns(grad):
    parts, d, cols = grad.shape
    return grad.transpose(0, 2, 1).reshape(parts * cols, d)


def shards(
    tokens, seq_lengths, seq_device, w_query, w_keyval, w_project, w_gate, w_upward, w_down,
    gain_input, gain_query, gain_key, gain_attend, gain_before, gain_after, cotangent,
):
    n_shard = lax.axis_size("shard")
    own_kernels = (n_shard, lax.axis_size("rep")) == (8, 4)
    me = lax.axis_index("shard")
    packing = (seq_lengths[None, :], seq_device[None, :])
    part = w_query.shape[0]
    d = part * n_shard
    ff = w_gate.shape[1]
    qw = w_query.shape[1]
    head_part = gain_query.shape[0]
    wide = lambda g: jnp.pad(g, (0, 128 - g.shape[0]))
    own_gains = jnp.stack(
        [
            jnp.concatenate([wide(g) for g in (gain_input, gain_attend, gain_before, gain_after)]),
            jnp.concatenate([wide(gain_query), wide(gain_key), jnp.zeros((256,), BF)]),
        ]
        + [jnp.zeros((512,), BF)] * 14
    )
    early = [w_query, w_keyval, own_gains]
    late = [w_project, w_gate, w_upward, w_down]
    cosine, sine = (jnp.asarray(t) for t in tables(tokens.shape[0]))
    collect = lambda parts: [lax.all_gather(p, "shard", axis=0, tiled=True) for p in parts]
    if own_kernels:
        q, k, v, raw, att, lse, gains, query_full, keyval_full, *rest = attend(
            packing, tokens, cosine, sine, n_shard, early + late, [], 3
        )
    else:
        fulls = collect(early)
        q, k, v, raw, att, lse, gains = attend(packing, tokens, cosine, sine, n_shard, [], fulls, 3)
        query_full, keyval_full = fulls[:2]
        rest = collect(late)
    act, dmid, datt, spread, gg, gate_grad, up_grad, down_grad, project_grad = feed(
        packing, tokens, att, cotangent, *rest[1:], rest[0], gains
    )
    pieces = lambda g: g.reshape(COLUMN_STEPS, 8, d // 8, g.shape[2])
    late_sums = ([], [])
    if own_kernels:
        late_sums = (
            [gate_grad, up_grad, pieces(down_grad), pieces(project_grad)],
            [w_gate.shape, w_upward.shape, w_down.shape[::-1], w_project.shape[::-1], w_query.shape, w_keyval.shape],
        )
    din, gg, *rest = back(
        packing, tokens, q, k, v, raw, datt, lse, spread, dmid, query_full, keyval_full, gains, gg, cosine, sine,
        *late_sums, 4,
    )
    if own_kernels:
        gate, upward, down, project, query, keyval, sums = rest
        down, project = down.T, project.T
    else:
        gate, upward = scatter(by_rows(gate_grad)), scatter(by_rows(up_grad))
        both = scatter(by_rows(rest[0].reshape(COLUMN_STEPS, -1, *rest[0].shape[5:])))
        query, keyval = both[:, :qw], both[:, qw:]
        down, project = scatter(by_columns(down_grad)), scatter(by_columns(project_grad))
        sums = lax.psum(gg, ("shard", "rep"))
    own = lambda row, size: lax.dynamic_slice(sums, (row, me * size), (1, size))[0]
    return (
        act, din, query, keyval, project, gate, upward, down,
        own(0, part), own(4, head_part), own(5, head_part), own(1, part), own(2, part), own(3, part),
    )


def solution(mesh):
    rows, weight, gain = P(("shard", "rep"), None), P("shard", None), P("shard")
    return jax.shard_map(
        shards,
        mesh=mesh,
        in_specs=(rows, P(), P()) + (weight,) * 6 + (gain,) * 6 + (rows,),
        out_specs=(rows, rows) + (weight,) * 6 + (gain,) * 6,
        check_vma=False,
    )
```
